128 devices in a mesh: ap: 32 (over z, x, core), ut: 4 (over y).
Axes of the slice: x: 4, y: 4, z: 4, core: 2. Of those that a mesh axis runs over, the one named last changes fastest.
Arguments:
- channel: bfloat16 [2, 2, 128, 64, 1024], P(None, None, 'ap', None, 'ut'), may hold values from -0.001953125 to 0.001953125
- start_precoder: bfloat16 [2, 2, 128, 64, 1024], P(None, None, 'ap', None, 'ut'), may hold values from -6 to 6
- cluster: int32 [128, 4], P('ap', 'ut'), may hold values 0 or 1
- noise: float32 [2, 1024], P(None, 'ut'), may hold values from 0.2 to 2
- penalty: float32 [128], P('ap'), may hold values from 5.9604646e-09 to 1.1920929e-07
- power: float32 [128], P('ap'), may hold values from 0.5 to 2
Outputs:
- precoder: bfloat16 [2, 2, 128, 64, 1024], P(None, None, 'ap', None, 'ut')
- user_weight: float32 [2, 1024], P(None, 'ut')
The draws below stay inside these ranges and needn't reach their ends.
All inputs are finite; a program needn't handle non-finite values. No bound on the sum of `cluster` on one device may be relied on, other than what follows from the above.
Results may differ from the reference program's by a relative error of at most 0.003.
Values may be sent and summed in bfloat16 or wider, within the bound.
No kernel may reach another device: no remote copies, remote signals or barrier semaphores. Data moves between devices by JAX's collectives and lax.ppermute only.
A program may use at most 64 MiB of HBM per device.

```python
import math
import jax
import jax.numpy as jnp
from jax import lax

M = 64
S = 2
ITERS = 1
U_ALL = 1024
AP_ALL = 128
TILES = 4


def with_ends(values, rng, least, largest):
    place = [jax.random.randint(jax.random.fold_in(rng, axis), (), 0, length) for axis, length in enumerate(values.shape)]
    longest = values.shape.index(max(values.shape))
    next_to = place[:longest] + [(place[longest] + 1) % values.shape[longest]] + place[longest + 1:]
    return values.at[tuple(place)].set(least).at[tuple(next_to)].set(largest)


def block_scale(own_key, dims, shards, least, top_value):
    def one(dim, shards_of):
        draws = jax.random.uniform(jax.random.fold_in(jax.random.fold_in(own_key, 6), dim), (shards_of,), jnp.float32, least / len(shards), top_value / len(shards))
        return jnp.repeat(jnp.exp(draws), dims[dim] // shards_of).reshape((-1,) + (1,) * (len(dims) - dim - 1))

    factor_of = one(*shards[0])
    for cut in shards[1:]:
        factor_of = factor_of * one(*cut)
    return factor_of


def centred(own_key, extent, spread, most, pieces=(), kind=jnp.bfloat16):
    level = block_scale(own_key, extent, pieces, -0.22, 0.18) if pieces else 1.0
    entries = jax.random.normal(own_key, extent, jnp.float32) * spread * level
    return jnp.minimum(jnp.maximum(entries, -most), most).astype(kind)


def setup_inputs(seed: int = 0) -> dict:
    seeds = jax.random.split(jax.random.key(seed), 7)
    channel = centred(seeds[0], (S, 2, AP_ALL, M, U_ALL), ((M * AP_ALL * U_ALL) ** -0.5), 0.001953125, ((2, 32), (4, 4)))
    start_precoder = centred(seeds[1], (S, 2, AP_ALL, M, U_ALL), 1.0, 6.0, ((2, 32), (4, 4)))
    cluster = with_ends((jax.random.randint(seeds[2], (AP_ALL, TILES), 0, 2) < 1).astype(jnp.int32), jax.random.fold_in(seeds[2], 1), 0, 1)
    noise = jnp.clip(jnp.exp(math.log(2.0) - 2.3025851 * jax.random.uniform(seeds[3], (S, U_ALL), jnp.float32) ** block_scale(seeds[3], (S, U_ALL), ((1, 4),), -0.2, 0.2)), 0.2, 2.0)
    penalty = jnp.clip(jnp.exp(math.log(1.1920928955078125e-07) - 2.9957323 * jax.random.uniform(seeds[4], (AP_ALL,), jnp.float32) ** block_scale(seeds[4], (AP_ALL,), ((0, 32),), -0.2, 0.2)), 5.9604645663569045e-09, 1.1920928955078125e-07)
    power = jnp.clip(jnp.exp(math.log(2.0) - 1.3862944 * jax.random.uniform(seeds[5], (AP_ALL,), jnp.float32) ** block_scale(seeds[5], (AP_ALL,), ((0, 32),), -0.2, 0.2)), 0.5, 2.0)
    return {"channel": channel, "start_precoder": start_precoder, "cluster": cluster, "noise": noise, "penalty": penalty, "power": power}


def masked_channel(channel, cluster):
    tile_users = channel.shape[-1] // cluster.shape[1]
    served = jnp.repeat(cluster, tile_users, axis=1).astype(jnp.bfloat16)
    return channel * served[None, None, :, None, :]

def stacked_rows(field):
    blocks, parts, points, antennas, users = field.shape
    return field.reshape(blocks, parts * points * antennas, users)

def partner(field):
    plain = stacked_rows(field)
    turned = stacked_rows(jnp.stack([field[:, 1], -field[:, 0]], axis=1))
    return jnp.stack([plain, turned], axis=1)

def user_terms(total, signal, noise):
    level = total + noise
    strength = signal[:, 0] * signal[:, 0] + signal[:, 1] * signal[:, 1]
    weight = level / (level - strength)
    filter_re = signal[:, 0] / level
    filter_im = signal[:, 1] / level
    coeff = weight * (filter_re * filter_re + filter_im * filter_im)
    return (weight, coeff, filter_re * weight, filter_im * weight)

def covariance(served, coeff):
    real_part = served[:, 0].astype(jnp.float32)
    imag_part = served[:, 1].astype(jnp.float32)
    first = jnp.concatenate([real_part, imag_part], axis=2)
    second = jnp.concatenate([-imag_part, real_part], axis=2)
    scaled = coeff[:, None, None, :]
    result = jnp.einsum('samk,sank->samn', first * scaled, first, precision=lax.Precision.HIGHEST)
    return result + jnp.einsum('samk,sank->samn', second * scaled, second, precision=lax.Precision.HIGHEST)

def transmit_rhs(served, scaled_re, scaled_im):
    real_part = served[:, 0].astype(jnp.float32)
    imag_part = served[:, 1].astype(jnp.float32)
    weight_re = scaled_re[:, None, None, :]
    weight_im = scaled_im[:, None, None, :]
    out_re = real_part * weight_re - imag_part * weight_im
    out_im = real_part * weight_im + imag_part * weight_re
    return jnp.concatenate([out_re, out_im], axis=2)

def cholesky_solve(system, rhs):
    factor = jnp.linalg.cholesky(system)
    middle = lax.linalg.triangular_solve(factor, rhs, left_side=True, lower=True)
    return lax.linalg.triangular_solve(factor, middle, left_side=True, lower=True, transpose_a=True)

def split_field(raw):
    antennas = raw.shape[2] // 2
    return jnp.stack([raw[:, :, :antennas], raw[:, :, antennas:]], axis=1)

def reference(channel, start_precoder, cluster, noise, penalty, power):
    served = masked_channel(channel, cluster)
    rows = stacked_rows(served).astype(jnp.float32)
    all_users = channel.shape[-1]
    antennas = channel.shape[3]
    ident = jnp.eye(2 * antennas, dtype=jnp.float32)
    precoder = start_precoder
    weight = jnp.zeros(noise.shape, jnp.float32)
    for _ in range(ITERS):
        gain = jnp.einsum('srk,scrj->sckj', rows, partner(precoder).astype(jnp.float32))
        total = lax.optimization_barrier(jnp.sum(gain * gain, axis=(1, 3)))
        signal = jnp.diagonal(gain, axis1=2, axis2=3)
        weight, coeff, scaled_re, scaled_im = user_terms(total, signal, noise)
        system = covariance(served, coeff) + penalty[None, :, None, None] * ident
        raw = cholesky_solve(system, transmit_rhs(served, scaled_re, scaled_im))
        field = split_field(raw)
        mean_sq = lax.optimization_barrier(jnp.sum(field * field, axis=(0, 1, 3, 4))) / (2.0 * field.shape[0] * antennas * all_users)
        factor = jnp.sqrt(power / (mean_sq + 1e-06))
        precoder = (field * factor[None, None, :, None, None]).astype(jnp.bfloat16)
    return (precoder, weight)
```

```python
import functools

import jax
import jax.numpy as jnp
from jax import lax
from jax.experimental import pallas as pl
from jax.experimental.pallas import tpu as pltpu
from jax.sharding import Mesh
from jax.sharding import PartitionSpec as P

AP = ("z", "x", "core")
CHIPS = ("z", "x")
EVERY = ("z", "x", "core", "ut")
SLOTS = (0, 1, 3, 2)
F32 = jnp.float32
BF16 = jnp.bfloat16
HIGHEST = lax.Precision.HIGHEST


def dot(a, b, dims, precision=None):
    return lax.dot_general(a, b, (dims, ((), ())), precision=precision, preferred_element_type=F32)


def three_parts(x):
    high = x.astype(BF16)
    rest = x - high.astype(F32)
    middle = rest.astype(BF16)
    low = (rest - middle.astype(F32)).astype(BF16)
    return high, middle, low


def iota(shape, dim):
    return lax.broadcasted_iota(jnp.int32, shape, dim)


def gain_kernel(core_ref, ht_ref, ha_ref, vt_ref, vb_ref, keep_ref, send_ref):
    core = core_ref[0]
    rows, users = ht_ref.shape
    half = rows // 2
    chips = keep_ref.shape[0]
    piece = users // chips
    vt, vb = vt_ref[...], vb_ref[...]
    first = core == 0
    keep_v = jnp.where(first, vt, vb)
    send_v = jnp.where(first, vb, vt)
    on_diag = iota((users, users), 0) == iota((users, users), 1)
    for v, out_ref, own in ((keep_v, keep_ref, first), (send_v, send_ref, jnp.logical_not(first))):
        turned = jnp.concatenate([v[half:], -v[:half]], axis=0)
        for tile, h_ref in enumerate((ht_ref, ha_ref)):
            h = h_ref[...]
            for part, w in enumerate((v, turned)):
                g = dot(h, w, ((0,), (0,)))
                if tile == 0:
                    g = jnp.where(jnp.logical_and(on_diag, own), 0.0, g)
                out_ref[:, part, tile] = g.reshape(chips, piece, users).astype(out_ref.dtype)


def partial_gains(core, ht, ha, vt, vb, chips):
    users = ht.shape[-1]
    shape = (chips, 2, 2, users // chips, users)
    vm = pl.BlockSpec(memory_space=pltpu.VMEM)
    return pl.pallas_call(
        gain_kernel,
        out_shape=(jax.ShapeDtypeStruct(shape, F32), jax.ShapeDtypeStruct(shape, BF16)),
        in_specs=[pl.BlockSpec(memory_space=pltpu.SMEM)] + [vm] * 4,
        out_specs=(vm, vm),
        name="gains",
    )(core, ht, ha, vt, vb)


def total_kernel(g0_ref, g1_ref, sig_ref, noise_ref, out_ref):
    chips, _, _, piece, _ = g0_ref.shape
    columns = []
    for g_ref in (g0_ref, g1_ref):
        total = None
        for part in range(2):
            g = g_ref[0, part].astype(F32)
            for chip in range(1, chips):
                g = g + g_ref[chip, part].astype(F32)
            square = jnp.sum(g * g, axis=-1, keepdims=True)
            total = square if total is None else total + square
        columns.append(total.reshape(2 * piece, 1))
    width = 4 * piece
    lane = iota((2 * piece, out_ref.shape[1]), 1)
    row = iota((2 * piece, out_ref.shape[1]), 0)
    line = jnp.zeros((1, out_ref.shape[1]), F32)
    for block in range(2):
        line = line + jnp.sum(jnp.where(lane == row + block * width, columns[block], 0.0), axis=0, keepdims=True)
    line = line + noise_ref[...] + sig_ref[...]
    out_ref[...] = jnp.broadcast_to(line, out_ref.shape)


def totals(g0, g1, sig, noise, devices):
    vm = pl.BlockSpec(memory_space=pltpu.VMEM)
    return pl.pallas_call(
        total_kernel,
        out_shape=jax.ShapeDtypeStruct((devices, 128), F32),
        in_specs=[vm] * 4,
        out_specs=vm,
        name="totals",
    )(g0, g1, sig, noise)


def user_lines(tile, r, users, chips):
    devices = r.shape[0]
    per_chip = devices // chips
    tiles = per_chip // 2
    piece = users // chips
    rows = tiles * chips
    slot = iota((rows, devices), 0) // chips
    chip = iota((rows, devices), 0) % chips
    wanted = tile ^ jnp.where(slot == 0, SLOTS[0], jnp.where(slot == 1, SLOTS[1], jnp.where(slot == 2, SLOTS[2], SLOTS[3])))
    source = iota((rows, devices), 1)
    same_chip = source // per_chip == chip
    own = jnp.logical_and(same_chip, source % tiles == wanted).astype(F32)
    mate = jnp.logical_and(same_chip, source % tiles == (wanted ^ 1)).astype(F32)
    from_own = dot(own, r, ((1,), (0,)), HIGHEST)
    from_mate = dot(mate, r, ((1,), (0,)), HIGHEST)
    keep = iota((rows, users), 1) // piece == iota((rows, users), 0) % chips

    def spread(values, block, quantity):
        start = block * 4 * piece + quantity * piece
        pick = iota((128, users), 0) == start + iota((128, users), 1) % piece
        return dot(values, pick.astype(F32), ((1,), (0,)), HIGHEST)

    def line(values):
        values = jnp.where(keep, values, 0.0).reshape(tiles, chips, users)
        return jnp.sum(values, axis=1, keepdims=True)

    blocks = []
    for block in range(2):
        rest = line(spread(from_own, block, 0) + spread(from_mate, block, 1))
        signal_re = line(spread(from_own, block, 2))
        signal_im = line(spread(from_own, block, 3))
        strength = signal_re * signal_re + signal_im * signal_im
        level = rest + strength
        blocks.append((level / rest, strength / (rest * level), signal_re / rest, signal_im / rest))
    return blocks


def solve_kernel(tile_ref, penalty_ref, power_ref, r_ref, *refs):
    h_refs = refs[:8]
    out_ref, weight_ref, line_ref, sys_ref, low_ref, scaled_ref, y_ref = refs[8:]
    blocks = 2
    _, points, antennas, users = h_refs[0].shape
    size = 2 * antennas
    chips = 16
    systems = blocks * points

    lines = user_lines(tile_ref[0], r_ref[...], users, chips)
    for block in range(blocks):
        weight, coeff, scaled_re, scaled_im = lines[block]
        weight_ref[block] = weight[0]
        line_ref[block, 0] = coeff
        line_ref[block, 1] = scaled_re
        line_ref[block, 2] = scaled_im

    lane = iota((antennas, size), 1)
    row = iota((antennas, size), 0)
    upper = jnp.where(lane < antennas, 1.0, -1.0).astype(F32)

    def channel(block, slot, point):
        h_ref = h_refs[slot * blocks + block]
        return jnp.concatenate([h_ref[0, point], h_ref[1, point]], axis=0)

    for block in range(blocks):

        def cover(point, carry, block=block):
            acc = jnp.zeros((3 * size, size), F32)
            for slot in range(4):
                x = channel(block, slot, point)
                weighted = x.astype(F32) * line_ref[block, 0, slot]
                parts = jnp.concatenate(three_parts(weighted), axis=0)
                acc = acc + dot(parts, x, ((1,), (1,)))
            p = acc[:size] + (acc[size : 2 * size] + acc[2 * size :])
            a = p[:antennas] * upper + pltpu.roll(p[antennas:], antennas, 1)
            a = a + jnp.where(lane == row, penalty_ref[point], 0.0)
            sys_ref[:, block * points + point, :] = a
            return carry

        lax.fori_loop(0, points, cover, 0)

    lane8 = iota((systems, size), 1)
    sign = jnp.where(lane8 < antennas, -1.0, 1.0).astype(F32)
    for k in range(antennas):
        pivot_row = sys_ref[k]
        inverse = 1.0 / pivot_row[:, k : k + 1]
        here = jnp.logical_or(lane8 == k, lane8 == antennas + k)
        done = jnp.logical_or(lane8 < k, jnp.logical_and(lane8 >= antennas, lane8 < antennas + k))
        one = jnp.where(lane8 == k, 1.0, 0.0)
        unit = jnp.where(here, one, pivot_row)
        low = jnp.where(done, pivot_row, one)
        low_ref[k] = low
        scaled_ref[k] = low * inverse
        if k + 1 < antennas:
            straight = unit * inverse
            turned = pltpu.roll(unit, antennas, 1) * sign * inverse
            for i in range(k + 1, antennas):
                w = sys_ref[i]
                f_re = w[:, k : k + 1]
                f_im = w[:, antennas + k : antennas + k + 1]
                sys_ref[i] = jnp.where(here, 0.0, w) - (f_re * straight + f_im * turned)

    sums = [None] * points

    for block in range(blocks):

        def apply(point, carry, block=block):
            n = block * points + point
            q = dot(scaled_ref[:, n, :], low_ref[:, n, :], ((0,), (0,)), HIGHEST)
            top = q[:antennas] * upper + pltpu.roll(q[antennas:], antennas, 1)
            bottom = pltpu.roll(top, antennas, 1) * (-upper)
            inverse = jnp.concatenate([top, bottom], axis=0)
            parts = jnp.concatenate(three_parts(inverse), axis=0)
            total = jnp.zeros((1, users), F32)
            for slot in range(4):
                x = channel(block, slot, point)
                acc = dot(parts, x, ((1,), (0,)))
                y = acc[:size] + (acc[size : 2 * size] + acc[2 * size :])
                w_re = line_ref[block, 1, slot]
                w_im = line_ref[block, 2, slot]
                total = total + jnp.sum(y * y, axis=0, keepdims=True) * (w_re * w_re + w_im * w_im)
                if slot == 0:
                    y_ref[n] = y
            power_sum = jnp.sum(total, axis=1, keepdims=True)
            return carry + jnp.where(iota((8, 1), 0) == point, power_sum, 0.0)

        part = lax.fori_loop(0, points, apply, jnp.zeros((8, 1), F32))
        sums[block] = part

    mean = (sums[0] + sums[1]) / (2.0 * blocks * antennas * 4 * users)
    for point in range(points):
        gain = jnp.sqrt(power_ref[point] / (mean[point : point + 1] + 1e-06))
        for block in range(blocks):
            y = y_ref[block * points + point]
            y_re, y_im = y[:antennas], y[antennas:]
            w_re = line_ref[block, 1, 0] * gain
            w_im = line_ref[block, 2, 0] * gain
            out_ref[block, 0, point] = (y_re * w_re - y_im * w_im).astype(out_ref.dtype)
            out_ref[block, 1, point] = (y_re * w_im + y_im * w_re).astype(out_ref.dtype)


def solve(tile, penalty, power, r, channels, out_shape):
    blocks, _, points, antennas, users = out_shape
    size = 2 * antennas
    vm = pl.BlockSpec(memory_space=pltpu.VMEM)
    sm = pl.BlockSpec(memory_space=pltpu.SMEM)
    return pl.pallas_call(
        solve_kernel,
        out_shape=(
            jax.ShapeDtypeStruct(out_shape, BF16),
            jax.ShapeDtypeStruct((blocks, 1, users), F32),
        ),
        in_specs=[sm] * 3 + [vm] * 9,
        out_specs=(vm, vm),
        scratch_shapes=[
            pltpu.VMEM((blocks, 3, 4, 1, users), F32),
            pltpu.VMEM((antennas, blocks * points, size), F32),
            pltpu.VMEM((antennas, blocks * points, size), F32),
            pltpu.VMEM((antennas, blocks * points, size), F32),
            pltpu.VMEM((blocks * points, size, users), F32),
        ],
        name="solve",
    )(tile, penalty, power, r, *channels)


def own_signal(served, precoder):
    chan_re = served[:, 0].astype(F32)
    chan_im = served[:, 1].astype(F32)
    prec_re = precoder[:, 0].astype(F32)
    prec_im = precoder[:, 1].astype(F32)
    signal_re = jnp.sum(chan_re * prec_re + chan_im * prec_im, axis=(1, 2))
    signal_im = jnp.sum(chan_re * prec_im - chan_im * prec_re, axis=(1, 2))
    return jnp.stack([signal_re, signal_im], axis=1)


def across(value, axis, mask):
    size = lax.axis_size(axis)
    return lax.ppermute(value, axis, [(i, i ^ mask) for i in range(size)])


def local(channel, start_precoder, cluster, noise, penalty, power):
    blocks, parts, points, antennas, users = channel.shape
    chips = lax.axis_size(CHIPS)
    devices = lax.axis_size(EVERY)
    piece = users // chips
    rows = parts * points * antennas
    core = lax.axis_index("core")
    tile = lax.axis_index("ut")
    chip = lax.axis_index(CHIPS)
    mask = cluster[:, 0].astype(BF16)[None, :, None, None]
    own = [channel[b] * mask for b in range(blocks)]
    served = jnp.stack(own)

    near = [across(own[b], "ut", 1) for b in range(blocks)]
    v_far = [across(start_precoder[b], "ut", 3) for b in range(blocks)]

    signal = own_signal(served, start_precoder)
    high = signal.astype(BF16)
    low = (signal - high.astype(F32)).astype(BF16)
    pairs = jnp.stack([high, low], axis=2).reshape(8, users)
    extra = jnp.broadcast_to(pairs, (chips, 8, users))

    summed = []
    for b in range(blocks):
        flat = [x.reshape(rows, users) for x in (own[b], near[b], start_precoder[b], v_far[b])]
        keep, send = partial_gains(core.reshape(1), *flat, chips)
        came = across(send, "core", 1)
        gains = (keep + came.astype(F32)).astype(BF16)
        if b == 0:
            gains = jnp.concatenate([gains.reshape(chips, 4 * piece, users), extra], axis=1)
        summed.append(lax.all_to_all(gains, CHIPS, 0, 0, tiled=True))

    far = [across(own[b], "ut", 3) for b in range(blocks)]
    far_near = [across(near[b], "ut", 3) for b in range(blocks)]

    g0 = summed[0][:, : 4 * piece].reshape(chips, 2, 2, piece, users)
    g1 = summed[1]
    sums = jnp.sum(summed[0][:, 4 * piece :].astype(F32), axis=0)
    sums = sums.reshape(blocks, 2, 2, users).sum(axis=2)
    mine = lax.dynamic_slice_in_dim(sums, chip * piece, piece, 2)
    sig_line = jnp.concatenate([jnp.zeros((blocks, 2, piece), F32), mine], axis=1).reshape(1, 128)
    noise_mine = lax.dynamic_slice_in_dim(noise, chip * piece, piece, 1)
    noise_mine = jnp.where(core == 0, noise_mine, 0.0)[:, None, :]
    noise_line = jnp.concatenate([noise_mine, jnp.zeros((blocks, 3, piece), F32)], axis=1).reshape(1, 128)
    line = totals(g0, g1, sig_line, noise_line, devices)
    r = lax.all_to_all(line, EVERY, 0, 0, tiled=True)

    channels = [x[b] for x in (own, near, far, far_near) for b in range(blocks)]
    precoder, weight = solve(tile.reshape(1), penalty, power, r, channels, channel.shape)
    return precoder, weight[:, 0]


def solution(mesh):
    split = Mesh(mesh.devices.reshape(4, 4, 2, mesh.shape["ut"]), EVERY)
    placed = (
        P(None, None, AP, None, "ut"),
        P(None, None, AP, None, "ut"),
        P(AP, "ut"),
        P(None, "ut"),
        P(AP),
        P(AP),
    )
    return jax.shard_map(
        local,
        mesh=split,
        in_specs=placed,
        out_specs=(P(None, None, AP, None, "ut"), P(None, "ut")),
        check_vma=False,
    )
```

```python
import functools

import jax
import jax.numpy as jnp
from jax import lax
from jax.experimental import pallas as pl
from jax.experimental.pallas import tpu as pltpu
from jax.sharding import Mesh
from jax.sharding import PartitionSpec as P

AP = ("z", "x", "core")
CHIPS = ("z", "x")
EVERY = ("z", "x", "core", "ut")
SLOTS = (0, 1, 3, 2)
F32 = jnp.float32
BF16 = jnp.bfloat16
HIGHEST = lax.Precision.HIGHEST


def dot(a, b, dims, precision=None):
    return lax.dot_general(a, b, (dims, ((), ())), precision=precision, preferred_element_type=F32)


def three_parts(x):
    high = x.astype(BF16)
    rest = x - high.astype(F32)
    middle = rest.astype(BF16)
    low = (rest - middle.astype(F32)).astype(BF16)
    return high, middle, low


def iota(shape, dim):
    return lax.broadcasted_iota(jnp.int32, shape, dim)


def gain_kernel(core_ref, ht_ref, ha_ref, vt_ref, vb_ref, keep_ref, send_ref):
    core = core_ref[0]
    rows, users = ht_ref.shape
    half = rows // 2
    chips = keep_ref.shape[0]
    piece = users // chips
    vt, vb = vt_ref[...], vb_ref[...]
    first = core == 0
    keep_v = jnp.where(first, vt, vb)
    send_v = jnp.where(first, vb, vt)
    on_diag = iota((users, users), 0) == iota((users, users), 1)
    pairs = []
    for v in (keep_v, send_v):
        pairs += [v, jnp.concatenate([v[half:], -v[:half]], axis=0)]
    for tile, h_ref in enumerate((ht_ref, ha_ref)):
        h = jnp.transpose(h_ref[...])
        for at, v in enumerate(pairs):
            side, part = at // 2, at % 2
            own = first if side == 0 else jnp.logical_not(first)
            out_ref = keep_ref if side == 0 else send_ref
            g = dot(h, v, ((1,), (0,)))
            if tile == 0:
                g = jnp.where(jnp.logical_and(on_diag, own), 0.0, g)
            out_ref[:, part, tile] = g.reshape(chips, piece, users).astype(out_ref.dtype)


def partial_gains(core, ht, ha, vt, vb, chips):
    users = ht.shape[-1]
    shape = (chips, 2, 2, users // chips, users)
    vm = pl.BlockSpec(memory_space=pltpu.VMEM)
    return pl.pallas_call(
        gain_kernel,
        out_shape=(jax.ShapeDtypeStruct(shape, F32), jax.ShapeDtypeStruct(shape, BF16)),
        in_specs=[pl.BlockSpec(memory_space=pltpu.SMEM)] + [vm] * 4,
        out_specs=(vm, vm),
        name="gains",
        cost_estimate=pl.CostEstimate(flops=8 * users * users * ht.shape[0] * 2, bytes_accessed=4 << 20, transcendentals=0),
    )(core, ht, ha, vt, vb)


def combine_kernel(keep0_ref, keep1_ref, came0_ref, came1_ref, extra_ref, out_ref):
    chips, _, _, piece, users = keep0_ref.shape
    rows = 4 * piece
    for block, (keep_ref, came_ref) in enumerate(((keep0_ref, came0_ref), (keep1_ref, came1_ref))):
        g = keep_ref[...] + came_ref[...].astype(F32)
        out_ref[:, block * rows : (block + 1) * rows] = g.reshape(chips, rows, users).astype(BF16)
    out_ref[:, 2 * rows :] = jnp.broadcast_to(extra_ref[...][None], (chips,) + extra_ref.shape)


def combined(keeps, cames, extra):
    chips, _, _, piece, users = keeps[0].shape
    vm = pl.BlockSpec(memory_space=pltpu.VMEM)
    return pl.pallas_call(
        combine_kernel,
        out_shape=jax.ShapeDtypeStruct((chips, 8 * piece + extra.shape[0], users), BF16),
        in_specs=[vm] * 5,
        out_specs=vm,
        name="combine",
    )(*keeps, *cames, extra)


def total_kernel(where_ref, g_ref, noise_ref, out_ref):
    chip, core = where_ref[0], where_ref[1]
    chips, rows, users = g_ref.shape
    piece = (rows - 16) // 8
    lanes = out_ref.shape[1]
    width = 4 * piece
    lane = iota((2 * piece, lanes), 1)
    row = iota((2 * piece, lanes), 0)

    extra = g_ref[0, 8 * piece :].astype(F32)
    for source in range(1, chips):
        extra = extra + g_ref[source, 8 * piece :].astype(F32)
    signal = extra[:8] + extra[8:]
    noise = jnp.where(core == 0, noise_ref[...], 0.0)
    signal = jnp.concatenate([signal[:4], noise, noise], axis=0)
    pick = iota((users, lanes), 0) == chip * piece + iota((users, lanes), 1) % piece
    mine = dot(signal, pick.astype(F32), ((1,), (0,)), HIGHEST)
    group = iota((1, lanes), 1) // piece
    line = jnp.zeros((1, lanes), F32)
    for block in range(2):
        for part in range(2):
            at = block * 2 + part
            line = line + jnp.where(group == block * 4 + 2 + part, mine[at : at + 1], 0.0)
        line = line + jnp.where(group == block * 4, mine[4 + block : 5 + block], 0.0)

    for block in range(2):
        total = None
        for part in range(2):
            base = (block * 2 + part) * 2 * piece
            g = g_ref[0, base : base + 2 * piece].astype(F32)
            for source in range(1, chips):
                g = g + g_ref[source, base : base + 2 * piece].astype(F32)
            square = g * g
            total = square if total is None else total + square
        total = jnp.sum(total, axis=1, keepdims=True)
        line = line + jnp.sum(jnp.where(lane == row + block * width, total, 0.0), axis=0, keepdims=True)
    out_ref[...] = jnp.broadcast_to(line, out_ref.shape)


def totals(where, g, noise, devices):
    vm = pl.BlockSpec(memory_space=pltpu.VMEM)
    return pl.pallas_call(
        total_kernel,
        out_shape=jax.ShapeDtypeStruct((devices, 128), F32),
        in_specs=[pl.BlockSpec(memory_space=pltpu.SMEM), vm, vm],
        out_specs=vm,
        name="totals",
    )(where, g, noise)


def user_lines(r_ref, line_ref, weight_ref, tile):
    chips, _, lanes = r_ref.shape
    groups = 8
    piece = lanes // groups
    halves = chips // groups
    group = iota((8, lanes), 1) // piece
    sublane = iota((8, lanes), 0)
    rolled = [r_ref[0]] + [pltpu.roll(r_ref[p], p * piece % lanes, 1) if p % groups else r_ref[p] for p in range(1, chips)]

    def gathered(g, half):
        total = None
        for p in range(half * groups, (half + 1) * groups):
            term = jnp.where(group == (p + g) % groups, rolled[p], 0.0)
            total = term if total is None else total + term
        if g:
            total = pltpu.roll(total, lanes - g * piece, 1)
        return total + pltpu.roll(total, 4, 0)

    def line(g):
        return jnp.concatenate([gathered(g, half) for half in range(halves)], axis=1)

    for block in range(2):
        base = block * 4
        from_mate = line(base + 1)
        even = iota(from_mate.shape, 0) % 2 == 0
        swapped = jnp.where(even, pltpu.roll(from_mate, 7, 0), pltpu.roll(from_mate, 1, 0))
        rest = line(base) + swapped
        signal_re = line(base + 2)
        signal_im = line(base + 3)
        strength = signal_re * signal_re + signal_im * signal_im
        level = rest + strength
        line_ref[block, 0] = strength / (rest * level)
        line_ref[block, 1] = signal_re / rest
        line_ref[block, 2] = signal_im / rest
        line_ref[block, 3] = level / rest
        weight_ref[block] = line_ref[block, 3, pl.ds(tile, 1)]


def solve_kernel(tile_ref, penalty_ref, power_ref, r_ref, *refs):
    h_refs = refs[:8]
    out_ref, weight_ref, line_ref, sys_ref, low_ref, scaled_ref, y_ref, sem = refs[8:]
    blocks = 2
    _, points, antennas, users = h_refs[0].shape
    size = 2 * antennas
    systems = blocks * points
    tile = tile_ref[0]

    user_lines(r_ref, line_ref, weight_ref, tile)

    def line(block, which, slot):
        return line_ref[block, which, pl.ds(tile ^ SLOTS[slot], 1), :]

    def channel(block, slot, point):
        h_ref = h_refs[slot * blocks + block]
        return jnp.concatenate([h_ref[0, point], h_ref[1, point]], axis=0)

    lane = iota((antennas, size), 1)
    row = iota((antennas, size), 0)
    upper = jnp.where(lane < antennas, 1.0, -1.0).astype(F32)

    for block in range(blocks):
        for point in range(points):
            acc = None
            for slot in range(4):
                x = channel(block, slot, point)
                weighted = x.astype(F32) * line(block, 0, slot)
                parts = jnp.concatenate(three_parts(weighted), axis=0)
                term = dot(parts, x, ((1,), (1,)))
                acc = term if acc is None else acc + term
            p = acc[:size] + (acc[size : 2 * size] + acc[2 * size :])
            a = p[:antennas] * upper + pltpu.roll(p[antennas:], antennas, 1)
            a = a + jnp.where(lane == row, penalty_ref[point], 0.0)
            sys_ref[:, block * points + point, :] = a

    lane8 = iota((systems, size), 1)
    sign = jnp.where(lane8 < antennas, -1.0, 1.0).astype(F32)

    def pivot(k, pivot_row):
        inverse = 1.0 / pivot_row[:, k : k + 1]
        here = jnp.logical_or(lane8 == k, lane8 == antennas + k)
        done = jnp.logical_or(lane8 < k, jnp.logical_and(lane8 >= antennas, lane8 < antennas + k))
        one = jnp.where(lane8 == k, 1.0, 0.0)
        unit = jnp.where(here, one, pivot_row)
        low = jnp.where(done, pivot_row, one)
        low_ref[k] = low
        scaled_ref[k] = low * inverse
        return unit * inverse, (pltpu.roll(unit, antennas, 1) * sign) * inverse, here

    def update(k, i, straight, turned, here):
        w = sys_ref[i]
        f_re = w[:, k : k + 1]
        f_im = w[:, antennas + k : antennas + k + 1]
        return jnp.where(here, 0.0, w) - (f_re * straight + f_im * turned)

    now = pivot(0, sys_ref[0])
    for k in range(antennas - 1):
        later = pivot(k + 1, update(k, k + 1, *now))
        for i in range(k + 2, antennas):
            sys_ref[i] = update(k, i, *now)
        now = later

    copies = []
    for point in range(points):
        total = jnp.zeros((1, users), F32)
        for block in range(blocks):
            n = block * points + point
            q = dot(scaled_ref[:, n, :], low_ref[:, n, :], ((0,), (0,)), HIGHEST)
            top = q[:antennas] * upper + pltpu.roll(q[antennas:], antennas, 1)
            bottom = pltpu.roll(top, antennas, 1) * (-upper)
            parts = three_parts(jnp.concatenate([top, bottom], axis=0))
            for slot in range(4):
                depth = 3 if slot == 0 else 2
                x = channel(block, slot, point)
                y = dot(jnp.concatenate(parts[:depth], axis=1), jnp.concatenate([x] * depth, axis=0), ((1,), (0,)))
                w_re, w_im = line(block, 1, slot), line(block, 2, slot)
                total = total + jnp.sum(y * y, axis=0, keepdims=True) * (w_re * w_re + w_im * w_im)
                if slot == 0:
                    y_ref[block] = y
        mean = jnp.sum(total, axis=1, keepdims=True) / (2.0 * blocks * antennas * 4 * users)
        gain = jnp.sqrt(power_ref[point] / (mean + 1e-06))
        for block in range(blocks):
            y_re, y_im = y_ref[block, :antennas], y_ref[block, antennas:]
            w_re = line(block, 1, 0) * gain
            w_im = line(block, 2, 0) * gain
            out_ref[block, 0, point] = (y_re * w_re - y_im * w_im).astype(out_ref.dtype)
            out_ref[block, 1, point] = (y_re * w_im + y_im * w_re).astype(out_ref.dtype)


def solve(tile, penalty, power, r, channels, out_shape):
    blocks, _, points, antennas, users = out_shape
    size = 2 * antennas
    vm = pl.BlockSpec(memory_space=pltpu.VMEM)
    sm = pl.BlockSpec(memory_space=pltpu.SMEM)
    return pl.pallas_call(
        solve_kernel,
        out_shape=(
            jax.ShapeDtypeStruct(out_shape, BF16),
            jax.ShapeDtypeStruct((blocks, 1, users), F32),
        ),
        in_specs=[sm] * 3 + [vm] * 9,
        out_specs=(vm, vm),
        scratch_shapes=[
            pltpu.VMEM((blocks, 4, 8, users), F32),
            pltpu.VMEM((antennas, blocks * points, size), F32),
            pltpu.VMEM((antennas, blocks * points, size), F32),
            pltpu.VMEM((antennas, blocks * points, size), F32),
            pltpu.VMEM((blocks, size, users), F32),
            pltpu.SemaphoreType.DMA((1,)),
        ],
        name="solve",
    )(tile, penalty, power, r, *channels)


def own_signal(served, precoder):
    chan_re, chan_im = served[0].astype(F32), served[1].astype(F32)
    prec_re, prec_im = precoder[0].astype(F32), precoder[1].astype(F32)
    signal_re = jnp.sum(chan_re * prec_re + chan_im * prec_im, axis=(0, 1))
    signal_im = jnp.sum(chan_re * prec_im - chan_im * prec_re, axis=(0, 1))
    return jnp.stack([signal_re, signal_im])


def across(value, axis, mask):
    size = lax.axis_size(axis)
    return lax.ppermute(value, axis, [(i, i ^ mask) for i in range(size)])


def local(channel, start_precoder, cluster, noise, penalty, power):
    blocks, parts, points, antennas, users = channel.shape
    chips = lax.axis_size(CHIPS)
    devices = lax.axis_size(EVERY)
    piece = users // chips
    rows = parts * points * antennas
    core = lax.axis_index("core")
    tile = lax.axis_index("ut")
    chip = lax.axis_index(CHIPS)

    v_far = [across(start_precoder[b], "ut", 3) for b in range(blocks)]
    mask = cluster[:, 0].astype(BF16)[None, :, None, None]
    own = [channel[b] * mask for b in range(blocks)]
    near = [across(own[b], "ut", 1) for b in range(blocks)]
    far = [across(own[b], "ut", 3) for b in range(blocks)]
    far_near = [across(near[b], "ut", 3) for b in range(blocks)]

    signal = jnp.concatenate([own_signal(own[b], start_precoder[b]) for b in range(blocks)])
    high = lax.reduce_precision(signal, 8, 7)
    pad = jnp.zeros_like(signal)
    extra = jnp.concatenate([high, pad, signal - high, pad]).astype(BF16)

    keeps, cames = [], []
    for b in range(blocks):
        flat = [x.reshape(rows, users) for x in (own[b], near[b], start_precoder[b], v_far[b])]
        keep, send = partial_gains(core.reshape(1), *flat, chips)
        keeps.append(keep)
        cames.append(across(send, "core", 1))
    gains = combined(keeps, cames, extra)
    summed = lax.all_to_all(gains, CHIPS, 0, 0, tiled=True)
    line = totals(jnp.stack([chip, core]), summed, noise, devices)
    r = lax.all_to_all(line, EVERY, 0, 0, tiled=True).reshape(chips, devices // chips, 128)

    channels = [x[b] for x in (own, near, far, far_near) for b in range(blocks)]
    precoder, weight = solve(tile.reshape(1), penalty, power, r, channels, channel.shape)
    return precoder, weight[:, 0]


def solution(mesh):
    split = Mesh(mesh.devices.reshape(4, 4, 2, mesh.shape["ut"]), EVERY)
    placed = (
        P(None, None, AP, None, "ut"),
        P(None, None, AP, None, "ut"),
        P(AP, "ut"),
        P(None, "ut"),
        P(AP),
        P(AP),
    )
    return jax.shard_map(
        local,
        mesh=split,
        in_specs=placed,
        out_specs=(P(None, None, AP, None, "ut"), P(None, "ut")),
        check_vma=False,
    )
```

```python
import functools

import jax
import jax.numpy as jnp
from jax import lax
from jax.experimental import pallas as pl
from jax.experimental.pallas import tpu as pltpu
from jax.sharding import Mesh
from jax.sharding import PartitionSpec as P

AP = ("z", "x", "core")
CHIPS = ("z", "x")
EVERY = ("z", "x", "core", "ut")
SLOTS = (0, 1, 3, 2)
F32 = jnp.float32
BF16 = jnp.bfloat16
HIGHEST = lax.Precision.HIGHEST


def dot(a, b, dims, precision=None):
    return lax.dot_general(a, b, (dims, ((), ())), precision=precision, preferred_element_type=F32)


def three_parts(x):
    high = x.astype(BF16)
    rest = x - high.astype(F32)
    middle = rest.astype(BF16)
    low = (rest - middle.astype(F32)).astype(BF16)
    return high, middle, low


def iota(shape, dim):
    return lax.broadcasted_iota(jnp.int32, shape, dim)


def gain_kernel(core_ref, ht_ref, ha_ref, vt_ref, vb_ref, keep_ref, send_ref):
    core = core_ref[0]
    rows, users = ht_ref.shape
    half = rows // 2
    chips = keep_ref.shape[0]
    piece = users // chips
    vt, vb = vt_ref[...], vb_ref[...]
    first = core == 0
    keep_v = jnp.where(first, vt, vb)
    send_v = jnp.where(first, vb, vt)
    on_diag = iota((users, users), 0) == iota((users, users), 1)
    pairs = []
    for v in (keep_v, send_v):
        pairs += [v, jnp.concatenate([v[half:], -v[:half]], axis=0)]
    for tile, h_ref in enumerate((ht_ref, ha_ref)):
        h = jnp.transpose(h_ref[...])
        for at, v in enumerate(pairs):
            side, part = at // 2, at % 2
            own = first if side == 0 else jnp.logical_not(first)
            out_ref = keep_ref if side == 0 else send_ref
            g = dot(h, v, ((1,), (0,)))
            if tile == 0:
                g = jnp.where(jnp.logical_and(on_diag, own), 0.0, g)
            out_ref[:, part, tile] = g.reshape(chips, piece, users).astype(out_ref.dtype)


def partial_gains(core, ht, ha, vt, vb, chips):
    users = ht.shape[-1]
    shape = (chips, 2, 2, users // chips, users)
    vm = pl.BlockSpec(memory_space=pltpu.VMEM)
    return pl.pallas_call(
        gain_kernel,
        out_shape=(jax.ShapeDtypeStruct(shape, F32), jax.ShapeDtypeStruct(shape, BF16)),
        in_specs=[pl.BlockSpec(memory_space=pltpu.SMEM)] + [vm] * 4,
        out_specs=(vm, vm),
        name="gains",
        compiler_params=pltpu.CompilerParams(vmem_limit_bytes=8 << 20),
        cost_estimate=pl.CostEstimate(flops=8 * users * users * ht.shape[0] * 2, bytes_accessed=4 << 20, transcendentals=0),
    )(core, ht, ha, vt, vb)


def combine_kernel(keep0_ref, keep1_ref, came0_ref, came1_ref, extra_ref, out_ref):
    chips, _, _, piece, users = keep0_ref.shape
    rows = 4 * piece
    for block, (keep_ref, came_ref) in enumerate(((keep0_ref, came0_ref), (keep1_ref, came1_ref))):
        g = keep_ref[...] + came_ref[...].astype(F32)
        out_ref[:, block * rows : (block + 1) * rows] = g.reshape(chips, rows, users).astype(BF16)
    out_ref[:, 2 * rows :] = jnp.broadcast_to(extra_ref[...][None], (chips,) + extra_ref.shape)


def combined(keeps, cames, extra):
    chips, _, _, piece, users = keeps[0].shape
    vm = pl.BlockSpec(memory_space=pltpu.VMEM)
    return pl.pallas_call(
        combine_kernel,
        out_shape=jax.ShapeDtypeStruct((chips, 8 * piece + extra.shape[0], users), BF16),
        in_specs=[vm] * 5,
        out_specs=vm,
        name="combine",
        compiler_params=pltpu.CompilerParams(vmem_limit_bytes=8 << 20),
    )(*keeps, *cames, extra)


def total_kernel(where_ref, g_ref, noise_ref, out_ref):
    chip, core = where_ref[0], where_ref[1]
    chips, rows, users = g_ref.shape
    piece = (rows - 16) // 8
    lanes = out_ref.shape[1]
    width = 4 * piece
    lane = iota((2 * piece, lanes), 1)
    row = iota((2 * piece, lanes), 0)

    extra = g_ref[0, 8 * piece :].astype(F32)
    for source in range(1, chips):
        extra = extra + g_ref[source, 8 * piece :].astype(F32)
    signal = extra[:8] + extra[8:]
    noise = jnp.where(core == 0, noise_ref[...], 0.0)
    signal = jnp.concatenate([signal[:4], noise, noise], axis=0)
    pick = iota((users, lanes), 0) == chip * piece + iota((users, lanes), 1) % piece
    mine = dot(signal, pick.astype(F32), ((1,), (0,)), HIGHEST)
    group = iota((1, lanes), 1) // piece
    line = jnp.zeros((1, lanes), F32)
    for block in range(2):
        for part in range(2):
            at = block * 2 + part
            line = line + jnp.where(group == block * 4 + 2 + part, mine[at : at + 1], 0.0)
        line = line + jnp.where(group == block * 4, mine[4 + block : 5 + block], 0.0)

    for block in range(2):
        total = None
        for part in range(2):
            base = (block * 2 + part) * 2 * piece
            g = g_ref[0, base : base + 2 * piece].astype(F32)
            for source in range(1, chips):
                g = g + g_ref[source, base : base + 2 * piece].astype(F32)
            square = g * g
            total = square if total is None else total + square
        total = jnp.sum(total, axis=1, keepdims=True)
        line = line + jnp.sum(jnp.where(lane == row + block * width, total, 0.0), axis=0, keepdims=True)
    out_ref[...] = jnp.broadcast_to(line, out_ref.shape)


def totals(where, g, noise, devices):
    vm = pl.BlockSpec(memory_space=pltpu.VMEM)
    return pl.pallas_call(
        total_kernel,
        out_shape=jax.ShapeDtypeStruct((devices, 128), F32),
        in_specs=[pl.BlockSpec(memory_space=pltpu.SMEM), vm, vm],
        out_specs=vm,
        name="totals",
        compiler_params=pltpu.CompilerParams(vmem_limit_bytes=8 << 20),
    )(where, g, noise)


def user_lines(r_ref, line_ref, weight_ref, tile):
    chips, _, lanes = r_ref.shape
    groups = 8
    piece = lanes // groups
    halves = chips // groups
    group = iota((8, lanes), 1) // piece
    sublane = iota((8, lanes), 0)
    rolled = [r_ref[0]] + [pltpu.roll(r_ref[p], p * piece % lanes, 1) if p % groups else r_ref[p] for p in range(1, chips)]

    def gathered(g, half):
        total = None
        for p in range(half * groups, (half + 1) * groups):
            term = jnp.where(group == (p + g) % groups, rolled[p], 0.0)
            total = term if total is None else total + term
        if g:
            total = pltpu.roll(total, lanes - g * piece, 1)
        return total + pltpu.roll(total, 4, 0)

    def line(g):
        return jnp.concatenate([gathered(g, half) for half in range(halves)], axis=1)

    for block in range(2):
        base = block * 4
        from_mate = line(base + 1)
        even = iota(from_mate.shape, 0) % 2 == 0
        swapped = jnp.where(even, pltpu.roll(from_mate, 7, 0), pltpu.roll(from_mate, 1, 0))
        rest = line(base) + swapped
        signal_re = line(base + 2)
        signal_im = line(base + 3)
        strength = signal_re * signal_re + signal_im * signal_im
        level = rest + strength
        line_ref[block, 0] = strength / (rest * level)
        line_ref[block, 1] = signal_re / rest
        line_ref[block, 2] = signal_im / rest
        line_ref[block, 3] = level / rest
        weight_ref[block] = line_ref[block, 3, pl.ds(tile, 1)]


def regrouped(pieces, wanted):
    lanes = pieces[0].shape[1]
    width = lanes // 8
    group = iota(pieces[0].shape, 1) // width
    rolled = [pltpu.roll(piece, s * width, 1) if s else piece for s, piece in enumerate(pieces)]
    results = []
    for g in range(8):
        if not wanted[g]:
            results.append(None)
            continue
        total = rolled[0]
        for s in range(1, 8):
            total = jnp.where(group == (s + g) % 8, rolled[s], total)
        results.append(pltpu.roll(total, lanes - g * width, 1) if g else total)
    return results


def eliminate(work_ref, sys_ref, scale_ref):
    _, rows, lanes = work_ref.shape
    width = lanes // 8
    lane = iota((8, lanes), 1)
    sublane = iota((8, lanes), 0)
    for high in range(rows // 8):
        at = slice(high * 8, high * 8 + 8)
        groups = regrouped([sys_ref[s, at, :] for s in range(8)], [True] * 8)
        for g in range(8):
            work_ref[g, at, :] = groups[g]

    def spread(value, k):
        return jnp.take_along_axis(value, lane // width * width + k % width, axis=1, mode="promise_in_bounds")

    def row_of(g, k):
        return jnp.broadcast_to(work_ref[g, k : k + 1, :], (8, lanes))

    def pivot(k):
        column = k // width
        line = [row_of(g, k) for g in range(8)]
        value = spread(line[column], k)
        root = lax.rsqrt(value)
        scale_ref[k : k + 1, :] = root[:1]
        line[column] = line[column] + jnp.where(lane % width == k % width, 1.0, 0.0)
        return line, 1.0 / value

    def update(k, high, line, inverse):
        column = k // width
        at = slice(high * 8, high * 8 + 8)
        f_re = spread(work_ref[column, at, :], k) * inverse
        f_im = spread(work_ref[4 + column, at, :], k) * inverse
        if high == k // 8:
            below = sublane > k % 8
            f_re = jnp.where(below, f_re, 0.0)
            f_im = jnp.where(below, f_im, 0.0)
        for c in range(4):
            real, imag = line[c], line[4 + c]
            work_ref[c, at, :] = work_ref[c, at, :] - (f_re * real - f_im * imag)
            work_ref[4 + c, at, :] = work_ref[4 + c, at, :] - (f_re * imag + f_im * real)

    now = pivot(0)
    for k in range(rows - 1):
        first = (k + 1) // 8
        update(k, first, *now)
        later = pivot(k + 1)
        if first != k // 8:
            pass
        for high in range(first + 1, rows // 8):
            update(k, high, *now)
        now = later

    for high in range(rows // 8):
        at = slice(high * 8, high * 8 + 8)
        scale = scale_ref[at, :]
        pieces = []
        for g in range(8):
            start = g % 4 * width
            here = start + lane % width
            row = high * 8 + sublane
            kept = jnp.where(here < row, work_ref[g, at, :], 0.0)
            if g < 4:
                kept = jnp.where(here == row, 1.0, kept)
            pieces.append(kept * scale)
        systems = regrouped(pieces, [True] * 8)
        for s in range(8):
            sys_ref[s, at, :] = systems[s]


def solve_kernel(tile_ref, penalty_ref, power_ref, r_ref, *refs):
    h_refs = refs[:8]
    out_ref, weight_ref, line_ref, sys_ref, work_ref, scale_ref, y_ref = refs[8:]
    blocks = 2
    _, points, antennas, users = h_refs[0].shape
    size = 2 * antennas
    systems = blocks * points
    tile = tile_ref[0]

    user_lines(r_ref, line_ref, weight_ref, tile)

    def line(block, which, slot):
        return line_ref[block, which, pl.ds(tile ^ SLOTS[slot], 1), :]

    def channel(block, slot, point):
        h_ref = h_refs[slot * blocks + block]
        return jnp.concatenate([h_ref[0, point], h_ref[1, point]], axis=0)

    lane = iota((antennas, size), 1)
    row = iota((antennas, size), 0)
    upper = jnp.where(lane < antennas, 1.0, -1.0).astype(F32)

    for block in range(blocks):
        for point in range(points):
            acc = None
            for slot in range(4):
                x = channel(block, slot, point)
                weighted = x.astype(F32) * line(block, 0, slot)
                parts = jnp.concatenate(three_parts(weighted), axis=0)
                term = dot(parts, x, ((1,), (1,)))
                acc = term if acc is None else acc + term
            p = acc[:size] + (acc[size : 2 * size] + acc[2 * size :])
            a = p[:antennas] * upper + pltpu.roll(p[antennas:], antennas, 1)
            a = a + jnp.where(lane == row, penalty_ref[point], 0.0)
            sys_ref[block * points + point] = a

    eliminate(work_ref, sys_ref, scale_ref)

    for point in range(points):
        total = jnp.zeros((1, users), F32)
        for block in range(blocks):
            n = block * points + point
            z = sys_ref[n]
            q = dot(z, z, ((0,), (0,)), HIGHEST)
            top = q[:antennas] * upper + pltpu.roll(q[antennas:], antennas, 1)
            bottom = pltpu.roll(top, antennas, 1) * (-upper)
            parts = three_parts(jnp.concatenate([top, bottom], axis=0))
            for slot in range(4):
                depth = 3 if slot == 0 else 2
                x = channel(block, slot, point)
                y = dot(jnp.concatenate(parts[:depth], axis=1), jnp.concatenate([x] * depth, axis=0), ((1,), (0,)))
                w_re, w_im = line(block, 1, slot), line(block, 2, slot)
                total = total + jnp.sum(y * y, axis=0, keepdims=True) * (w_re * w_re + w_im * w_im)
                if slot == 0:
                    y_ref[block] = y
        mean = jnp.sum(total, axis=1, keepdims=True) / (2.0 * blocks * antennas * 4 * users)
        gain = jnp.sqrt(power_ref[point] / (mean + 1e-06))
        for block in range(blocks):
            y_re, y_im = y_ref[block, :antennas], y_ref[block, antennas:]
            w_re = line(block, 1, 0) * gain
            w_im = line(block, 2, 0) * gain
            out_ref[block, 0, point] = (y_re * w_re - y_im * w_im).astype(out_ref.dtype)
            out_ref[block, 1, point] = (y_re * w_im + y_im * w_re).astype(out_ref.dtype)


def solve(tile, penalty, power, r, channels, out_shape):
    blocks, _, points, antennas, users = out_shape
    size = 2 * antennas
    vm = pl.BlockSpec(memory_space=pltpu.VMEM)
    sm = pl.BlockSpec(memory_space=pltpu.SMEM)
    return pl.pallas_call(
        solve_kernel,
        out_shape=(
            jax.ShapeDtypeStruct(out_shape, BF16),
            jax.ShapeDtypeStruct((blocks, 1, users), F32),
        ),
        in_specs=[sm] * 3 + [vm] * 9,
        out_specs=(vm, vm),
        scratch_shapes=[
            pltpu.VMEM((blocks, 4, 8, users), F32),
            pltpu.VMEM((blocks * points, antennas, size), F32),
            pltpu.VMEM((8, antennas, size), F32),
            pltpu.VMEM((antennas, size), F32),
            pltpu.VMEM((blocks, size, users), F32),
        ],
        name="solve",
        compiler_params=pltpu.CompilerParams(vmem_limit_bytes=16 << 20),
    )(tile, penalty, power, r, *channels)


def own_signal(served, precoder):
    chan_re, chan_im = served[0].astype(F32), served[1].astype(F32)
    prec_re, prec_im = precoder[0].astype(F32), precoder[1].astype(F32)
    signal_re = jnp.sum(chan_re * prec_re + chan_im * prec_im, axis=(0, 1))
    signal_im = jnp.sum(chan_re * prec_im - chan_im * prec_re, axis=(0, 1))
    return jnp.stack([signal_re, signal_im])


def across(value, axis, mask):
    size = lax.axis_size(axis)
    return lax.ppermute(value, axis, [(i, i ^ mask) for i in range(size)])


def local(channel, start_precoder, cluster, noise, penalty, power):
    blocks, parts, points, antennas, users = channel.shape
    chips = lax.axis_size(CHIPS)
    devices = lax.axis_size(EVERY)
    piece = users // chips
    rows = parts * points * antennas
    core = lax.axis_index("core")
    tile = lax.axis_index("ut")
    chip = lax.axis_index(CHIPS)

    v_far = [across(start_precoder[b], "ut", 3) for b in range(blocks)]
    mask = cluster[:, 0].astype(BF16)[None, :, None, None]
    own = [channel[b] * mask for b in range(blocks)]
    near = [across(own[b], "ut", 1) for b in range(blocks)]
    far = [across(own[b], "ut", 3) for b in range(blocks)]
    far_near = [across(near[b], "ut", 3) for b in range(blocks)]

    signal = jnp.concatenate([own_signal(own[b], start_precoder[b]) for b in range(blocks)])
    high = lax.reduce_precision(signal, 8, 7)
    pad = jnp.zeros_like(signal)
    extra = jnp.concatenate([high, pad, signal - high, pad]).astype(BF16)

    keeps, cames = [], []
    for b in range(blocks):
        flat = [x.reshape(rows, users) for x in (own[b], near[b], start_precoder[b], v_far[b])]
        keep, send = partial_gains(core.reshape(1), *flat, chips)
        keeps.append(keep)
        cames.append(across(send, "core", 1))
    gains = combined(keeps, cames, extra)
    summed = lax.all_to_all(gains, CHIPS, 0, 0, tiled=True)
    line = totals(jnp.stack([chip, core]), summed, noise, devices)
    r = lax.all_to_all(line, EVERY, 0, 0, tiled=True).reshape(chips, devices // chips, 128)

    channels = [x[b] for x in (own, near, far, far_near) for b in range(blocks)]
    precoder, weight = solve(tile.reshape(1), penalty, power, r, channels, channel.shape)
    return precoder, weight[:, 0]


def solution(mesh):
    split = Mesh(mesh.devices.reshape(4, 4, 2, mesh.shape["ut"]), EVERY)
    placed = (
        P(None, None, AP, None, "ut"),
        P(None, None, AP, None, "ut"),
        P(AP, "ut"),
        P(None, "ut"),
        P(AP),
        P(AP),
    )
    return jax.shard_map(
        local,
        mesh=split,
        in_specs=placed,
        out_specs=(P(None, None, AP, None, "ut"), P(None, "ut")),
        check_vma=False,
    )
```

```python
import functools

import jax
import jax.numpy as jnp
from jax import lax
from jax.experimental import pallas as pl
from jax.experimental.pallas import tpu as pltpu
from jax.sharding import Mesh
from jax.sharding import PartitionSpec as P

AP = ("z", "x", "core")
CHIPS = ("z", "x")
EVERY = ("z", "x", "core", "ut")
SLOTS = (0, 1, 3, 2)
F32 = jnp.float32
BF16 = jnp.bfloat16
HIGHEST = lax.Precision.HIGHEST


def dot(a, b, dims, precision=None):
    return lax.dot_general(a, b, (dims, ((), ())), precision=precision, preferred_element_type=F32)


def two_parts(x):
    high = x.astype(BF16)
    return high, (x - high.astype(F32)).astype(BF16)


def iota(shape, dim):
    return lax.broadcasted_iota(jnp.int32, shape, dim)


def gain_kernel(block, core_ref, ht_ref, ha_ref, vt_ref, vb_ref, keep_ref, send_ref):
    core = core_ref[0]
    _, rows, users = ht_ref.shape
    half = rows // 2
    chips = keep_ref.shape[0]
    piece = users // chips
    vt, vb = vt_ref[block], vb_ref[block]
    first = core == 0
    keep_v = jnp.where(first, vt, vb)
    send_v = jnp.where(first, vb, vt)
    on_diag = iota((users, users), 0) == iota((users, users), 1)
    pairs = []
    for v in (keep_v, send_v):
        pairs += [v, jnp.concatenate([v[half:], -v[:half]], axis=0)]
    for tile, h_ref in enumerate((ht_ref, ha_ref)):
        h = jnp.transpose(h_ref[block])
        for at, v in enumerate(pairs):
            side, part = at // 2, at % 2
            own = first if side == 0 else jnp.logical_not(first)
            out_ref = keep_ref if side == 0 else send_ref
            g = dot(h, v, ((1,), (0,)))
            if tile == 0:
                g = jnp.where(jnp.logical_and(on_diag, own), 0.0, g)
            out_ref[:, part, tile] = g.reshape(chips, piece, users).astype(out_ref.dtype)


def partial_gains(block, core, ht, ha, vt, vb, chips):
    _, rows, users = ht.shape
    shape = (chips, 2, 2, users // chips, users)
    vm = pl.BlockSpec(memory_space=pltpu.VMEM)
    return pl.pallas_call(
        functools.partial(gain_kernel, block),
        out_shape=(jax.ShapeDtypeStruct(shape, BF16), jax.ShapeDtypeStruct(shape, BF16)),
        in_specs=[pl.BlockSpec(memory_space=pltpu.SMEM)] + [vm] * 4,
        out_specs=(vm, vm),
        name="gains",
        compiler_params=pltpu.CompilerParams(vmem_limit_bytes=8 << 20),
        cost_estimate=pl.CostEstimate(flops=8 * users * users * rows * 2, bytes_accessed=4 << 20, transcendentals=0),
    )(core, ht, ha, vt, vb)


def combine_kernel(keep0_ref, keep1_ref, came0_ref, came1_ref, extra_ref, out_ref):
    chips, _, _, piece, users = keep0_ref.shape
    rows = 4 * piece
    for block, (keep_ref, came_ref) in enumerate(((keep0_ref, came0_ref), (keep1_ref, came1_ref))):
        g = keep_ref[...].astype(F32) + came_ref[...].astype(F32)
        out_ref[:, block * rows : (block + 1) * rows] = g.reshape(chips, rows, users).astype(BF16)
    out_ref[:, 2 * rows :] = jnp.broadcast_to(extra_ref[...][None], (chips,) + extra_ref.shape)


def combined(keeps, cames, extra):
    chips, _, _, piece, users = keeps[0].shape
    vm = pl.BlockSpec(memory_space=pltpu.VMEM)
    return pl.pallas_call(
        combine_kernel,
        out_shape=jax.ShapeDtypeStruct((chips, 8 * piece + extra.shape[0], users), BF16),
        in_specs=[vm] * 5,
        out_specs=vm,
        name="combine",
        compiler_params=pltpu.CompilerParams(vmem_limit_bytes=8 << 20),
    )(*keeps, *cames, extra)


def total_kernel(where_ref, g_ref, noise_ref, out_ref):
    chip, core = where_ref[0], where_ref[1]
    chips, rows, users = g_ref.shape
    piece = (rows - 8) // 8
    lanes = out_ref.shape[1]
    width = 4 * piece
    lane = iota((2 * piece, lanes), 1)
    row = iota((2 * piece, lanes), 0)

    extra = g_ref[0, 8 * piece :].astype(F32)
    for source in range(1, chips):
        extra = extra + g_ref[source, 8 * piece :].astype(F32)
    signal = extra + pltpu.roll(extra, 4, 0)
    noise = jnp.where(core == 0, noise_ref[...], 0.0)
    signal = jnp.concatenate([signal[:4], noise, noise], axis=0)
    pick = iota((users, lanes), 0) == chip * piece + iota((users, lanes), 1) % piece
    mine = dot(signal, pick.astype(F32), ((1,), (0,)), HIGHEST)
    group = iota((1, lanes), 1) // piece
    line = jnp.zeros((1, lanes), F32)
    for block in range(2):
        for part in range(2):
            at = block * 2 + part
            line = line + jnp.where(group == block * 4 + 2 + part, mine[at : at + 1], 0.0)
        line = line + jnp.where(group == block * 4, mine[4 + block : 5 + block], 0.0)

    for block in range(2):
        total = None
        for part in range(2):
            base = (block * 2 + part) * 2 * piece
            g = g_ref[0, base : base + 2 * piece].astype(F32)
            for source in range(1, chips):
                g = g + g_ref[source, base : base + 2 * piece].astype(F32)
            square = g * g
            total = square if total is None else total + square
        total = jnp.sum(total, axis=1, keepdims=True)
        line = line + jnp.sum(jnp.where(lane == row + block * width, total, 0.0), axis=0, keepdims=True)
    out_ref[...] = jnp.broadcast_to(line, out_ref.shape)


def totals(where, g, noise, devices):
    vm = pl.BlockSpec(memory_space=pltpu.VMEM)
    return pl.pallas_call(
        total_kernel,
        out_shape=jax.ShapeDtypeStruct((devices, 128), F32),
        in_specs=[pl.BlockSpec(memory_space=pltpu.SMEM), vm, vm],
        out_specs=vm,
        name="totals",
        compiler_params=pltpu.CompilerParams(vmem_limit_bytes=8 << 20),
    )(where, g, noise)


def user_lines(r_ref, line_ref, weight_ref, tile):
    chips, _, lanes = r_ref.shape
    groups = 8
    piece = lanes // groups
    halves = chips // groups
    group = iota((8, lanes), 1) // piece
    sublane = iota((8, lanes), 0)
    rolled = [r_ref[0]] + [pltpu.roll(r_ref[p], p * piece % lanes, 1) if p % groups else r_ref[p] for p in range(1, chips)]

    def gathered(g, half):
        total = None
        for p in range(half * groups, (half + 1) * groups):
            term = jnp.where(group == (p + g) % groups, rolled[p], 0.0)
            total = term if total is None else total + term
        if g:
            total = pltpu.roll(total, lanes - g * piece, 1)
        return total + pltpu.roll(total, 4, 0)

    def line(g):
        return jnp.concatenate([gathered(g, half) for half in range(halves)], axis=1)

    for block in range(2):
        base = block * 4
        from_mate = line(base + 1)
        even = iota(from_mate.shape, 0) % 2 == 0
        swapped = jnp.where(even, pltpu.roll(from_mate, 7, 0), pltpu.roll(from_mate, 1, 0))
        rest = line(base) + swapped
        signal_re = line(base + 2)
        signal_im = line(base + 3)
        strength = signal_re * signal_re + signal_im * signal_im
        level = rest + strength
        line_ref[block, 0] = strength / (rest * level)
        line_ref[block, 1] = signal_re / rest
        line_ref[block, 2] = signal_im / rest
        line_ref[block, 3] = level / rest
        weight_ref[block : block + 1, :] = line_ref[block, 3, pl.ds(tile, 1)]


def regrouped(pieces, wanted):
    lanes = pieces[0].shape[1]
    width = lanes // 8
    group = iota(pieces[0].shape, 1) // width
    rolled = [pltpu.roll(piece, s * width, 1) if s else piece for s, piece in enumerate(pieces)]
    results = []
    for g in range(8):
        if not wanted[g]:
            results.append(None)
            continue
        total = rolled[0]
        for s in range(1, 8):
            total = jnp.where(group == (s + g) % 8, rolled[s], total)
        results.append(pltpu.roll(total, lanes - g * width, 1) if g else total)
    return results


def eliminate(work_ref, sys_ref, scale_ref):
    _, rows, lanes = work_ref.shape
    width = lanes // 8
    lane = iota((8, lanes), 1)
    sublane = iota((8, lanes), 0)
    for high in range(rows // 8):
        at = slice(high * 8, high * 8 + 8)
        groups = regrouped([sys_ref[s, at, :] for s in range(8)], [True] * 8)
        for g in range(8):
            work_ref[g, at, :] = groups[g]

    def spread(value, k):
        return jnp.take_along_axis(value, lane // width * width + k % width, axis=1, mode="promise_in_bounds")

    def row_of(g, k):
        return jnp.broadcast_to(work_ref[g, k : k + 1, :], (8, lanes))

    def pivot(k):
        column = k // width
        line = [row_of(g, k) for g in range(8)]
        value = spread(line[column], k)
        root = lax.rsqrt(value)
        scale_ref[k : k + 1, :] = root[:1]
        line[column] = line[column] + jnp.where(lane % width == k % width, 1.0, 0.0)
        return line, 1.0 / value

    def update(k, high, line, inverse):
        column = k // width
        at = slice(high * 8, high * 8 + 8)
        f_re = spread(work_ref[column, at, :], k) * inverse
        f_im = spread(work_ref[4 + column, at, :], k) * inverse
        if high == k // 8:
            below = sublane > k % 8
            f_re = jnp.where(below, f_re, 0.0)
            f_im = jnp.where(below, f_im, 0.0)
        for c in range(4):
            real, imag = line[c], line[4 + c]
            work_ref[c, at, :] = work_ref[c, at, :] - (f_re * real - f_im * imag)
            work_ref[4 + c, at, :] = work_ref[4 + c, at, :] - (f_re * imag + f_im * real)

    now = pivot(0)
    for k in range(rows - 1):
        first = (k + 1) // 8
        update(k, first, *now)
        later = pivot(k + 1)
        if first != k // 8:
            pass
        for high in range(first + 1, rows // 8):
            update(k, high, *now)
        now = later

    for high in range(rows // 8):
        at = slice(high * 8, high * 8 + 8)
        scale = scale_ref[at, :]
        pieces = []
        for g in range(8):
            start = g % 4 * width
            here = start + lane % width
            row = high * 8 + sublane
            kept = jnp.where(here < row, work_ref[g, at, :], 0.0)
            if g < 4:
                kept = jnp.where(here == row, 1.0, kept)
            pieces.append(kept * scale)
        systems = regrouped(pieces, [True] * 8)
        for s in range(8):
            sys_ref[s, at, :] = systems[s]


def solve_kernel(tile_ref, penalty_ref, power_ref, r_ref, *refs):
    h_refs = refs[:4]
    out_ref, weight_ref, line_ref, sys_ref, work_ref, scale_ref, y_ref, made_ref, sems = refs[4:]
    blocks, _, points, antennas, users = h_refs[0].shape
    size = 2 * antennas
    systems = blocks * points
    tile = tile_ref[0]

    user_lines(r_ref, line_ref, weight_ref, tile)

    def line(block, which, slot):
        return line_ref[block, which, pl.ds(tile ^ SLOTS[slot], 1), :]

    def channel(block, slot, point):
        h_ref = h_refs[slot]
        return jnp.concatenate([h_ref[block, 0, point], h_ref[block, 1, point]], axis=0)

    lane = iota((antennas, size), 1)
    row = iota((antennas, size), 0)
    upper = jnp.where(lane < antennas, 1.0, -1.0).astype(F32)

    for block in range(blocks):
        for point in range(points):
            acc = None
            for slot in range(4):
                x = channel(block, slot, point)
                weighted = x.astype(F32) * line(block, 0, slot)
                parts = jnp.concatenate(two_parts(weighted), axis=0)
                term = dot(x, parts, ((1,), (1,)))
                acc = term if acc is None else acc + term
            p = acc[:, :size] + acc[:, size:]
            a = p[:antennas] * upper + pltpu.roll(p[antennas:], antennas, 1)
            a = a + jnp.where(lane == row, penalty_ref[point], 0.0)
            sys_ref[block * points + point] = a

    eliminate(work_ref, sys_ref, scale_ref)

    copies = []
    for point in range(points):
        total = jnp.zeros((1, users), F32)
        for block in range(blocks):
            n = block * points + point
            z = sys_ref[n]
            q = dot(z, z, ((0,), (0,)), HIGHEST)
            top = q[:antennas] * upper + pltpu.roll(q[antennas:], antennas, 1)
            bottom = pltpu.roll(top, antennas, 1) * (-upper)
            parts = jnp.concatenate(two_parts(jnp.concatenate([top, bottom], axis=0)), axis=1)
            for slot in range(4):
                x = channel(block, slot, point)
                y = dot(parts, jnp.concatenate([x, x], axis=0), ((1,), (0,)))
                w_re, w_im = line(block, 1, slot), line(block, 2, slot)
                total = total + jnp.sum(y * y, axis=0, keepdims=True) * (w_re * w_re + w_im * w_im)
                if slot == 0:
                    y_ref[block] = y
        mean = jnp.sum(total, axis=1, keepdims=True) / (2.0 * blocks * antennas * 4 * users)
        gain = jnp.sqrt(power_ref[point] / (mean + 1e-06))
        for block in range(blocks):
            y_re, y_im = y_ref[block, :antennas], y_ref[block, antennas:]
            w_re = line(block, 1, 0) * gain
            w_im = line(block, 2, 0) * gain
            made_ref[point, block, 0] = (y_re * w_re - y_im * w_im).astype(out_ref.dtype)
            made_ref[point, block, 1] = (y_re * w_im + y_im * w_re).astype(out_ref.dtype)
        copy = pltpu.make_async_copy(made_ref.at[point], out_ref.at[:, :, point], sems.at[point])
        copy.start()
        copies.append(copy)
    for copy in copies:
        copy.wait()


def solve(tile, penalty, power, r, channels, out_shape):
    blocks, _, points, antennas, users = out_shape
    size = 2 * antennas
    vm = pl.BlockSpec(memory_space=pltpu.VMEM)
    sm = pl.BlockSpec(memory_space=pltpu.SMEM)
    return pl.pallas_call(
        solve_kernel,
        out_shape=(
            jax.ShapeDtypeStruct(out_shape, BF16),
            jax.ShapeDtypeStruct((blocks, users), F32),
        ),
        in_specs=[sm] * 3 + [vm] * 5,
        out_specs=(pl.BlockSpec(memory_space=pl.ANY), vm),
        scratch_shapes=[
            pltpu.VMEM((blocks, 4, 8, users), F32),
            pltpu.VMEM((blocks * points, antennas, size), F32),
            pltpu.VMEM((8, antennas, size), F32),
            pltpu.VMEM((antennas, size), F32),
            pltpu.VMEM((blocks, size, users), F32),
            pltpu.VMEM((points, blocks, 2, antennas, users), BF16),
            pltpu.SemaphoreType.DMA((points,)),
        ],
        name="solve",
        compiler_params=pltpu.CompilerParams(vmem_limit_bytes=16 << 20),
    )(tile, penalty, power, r, *channels)


def own_signal(served, precoder):
    chan_re, chan_im = served[0].astype(F32), served[1].astype(F32)
    prec_re, prec_im = precoder[0].astype(F32), precoder[1].astype(F32)
    signal_re = jnp.sum(chan_re * prec_re + chan_im * prec_im, axis=(0, 1))
    signal_im = jnp.sum(chan_re * prec_im - chan_im * prec_re, axis=(0, 1))
    return jnp.stack([signal_re, signal_im])


def across(value, axis, mask):
    size = lax.axis_size(axis)
    return lax.ppermute(value, axis, [(i, i ^ mask) for i in range(size)])


def local(channel, start_precoder, cluster, noise, penalty, power):
    blocks, parts, points, antennas, users = channel.shape
    chips = lax.axis_size(CHIPS)
    devices = lax.axis_size(EVERY)
    piece = users // chips
    rows = parts * points * antennas
    core = lax.axis_index("core")
    tile = lax.axis_index("ut")
    chip = lax.axis_index(CHIPS)

    def masked(field, served):
        return field * served[:, 0].astype(BF16)[None, None, :, None, None]

    near_cluster = across(cluster, "ut", 1)
    near = across(channel, "ut", 1)
    v_far = across(start_precoder, "ut", 3)
    own = masked(channel, cluster)
    near = masked(near, near_cluster)
    far = across(own, "ut", 3)
    far_near = across(near, "ut", 3)

    signal = jnp.concatenate([own_signal(own[b], start_precoder[b]) for b in range(blocks)])
    high = lax.reduce_precision(signal, 8, 7)
    extra = jnp.concatenate([high, signal - high]).astype(BF16)

    keeps, cames = [], []
    flat = [x.reshape(blocks, rows, users) for x in (own, near, start_precoder, v_far)]
    for b in range(blocks):
        keep, send = partial_gains(b, core.reshape(1), *flat, chips)
        keeps.append(keep)
        cames.append(across(send, "core", 1))
    gains = combined(keeps, cames, extra)
    summed = lax.all_to_all(gains, CHIPS, 0, 0, tiled=True)
    line = totals(jnp.stack([chip, core]), summed, noise, devices)
    r = lax.all_to_all(line, EVERY, 0, 0, tiled=True).reshape(chips, devices // chips, 128)

    precoder, weight = solve(tile.reshape(1), penalty, power, r, (own, near, far, far_near), channel.shape)
    return precoder, weight


def solution(mesh):
    split = Mesh(mesh.devices.reshape(4, 4, 2, mesh.shape["ut"]), EVERY)
    placed = (
        P(None, None, AP, None, "ut"),
        P(None, None, AP, None, "ut"),
        P(AP, "ut"),
        P(None, "ut"),
        P(AP),
        P(AP),
    )
    return jax.shard_map(
        local,
        mesh=split,
        in_specs=placed,
        out_specs=(P(None, None, AP, None, "ut"), P(None, "ut")),
        check_vma=False,
    )
```

```python
import functools

import jax
import jax.numpy as jnp
from jax import lax
from jax.experimental import pallas as pl
from jax.experimental.pallas import tpu as pltpu
from jax.sharding import Mesh
from jax.sharding import PartitionSpec as P

AP = ("z", "x", "core")
CHIPS = ("z", "x")
EVERY = ("z", "x", "core", "ut")
SLOTS = (0, 1, 3, 2)
F32 = jnp.float32
BF16 = jnp.bfloat16
HIGHEST = lax.Precision.HIGHEST


def dot(a, b, dims, precision=None):
    return lax.dot_general(a, b, (dims, ((), ())), precision=precision, preferred_element_type=F32)


def two_parts(x):
    high = x.astype(BF16)
    return high, (x - high.astype(F32)).astype(BF16)


def iota(shape, dim):
    return lax.broadcasted_iota(jnp.int32, shape, dim)


def turned(v):
    half = v.shape[0] // 2
    return jnp.concatenate([v[half:], -v[:half]], axis=0)


def own_kernel(h_ref, v_ref, out_ref):
    blocks, _, users = h_ref.shape
    chips = out_ref.shape[0]
    piece = users // chips
    on_diag = iota((users, users), 0) == iota((users, users), 1)
    high, low = [], []
    for block in range(blocks):
        h = jnp.transpose(h_ref[block])
        v = v_ref[block]
        for part, w in enumerate((v, turned(v))):
            g = dot(h, w, ((1,), (0,)))
            own = jnp.sum(jnp.where(on_diag, g, 0.0), axis=0, keepdims=True)
            first, second = two_parts(own)
            high.append(first.astype(F32))
            low.append(second.astype(F32))
            g = jnp.where(on_diag, 0.0, g)
            at = (block * 2 + part) * piece
            out_ref[:, at : at + piece] = g.reshape(chips, piece, users).astype(BF16)
    extra = jnp.concatenate(high + low, axis=0).astype(BF16)
    out_ref[:, 4 * piece :] = jnp.broadcast_to(extra[None], (chips,) + extra.shape)


def own_gains(h, v, chips):
    blocks, _, users = h.shape
    vm = pl.BlockSpec(memory_space=pltpu.VMEM)
    return pl.pallas_call(
        own_kernel,
        out_shape=jax.ShapeDtypeStruct((chips, 4 * (users // chips) + 8, users), BF16),
        in_specs=[vm] * 2,
        out_specs=vm,
        name="own_gains",
        compiler_params=pltpu.CompilerParams(vmem_limit_bytes=8 << 20),
    )(h, v)


def gain_kernel(block, core_ref, ht_ref, ha_ref, vt_ref, vb_ref, keep_ref, send_ref):
    _, _, users = ht_ref.shape
    half = users // 2
    chips = keep_ref.shape[0]
    piece = users // chips
    first = core_ref[0] == 0
    vt, vb = vt_ref[block], vb_ref[block]
    ht, ha = jnp.transpose(ht_ref[block]), jnp.transpose(ha_ref[block])
    for out_ref, low in ((keep_ref, first), (send_ref, jnp.logical_not(first))):
        own = jnp.where(low, vt[:, :half], vt[:, half:])
        far = jnp.where(low, vb[:, :half], vb[:, half:])
        both = jnp.concatenate([own, far], axis=1)
        g = dot(ht, jnp.concatenate([far, turned(far)], axis=1), ((1,), (0,)))
        for part in range(2):
            out_ref[:, part, :, :half] = g[:, part * half : (part + 1) * half].reshape(chips, piece, half).astype(BF16)
        for part, w in enumerate((both, turned(both))):
            out_ref[:, part, :, half:] = dot(ha, w, ((1,), (0,))).reshape(chips, piece, users).astype(BF16)


def partial_gains(block, core, ht, ha, vt, vb, chips):
    _, rows, users = ht.shape
    shape = (chips, 2, users // chips, users + users // 2)
    vm = pl.BlockSpec(memory_space=pltpu.VMEM)
    return pl.pallas_call(
        functools.partial(gain_kernel, block),
        out_shape=(jax.ShapeDtypeStruct(shape, BF16), jax.ShapeDtypeStruct(shape, BF16)),
        in_specs=[pl.BlockSpec(memory_space=pltpu.SMEM)] + [vm] * 4,
        out_specs=(vm, vm),
        name="gains",
        compiler_params=pltpu.CompilerParams(vmem_limit_bytes=8 << 20),
        cost_estimate=pl.CostEstimate(flops=12 * users * users * rows, bytes_accessed=4 << 20, transcendentals=0),
    )(core, ht, ha, vt, vb)


def combine_kernel(keep0_ref, keep1_ref, came0_ref, came1_ref, out_ref):
    chips, _, piece, width = keep0_ref.shape
    rows = 2 * piece
    for block, (keep_ref, came_ref) in enumerate(((keep0_ref, came0_ref), (keep1_ref, came1_ref))):
        g = keep_ref[...] + came_ref[...]
        out_ref[:, block * rows : (block + 1) * rows] = g.reshape(chips, rows, width)


def combined(keeps, cames):
    chips, _, piece, width = keeps[0].shape
    vm = pl.BlockSpec(memory_space=pltpu.VMEM)
    return pl.pallas_call(
        combine_kernel,
        out_shape=jax.ShapeDtypeStruct((chips, 4 * piece, width), BF16),
        in_specs=[vm] * 4,
        out_specs=vm,
        name="combine",
        compiler_params=pltpu.CompilerParams(vmem_limit_bytes=8 << 20),
    )(*keeps, *cames)


def own_sum_kernel(where_ref, g_ref, noise_ref, sum_ref, line_ref):
    chip, core = where_ref[0], where_ref[1]
    chips, rows, users = g_ref.shape
    piece = (rows - 8) // 4
    lanes = line_ref.shape[1]

    def summed(at):
        total = g_ref[0, at].astype(F32)
        for source in range(1, chips):
            total = total + g_ref[source, at].astype(F32)
        return total

    sum_ref[...] = summed(slice(0, 4 * piece))
    extra = summed(slice(4 * piece, 4 * piece + 8))
    signal = extra + pltpu.roll(extra, 4, 0)
    noise = jnp.where(core == 0, noise_ref[...], 0.0)
    signal = jnp.concatenate([signal[:4], noise, noise], axis=0)
    pick = iota((users, lanes), 0) == chip * piece + iota((users, lanes), 1) % piece
    mine = dot(signal, pick.astype(F32), ((1,), (0,)), HIGHEST)
    group = iota((1, lanes), 1) // piece
    line = jnp.zeros((1, lanes), F32)
    for block in range(2):
        for part in range(2):
            at = block * 2 + part
            line = line + jnp.where(group == block * 4 + 2 + part, mine[at : at + 1], 0.0)
        line = line + jnp.where(group == block * 4, mine[4 + block : 5 + block], 0.0)
    line_ref[...] = line


def own_sum(where, g, noise):
    chips, rows, users = g.shape
    vm = pl.BlockSpec(memory_space=pltpu.VMEM)
    return pl.pallas_call(
        own_sum_kernel,
        out_shape=(jax.ShapeDtypeStruct((rows - 8, users), F32), jax.ShapeDtypeStruct((1, 128), F32)),
        in_specs=[pl.BlockSpec(memory_space=pltpu.SMEM), vm, vm],
        out_specs=(vm, vm),
        name="own_sum",
        compiler_params=pltpu.CompilerParams(vmem_limit_bytes=8 << 20),
    )(where, g, noise)


def total_kernel(where_ref, g_ref, mine_ref, came_ref, line_ref, out_ref):
    core = where_ref[1]
    chips, rows, width = g_ref.shape
    piece = rows // 4
    users = mine_ref.shape[1]
    half = width - users
    lanes = out_ref.shape[1]
    lane = iota((piece, lanes), 1)
    row = iota((piece, lanes), 0)
    line = line_ref[...]
    for block in range(2):
        own, near = None, None
        for part in range(2):
            at = slice((block * 2 + part) * piece, (block * 2 + part + 1) * piece)
            g = g_ref[0, at].astype(F32)
            for source in range(1, chips):
                g = g + g_ref[source, at].astype(F32)
            square = g * g
            g = mine_ref[at] + came_ref[at]
            g = jnp.where(core == 0, g, 0.0)
            here = square[:, :half] + g[:, :half] * g[:, :half] + g[:, half:] * g[:, half:]
            there = square[:, half : 2 * half] + square[:, 2 * half :]
            own = here if own is None else own + here
            near = there if near is None else near + there
        for quantity, total in enumerate((own, near)):
            total = jnp.sum(total, axis=1, keepdims=True)
            at = (block * 4 + quantity) * piece
            line = line + jnp.sum(jnp.where(lane == row + at, total, 0.0), axis=0, keepdims=True)
    out_ref[...] = jnp.broadcast_to(line, out_ref.shape)


def totals(where, g, mine, came, line, devices):
    vm = pl.BlockSpec(memory_space=pltpu.VMEM)
    return pl.pallas_call(
        total_kernel,
        out_shape=jax.ShapeDtypeStruct((devices, 128), F32),
        in_specs=[pl.BlockSpec(memory_space=pltpu.SMEM)] + [vm] * 4,
        out_specs=vm,
        name="totals",
        compiler_params=pltpu.CompilerParams(vmem_limit_bytes=8 << 20),
    )(where, g, mine, came, line)


def user_lines(r_ref, line_ref, weight_ref, tile):
    chips, _, lanes = r_ref.shape
    groups = 8
    piece = lanes // groups
    halves = chips // groups
    group = iota((8, lanes), 1) // piece
    sublane = iota((8, lanes), 0)
    rolled = [r_ref[0]] + [pltpu.roll(r_ref[p], p * piece % lanes, 1) if p % groups else r_ref[p] for p in range(1, chips)]

    def gathered(g, half):
        total = None
        for p in range(half * groups, (half + 1) * groups):
            term = jnp.where(group == (p + g) % groups, rolled[p], 0.0)
            total = term if total is None else total + term
        if g:
            total = pltpu.roll(total, lanes - g * piece, 1)
        return total + pltpu.roll(total, 4, 0)

    def line(g):
        return jnp.concatenate([gathered(g, half) for half in range(halves)], axis=1)

    for block in range(2):
        base = block * 4
        from_mate = line(base + 1)
        even = iota(from_mate.shape, 0) % 2 == 0
        swapped = jnp.where(even, pltpu.roll(from_mate, 7, 0), pltpu.roll(from_mate, 1, 0))
        rest = line(base) + swapped
        signal_re = line(base + 2)
        signal_im = line(base + 3)
        strength = signal_re * signal_re + signal_im * signal_im
        level = rest + strength
        line_ref[block, 0] = strength / (rest * level)
        line_ref[block, 1] = signal_re / rest
        line_ref[block, 2] = signal_im / rest
        line_ref[block, 3] = level / rest
        weight_ref[block : block + 1, :] = line_ref[block, 3, pl.ds(tile, 1)]


def picked(pieces, g):
    lanes = pieces[0].shape[1]
    group = iota(pieces[0].shape, 1) // (lanes // 8)
    total = pieces[0]
    for s in range(1, 8):
        total = jnp.where(group == (s + g) % 8, pieces[s], total)
    return total


def eliminate(work_ref, sys_ref, scale_ref):
    _, rows, lanes = work_ref.shape
    width = lanes // 8
    lane = iota((8, lanes), 1)
    sublane = iota((8, lanes), 0)
    for high in range(rows // 8):
        at = slice(high * 8, high * 8 + 8)
        pieces = [sys_ref[s, at, :] for s in range(8)]
        for g in range(8):
            group = picked(pieces, g)
            work_ref[g, at, :] = pltpu.roll(group, lanes - g * width, 1) if g else group

    def spread(value, k):
        return jnp.take_along_axis(value, lane // width * width + k % width, axis=1, mode="promise_in_bounds")

    def row_of(g, k):
        return jnp.broadcast_to(work_ref[g, k : k + 1, :], (8, lanes))

    def pivot(k):
        column = k // width
        line = [row_of(g, k) for g in range(8)]
        value = spread(line[column], k)
        root = lax.rsqrt(value)
        scale_ref[k : k + 1, :] = root[:1]
        line[column] = line[column] + jnp.where(lane % width == k % width, 1.0, 0.0)
        return line, 1.0 / value

    def update(k, high, line, inverse):
        column = k // width
        at = slice(high * 8, high * 8 + 8)
        f_re = spread(work_ref[column, at, :], k) * inverse
        f_im = spread(work_ref[4 + column, at, :], k) * inverse
        if high == k // 8:
            below = sublane > k % 8
            f_re = jnp.where(below, f_re, 0.0)
            f_im = jnp.where(below, f_im, 0.0)
        for c in range(4):
            real, imag = line[c], line[4 + c]
            work_ref[c, at, :] = work_ref[c, at, :] - (f_re * real - f_im * imag)
            work_ref[4 + c, at, :] = work_ref[4 + c, at, :] - (f_re * imag + f_im * real)

    now = pivot(0)
    for k in range(rows - 1):
        first = (k + 1) // 8
        update(k, first, *now)
        later = pivot(k + 1)
        for high in range(first + 1, rows // 8):
            update(k, high, *now)
        now = later

    for high in range(rows // 8):
        at = slice(high * 8, high * 8 + 8)
        scale = scale_ref[at, :]
        pieces = []
        for g in range(8):
            start = g % 4 * width
            here = start + lane % width
            row = high * 8 + sublane
            kept = jnp.where(here < row, work_ref[g, at, :], 0.0)
            if g < 4:
                kept = jnp.where(here == row, 1.0, kept)
            kept = kept * scale
            pieces.append(pltpu.roll(kept, g * width, 1) if g else kept)
        for s in range(8):
            sys_ref[s, at, :] = picked(pieces, s)


def solve_kernel(tile_ref, penalty_ref, power_ref, r_ref, *refs):
    h_refs = refs[:4]
    out_ref, weight_ref, line_ref, sys_ref, work_ref, scale_ref, y_ref, made_ref, sems = refs[4:]
    blocks, _, points, antennas, users = h_refs[0].shape
    size = 2 * antennas
    systems = blocks * points
    tile = tile_ref[0]

    user_lines(r_ref, line_ref, weight_ref, tile)

    def line(block, which, slot):
        return line_ref[block, which, pl.ds(tile ^ SLOTS[slot], 1), :]

    def channel(block, slot, point):
        h_ref = h_refs[slot]
        return jnp.concatenate([h_ref[block, 0, point], h_ref[block, 1, point]], axis=0)

    width = size // systems
    lane = iota((antennas, size), 1)
    row = iota((antennas, size), 0)

    def turn(x, n):
        cut = size - n * width
        return jnp.concatenate([x[cut:], x[:cut]], axis=0) if n else x

    def column(n):
        return (lane + (size - n * width)) % size

    for block in range(blocks):
        for point in range(points):
            n = block * points + point
            xs, highs, lows = [], [], []
            for slot in range(4):
                x = channel(block, slot, point)
                high, low = two_parts(turn(x, n).astype(F32) * line(block, 0, slot))
                xs.append(x)
                highs.append(high)
                lows.append(low)
            parts = jnp.concatenate([jnp.concatenate(highs, axis=1), jnp.concatenate(lows, axis=1)], axis=0)
            acc = dot(jnp.concatenate(xs, axis=1), parts, ((1,), (1,)))
            p = acc[:, :size] + acc[:, size:]
            a = jnp.where(column(n) < antennas, p[:antennas], -p[:antennas]) + pltpu.roll(p[antennas:], antennas, 1)
            a = a + jnp.where(column(n) == row, penalty_ref[point], 0.0)
            sys_ref[n] = a

    eliminate(work_ref, sys_ref, scale_ref)

    copies = []
    for point in range(points):
        total = jnp.zeros((1, users), F32)
        for block in range(blocks):
            n = block * points + point
            high, low = two_parts(sys_ref[n])
            left = jnp.concatenate([high, high, low, low], axis=0)
            right = jnp.concatenate([high, low, high, low], axis=0)
            q = turn(dot(left, right, ((0,), (0,))), (systems - n) % systems)
            top = jnp.where(column(n) < antennas, q[:antennas], -q[:antennas]) + pltpu.roll(q[antennas:], antennas, 1)
            bottom = pltpu.roll(top, antennas, 1)
            bottom = jnp.where(column(n) < antennas, -bottom, bottom)
            parts = jnp.concatenate(two_parts(jnp.concatenate([top, bottom], axis=0)), axis=1)
            for slot in range(4):
                x = turn(channel(block, slot, point), n)
                y = dot(parts, jnp.concatenate([x, x], axis=0), ((1,), (0,)))
                w_re, w_im = line(block, 1, slot), line(block, 2, slot)
                total = total + jnp.sum(y * y, axis=0, keepdims=True) * (w_re * w_re + w_im * w_im)
                if slot == 0:
                    y_ref[block] = y
        mean = jnp.sum(total, axis=1, keepdims=True) / (2.0 * blocks * antennas * 4 * users)
        gain = jnp.sqrt(power_ref[point] / (mean + 1e-06))
        for block in range(blocks):
            y_re, y_im = y_ref[block, :antennas], y_ref[block, antennas:]
            w_re = line(block, 1, 0) * gain
            w_im = line(block, 2, 0) * gain
            made_ref[point, block, 0] = (y_re * w_re - y_im * w_im).astype(out_ref.dtype)
            made_ref[point, block, 1] = (y_re * w_im + y_im * w_re).astype(out_ref.dtype)
        copy = pltpu.make_async_copy(made_ref.at[point], out_ref.at[:, :, point], sems.at[point])
        copy.start()
        copies.append(copy)
    for copy in copies:
        copy.wait()


def solve(tile, penalty, power, r, channels, out_shape):
    blocks, _, points, antennas, users = out_shape
    size = 2 * antennas
    vm = pl.BlockSpec(memory_space=pltpu.VMEM)
    sm = pl.BlockSpec(memory_space=pltpu.SMEM)
    return pl.pallas_call(
        solve_kernel,
        out_shape=(
            jax.ShapeDtypeStruct(out_shape, BF16),
            jax.ShapeDtypeStruct((blocks, users), F32),
        ),
        in_specs=[sm] * 3 + [vm] * 5,
        out_specs=(pl.BlockSpec(memory_space=pl.ANY), vm),
        scratch_shapes=[
            pltpu.VMEM((blocks, 4, 8, users), F32),
            pltpu.VMEM((blocks * points, antennas, size), F32),
            pltpu.VMEM((8, antennas, size), F32),
            pltpu.VMEM((antennas, size), F32),
            pltpu.VMEM((blocks, size, users), F32),
            pltpu.VMEM((points, blocks, 2, antennas, users), BF16),
            pltpu.SemaphoreType.DMA((points,)),
        ],
        name="solve",
        compiler_params=pltpu.CompilerParams(vmem_limit_bytes=16 << 20),
    )(tile, penalty, power, r, *channels)


def across(value, axis, mask):
    size = lax.axis_size(axis)
    return lax.ppermute(value, axis, [(i, i ^ mask) for i in range(size)])


def local(channel, start_precoder, cluster, noise, penalty, power):
    blocks, parts, points, antennas, users = channel.shape
    chips = lax.axis_size(CHIPS)
    devices = lax.axis_size(EVERY)
    piece = users // chips
    rows = parts * points * antennas
    core = lax.axis_index("core")
    tile = lax.axis_index("ut")
    chip = lax.axis_index(CHIPS)

    def masked(field, served):
        return field * served[:, 0].astype(BF16)[None, None, :, None, None]

    near_cluster = across(cluster, "ut", 1)
    near = across(channel, "ut", 1)
    v_far = across(start_precoder, "ut", 3)
    own = masked(channel, cluster)
    near = masked(near, near_cluster)
    far = across(own, "ut", 3)
    far_near = across(near, "ut", 3)

    where = jnp.stack([chip, core])
    flat = [x.reshape(blocks, rows, users) for x in (own, near, start_precoder, v_far)]
    early = lax.all_to_all(own_gains(flat[0], flat[2], chips), CHIPS, 0, 0, tiled=True)

    keeps, cames = [], []
    for b in range(blocks):
        keep, send = partial_gains(b, core.reshape(1), *flat, chips)
        keeps.append(keep)
        cames.append(across(send, "core", 1))
    late = lax.all_to_all(combined(keeps, cames), CHIPS, 0, 0, tiled=True)

    mine, line = own_sum(where, early, noise)
    came = across(mine, "core", 1)
    line = totals(where, late, mine, came, line, devices)
    r = lax.all_to_all(line, EVERY, 0, 0, tiled=True).reshape(chips, devices // chips, 128)

    precoder, weight = solve(tile.reshape(1), penalty, power, r, (own, near, far, far_near), channel.shape)
    return precoder, weight


def solution(mesh):
    split = Mesh(mesh.devices.reshape(4, 4, 2, mesh.shape["ut"]), EVERY)
    placed = (
        P(None, None, AP, None, "ut"),
        P(None, None, AP, None, "ut"),
        P(AP, "ut"),
        P(None, "ut"),
        P(AP),
        P(AP),
    )
    return jax.shard_map(
        local,
        mesh=split,
        in_specs=placed,
        out_specs=(P(None, None, AP, None, "ut"), P(None, "ut")),
        check_vma=False,
    )
```

```python
import functools

import jax
import jax.numpy as jnp
from jax import lax
from jax.experimental import pallas as pl
from jax.experimental.pallas import tpu as pltpu
from jax.sharding import Mesh
from jax.sharding import PartitionSpec as P


AP = ("z", "x", "core")
CHIPS = ("z", "x")
EVERY = ("z", "x", "core", "ut")
SLOTS = (0, 1, 3, 2)
F32 = jnp.float32
BF16 = jnp.bfloat16
HIGHEST = lax.Precision.HIGHEST


def dot(a, b, dims, precision=None):
    return lax.dot_general(a, b, (dims, ((), ())), precision=precision, preferred_element_type=F32)


def two_parts(x):
    high = x.astype(BF16)
    return high, (x - high.astype(F32)).astype(BF16)


def iota(shape, dim):
    return lax.broadcasted_iota(jnp.int32, shape, dim)


def turned(v):
    half = v.shape[0] // 2
    return jnp.concatenate([v[half:], -v[:half]], axis=0)


def signal_kernel(core_ref, cluster_ref, noise_ref, penalty_ref, power_ref, h_ref, v_ref, out_ref, noise_out, penalty_out, power_out):
    blocks, _, points, _, users = h_ref.shape
    chips, lanes = out_ref.shape
    piece = users // chips
    at_chip = iota((chips, users), 1) // piece == iota((chips, users), 0)
    placed = []
    for block in range(blocks):
        real = jnp.zeros((1, users), F32)
        imag = jnp.zeros((1, users), F32)
        for point in range(points):
            h_re, h_im = h_ref[block, 0, point].astype(F32), h_ref[block, 1, point].astype(F32)
            v_re, v_im = v_ref[block, 0, point].astype(F32), v_ref[block, 1, point].astype(F32)
            served = cluster_ref[point, 0].astype(F32)
            real = real + jnp.sum(h_re * v_re + h_im * v_im, axis=0, keepdims=True) * served
            imag = imag + jnp.sum(h_re * v_im - h_im * v_re, axis=0, keepdims=True) * served
        noise = jnp.where(core_ref[0] == 0, noise_ref[block : block + 1], 0.0)
        placed += [jnp.where(at_chip, x, 0.0) for x in (real, imag)]
        noise_out[block : block + 1] = noise
    pick = (iota((users, lanes), 0) % piece == iota((users, lanes), 1) % piece).astype(F32)
    mine = dot(jnp.concatenate(placed, axis=0), pick, ((1,), (0,)), HIGHEST)
    group = iota((chips, lanes), 1) // piece
    line = jnp.zeros((chips, lanes), F32)
    for block in range(blocks):
        for part in range(2):
            at = block * 2 + part
            line = line + jnp.where(group == block * 4 + 2 + part, mine[at * chips : (at + 1) * chips], 0.0)
    out_ref[...] = line
    penalty_out[...] = penalty_ref[...]
    power_out[...] = power_ref[...]


def signals(core, cluster, noise, penalty, power, h, v, chips):
    vm = pl.BlockSpec(memory_space=pltpu.VMEM)
    sm = pl.BlockSpec(memory_space=pltpu.SMEM)
    points = penalty.shape[0]
    return pl.pallas_call(
        signal_kernel,
        out_shape=(
            jax.ShapeDtypeStruct((chips, 128), F32),
            jax.ShapeDtypeStruct(noise.shape, F32),
            jax.ShapeDtypeStruct((1, points), F32),
            jax.ShapeDtypeStruct((1, points), F32),
        ),
        in_specs=[sm] * 2 + [vm] * 5,
        out_specs=(vm,) * 4,
        name="signals",
        compiler_params=pltpu.CompilerParams(vmem_limit_bytes=8 << 20),
    )(core, cluster, noise, penalty.reshape(1, points), power.reshape(1, points), h, v)


def gain_kernel(block, core_ref, ht_ref, ha_ref, vt_ref, vb_ref, keep_ref, send_ref):
    _, _, users = ht_ref.shape
    chips = keep_ref.shape[0]
    piece = users // chips
    vt, vb = vt_ref[block], vb_ref[block]
    first = core_ref[0] == 0
    on_diag = iota((users, users), 0) == iota((users, users), 1)
    hs = [jnp.transpose(h_ref[block]) for h_ref in (ht_ref, ha_ref)]
    for out_ref, own in ((keep_ref, first), (send_ref, jnp.logical_not(first))):
        v = jnp.where(own, vt, vb)
        for part, w in enumerate((v, turned(v))):
            for tile, h in enumerate(hs):
                g = dot(h, w, ((1,), (0,)))
                if tile == 0:
                    g = jnp.where(jnp.logical_and(on_diag, own), 0.0, g)
                out_ref[:, part, tile] = g.reshape(chips, piece, users).astype(BF16)


def partial_gains(block, core, ht, ha, vt, vb, chips):
    _, rows, users = ht.shape
    shape = (chips, 2, 2, users // chips, users)
    vm = pl.BlockSpec(memory_space=pltpu.VMEM)
    return pl.pallas_call(
        functools.partial(gain_kernel, block),
        out_shape=(jax.ShapeDtypeStruct(shape, BF16), jax.ShapeDtypeStruct(shape, BF16)),
        in_specs=[pl.BlockSpec(memory_space=pltpu.SMEM)] + [vm] * 4,
        out_specs=(vm, vm),
        name="gains",
        compiler_params=pltpu.CompilerParams(vmem_limit_bytes=8 << 20),
        cost_estimate=pl.CostEstimate(flops=16 * users * users * rows, bytes_accessed=4 << 20, transcendentals=0),
    )(core, ht, ha, vt, vb)


def combine_kernel(keep0_ref, keep1_ref, came0_ref, came1_ref, out_ref):
    chips, _, _, piece, users = keep0_ref.shape
    rows = 4 * piece
    for block, (keep_ref, came_ref) in enumerate(((keep0_ref, came0_ref), (keep1_ref, came1_ref))):
        g = keep_ref[...] + came_ref[...]
        out_ref[:, block * rows : (block + 1) * rows] = g.reshape(chips, rows, users)


def combined(keeps, cames):
    chips, _, _, piece, users = keeps[0].shape
    vm = pl.BlockSpec(memory_space=pltpu.VMEM)
    return pl.pallas_call(
        combine_kernel,
        out_shape=jax.ShapeDtypeStruct((chips, 8 * piece, users), BF16),
        in_specs=[vm] * 4,
        out_specs=vm,
        name="combine",
        compiler_params=pltpu.CompilerParams(vmem_limit_bytes=8 << 20),
    )(*keeps, *cames)


def total_kernel(chip_ref, g_ref, signal_ref, noise_ref, out_ref):
    chip = chip_ref[0]
    chips, rows, users = g_ref.shape
    piece = rows // 8
    lanes = out_ref.shape[1]
    lane = iota((2 * piece, lanes), 1)
    row = iota((2 * piece, lanes), 0)
    line = jnp.sum(signal_ref[...], axis=0)
    noise = noise_ref[...]
    pick = iota((users, lanes), 0) == chip * piece + iota((users, lanes), 1) % piece
    noise = dot(jnp.concatenate([noise] * 4, axis=0), pick.astype(F32), ((1,), (0,)), HIGHEST)
    group = iota((1, lanes), 1) // piece
    for block in range(2):
        line = line + jnp.where(group == block * 4, noise[block : block + 1], 0.0)
        total = None
        for part in range(2):
            at = slice((block * 2 + part) * 2 * piece, (block * 2 + part + 1) * 2 * piece)
            g = g_ref[0, at].astype(F32)
            for source in range(1, chips):
                g = g + g_ref[source, at].astype(F32)
            total = g * g if total is None else total + g * g
        total = jnp.sum(total, axis=1, keepdims=True)
        line = line + jnp.sum(jnp.where(lane == row + block * 4 * piece, total, 0.0), axis=0, keepdims=True)
    out_ref[...] = jnp.broadcast_to(line, out_ref.shape)


def totals(chip, g, signal, noise, devices):
    vm = pl.BlockSpec(memory_space=pltpu.VMEM)
    return pl.pallas_call(
        total_kernel,
        out_shape=jax.ShapeDtypeStruct((devices, 128), F32),
        in_specs=[pl.BlockSpec(memory_space=pltpu.SMEM)] + [vm] * 3,
        out_specs=vm,
        name="totals",
        compiler_params=pltpu.CompilerParams(vmem_limit_bytes=8 << 20),
    )(chip, g, signal, noise)


def user_lines(r_ref, line_ref, weight_ref, tile):
    chips, _, lanes = r_ref.shape
    groups = 8
    piece = lanes // groups
    halves = chips // groups
    group = iota((8, lanes), 1) // piece
    sublane = iota((8, lanes), 0)
    rolled = [r_ref[0]] + [pltpu.roll(r_ref[p], p * piece % lanes, 1) if p % groups else r_ref[p] for p in range(1, chips)]

    def gathered(g, half):
        total = None
        for p in range(half * groups, (half + 1) * groups):
            term = jnp.where(group == (p + g) % groups, rolled[p], 0.0)
            total = term if total is None else total + term
        if g:
            total = pltpu.roll(total, lanes - g * piece, 1)
        return total + pltpu.roll(total, 4, 0)

    def line(g):
        return jnp.concatenate([gathered(g, half) for half in range(halves)], axis=1)

    for block in range(2):
        base = block * 4
        from_mate = line(base + 1)
        even = iota(from_mate.shape, 0) % 2 == 0
        swapped = jnp.where(even, pltpu.roll(from_mate, 7, 0), pltpu.roll(from_mate, 1, 0))
        rest = line(base) + swapped
        signal_re = line(base + 2)
        signal_im = line(base + 3)
        strength = signal_re * signal_re + signal_im * signal_im
        level = rest + strength
        line_ref[block, 0] = strength / (rest * level)
        line_ref[block, 1] = signal_re / rest
        line_ref[block, 2] = signal_im / rest
        line_ref[block, 3] = level / rest
        weight_ref[block : block + 1, :] = line_ref[block, 3, pl.ds(tile, 1)]


def picked(pieces, g):
    lanes = pieces[0].shape[1]
    group = iota(pieces[0].shape, 1) // (lanes // 8)
    total = pieces[0]
    for s in range(1, 8):
        total = jnp.where(group == (s + g) % 8, pieces[s], total)
    return total


def eliminate(work_ref, sys_ref, scale_ref):
    _, rows, lanes = work_ref.shape
    width = lanes // 8
    lane = iota((8, lanes), 1)
    sublane = iota((8, lanes), 0)
    for high in range(rows // 8):
        at = slice(high * 8, high * 8 + 8)
        pieces = [sys_ref[s, at, :] for s in range(8)]
        for g in range(8):
            group = picked(pieces, g)
            work_ref[g, at, :] = pltpu.roll(group, lanes - g * width, 1) if g else group

    def spread(value, k):
        return jnp.take_along_axis(value, lane // width * width + k % width, axis=1, mode="promise_in_bounds")

    def row_of(g, k):
        return jnp.broadcast_to(work_ref[g, k : k + 1, :], (8, lanes))

    def pivot(k):
        column = k // width
        line = [row_of(g, k) for g in range(8)]
        value = spread(line[column], k)
        root = lax.rsqrt(value)
        scale_ref[k : k + 1, :] = root[:1]
        line[column] = line[column] + jnp.where(lane % width == k % width, 1.0, 0.0)
        return line, 1.0 / value

    def update(k, high, line, inverse):
        column = k // width
        at = slice(high * 8, high * 8 + 8)
        f_re = spread(work_ref[column, at, :], k) * inverse
        f_im = spread(work_ref[4 + column, at, :], k) * inverse
        if high == k // 8:
            below = sublane > k % 8
            f_re = jnp.where(below, f_re, 0.0)
            f_im = jnp.where(below, f_im, 0.0)
        for c in range(4):
            real, imag = line[c], line[4 + c]
            work_ref[c, at, :] = work_ref[c, at, :] - (f_re * real - f_im * imag)
            work_ref[4 + c, at, :] = work_ref[4 + c, at, :] - (f_re * imag + f_im * real)

    now = pivot(0)
    for k in range(rows - 1):
        first = (k + 1) // 8
        update(k, first, *now)
        later = pivot(k + 1)
        for high in range(first + 1, rows // 8):
            update(k, high, *now)
        now = later

    for high in range(rows // 8):
        at = slice(high * 8, high * 8 + 8)
        scale = scale_ref[at, :]
        pieces = []
        for g in range(8):
            start = g % 4 * width
            here = start + lane % width
            row = high * 8 + sublane
            kept = jnp.where(here < row, work_ref[g, at, :], 0.0)
            if g < 4:
                kept = jnp.where(here == row, 1.0, kept)
            kept = kept * scale
            pieces.append(pltpu.roll(kept, g * width, 1) if g else kept)
        for s in range(8):
            sys_ref[s, at, :] = picked(pieces, s)


def solve_kernel(tile_ref, penalty_ref, power_ref, r_ref, *refs):
    h_refs = refs[:4]
    out_ref, weight_ref, line_ref, sys_ref, work_ref, scale_ref, y_ref, made_ref, sems = refs[4:]
    blocks, _, points, antennas, users = h_refs[0].shape
    size = 2 * antennas
    systems = blocks * points
    tile = tile_ref[0]

    user_lines(r_ref, line_ref, weight_ref, tile)

    def line(block, which, slot):
        return line_ref[block, which, pl.ds(tile ^ SLOTS[slot], 1), :]

    def channel(block, slot, point):
        h_ref = h_refs[slot]
        return jnp.concatenate([h_ref[block, 0, point], h_ref[block, 1, point]], axis=0)

    width = size // systems
    lane = iota((antennas, size), 1)
    row = iota((antennas, size), 0)

    def turn(x, n):
        cut = size - n * width
        return jnp.concatenate([x[cut:], x[:cut]], axis=0) if n else x

    def column(n):
        return (lane + (size - n * width)) % size

    for block in range(blocks):
        for point in range(points):
            n = block * points + point
            xs, highs, lows = [], [], []
            for slot in range(4):
                x = channel(block, slot, point)
                high, low = two_parts(turn(x, n).astype(F32) * line(block, 0, slot))
                xs.append(x)
                highs.append(high)
                lows.append(low)
            parts = jnp.concatenate([jnp.concatenate(highs, axis=1), jnp.concatenate(lows, axis=1)], axis=0)
            acc = dot(jnp.concatenate(xs, axis=1), parts, ((1,), (1,)))
            p = acc[:, :size] + acc[:, size:]
            a = jnp.where(column(n) < antennas, p[:antennas], -p[:antennas]) + pltpu.roll(p[antennas:], antennas, 1)
            a = a + jnp.where(column(n) == row, penalty_ref[0, point], 0.0)
            sys_ref[n] = a

    eliminate(work_ref, sys_ref, scale_ref)

    copies = []
    for point in range(points):
        total = jnp.zeros((1, users), F32)
        for block in range(blocks):
            n = block * points + point
            high, low = two_parts(sys_ref[n])
            left = jnp.concatenate([high, high, low, low], axis=0)
            right = jnp.concatenate([high, low, high, low], axis=0)
            q = turn(dot(left, right, ((0,), (0,))), (systems - n) % systems)
            top = jnp.where(column(n) < antennas, q[:antennas], -q[:antennas]) + pltpu.roll(q[antennas:], antennas, 1)
            bottom = pltpu.roll(top, antennas, 1)
            bottom = jnp.where(column(n) < antennas, -bottom, bottom)
            parts = jnp.concatenate(two_parts(jnp.concatenate([top, bottom], axis=0)), axis=1)
            for slot in range(4):
                x = turn(channel(block, slot, point), n)
                y = dot(parts, jnp.concatenate([x, x], axis=0), ((1,), (0,)))
                w_re, w_im = line(block, 1, slot), line(block, 2, slot)
                total = total + jnp.sum(y * y, axis=0, keepdims=True) * (w_re * w_re + w_im * w_im)
                if slot == 0:
                    y_ref[block] = y
        mean = jnp.sum(total, axis=1, keepdims=True) / (2.0 * blocks * antennas * 4 * users)
        gain = jnp.sqrt(power_ref[0, point] / (mean + 1e-06))
        for block in range(blocks):
            y_re, y_im = y_ref[block, :antennas], y_ref[block, antennas:]
            w_re = line(block, 1, 0) * gain
            w_im = line(block, 2, 0) * gain
            made_ref[point, block, 0] = (y_re * w_re - y_im * w_im).astype(out_ref.dtype)
            made_ref[point, block, 1] = (y_re * w_im + y_im * w_re).astype(out_ref.dtype)
        copy = pltpu.make_async_copy(made_ref.at[point], out_ref.at[:, :, point], sems.at[point])
        copy.start()
        copies.append(copy)
    for copy in copies:
        copy.wait()


def solve(tile, penalty, power, r, channels, out_shape):
    blocks, _, points, antennas, users = out_shape
    size = 2 * antennas
    vm = pl.BlockSpec(memory_space=pltpu.VMEM)
    sm = pl.BlockSpec(memory_space=pltpu.SMEM)
    return pl.pallas_call(
        solve_kernel,
        out_shape=(
            jax.ShapeDtypeStruct(out_shape, BF16),
            jax.ShapeDtypeStruct((blocks, users), F32),
        ),
        in_specs=[sm] * 3 + [vm] * 5,
        out_specs=(pl.BlockSpec(memory_space=pl.ANY), vm),
        scratch_shapes=[
            pltpu.VMEM((blocks, 4, 8, users), F32),
            pltpu.VMEM((blocks * points, antennas, size), F32),
            pltpu.VMEM((8, antennas, size), F32),
            pltpu.VMEM((antennas, size), F32),
            pltpu.VMEM((blocks, size, users), F32),
            pltpu.VMEM((points, blocks, 2, antennas, users), BF16),
            pltpu.SemaphoreType.DMA((points,)),
        ],
        name="solve",
        compiler_params=pltpu.CompilerParams(vmem_limit_bytes=16 << 20),
    )(tile, penalty, power, r, *channels)


def across(value, axis, mask):
    size = lax.axis_size(axis)
    return lax.ppermute(value, axis, [(i, i ^ mask) for i in range(size)])


def local(channel, start_precoder, cluster, noise, penalty, power):
    blocks, parts, points, antennas, users = channel.shape
    chips = lax.axis_size(CHIPS)
    devices = lax.axis_size(EVERY)
    rows = parts * points * antennas
    core = lax.axis_index("core")
    tile = lax.axis_index("ut")
    chip = lax.axis_index(CHIPS)

    def masked(field, served):
        return field * served[:, 0].astype(BF16)[None, None, :, None, None]

    near_cluster = across(cluster, "ut", 1)
    near = across(channel, "ut", 1)
    v_far = across(start_precoder, "ut", 3)
    own = masked(channel, cluster)
    near = masked(near, near_cluster)
    far = across(own, "ut", 3)
    far_near = across(near, "ut", 3)

    core, chip = core.reshape(1), chip.reshape(1)
    signal, noise, penalty, power = signals(core, cluster, noise, penalty, power, channel, start_precoder, chips)
    signal = lax.all_to_all(signal.reshape(chips, 1, 128), CHIPS, 0, 0, tiled=True)

    flat = [x.reshape(blocks, rows, users) for x in (own, near, start_precoder, v_far)]
    keeps, cames = [], []
    for b in range(blocks):
        keep, send = partial_gains(b, core, *flat, chips)
        keeps.append(keep)
        cames.append(across(send, "core", 1))
    late = lax.all_to_all(combined(keeps, cames), CHIPS, 0, 0, tiled=True)
    line = totals(chip, late, signal, noise, devices)
    r = lax.all_to_all(line, EVERY, 0, 0, tiled=True).reshape(chips, devices // chips, 128)

    precoder, weight = solve(tile.reshape(1), penalty, power, r, (own, near, far, far_near), channel.shape)
    return precoder, weight


def solution(mesh):
    split = Mesh(mesh.devices.reshape(4, 4, 2, mesh.shape["ut"]), EVERY)
    placed = (
        P(None, None, AP, None, "ut"),
        P(None, None, AP, None, "ut"),
        P(AP, "ut"),
        P(None, "ut"),
        P(AP),
        P(AP),
    )

    return jax.shard_map(
        local,
        mesh=split,
        in_specs=placed,
        out_specs=(P(None, None, AP, None, "ut"), P(None, "ut")),
        check_vma=False,
    )
```

```python
import functools

import jax
import jax.numpy as jnp
from jax import lax
from jax.experimental import pallas as pl
from jax.experimental.pallas import tpu as pltpu
from jax.sharding import Mesh
from jax.sharding import PartitionSpec as P


AP = ("z", "x", "core")
CHIPS = ("z", "x")
EVERY = ("z", "x", "core", "ut")
SLOTS = (0, 1, 3, 2)
F32 = jnp.float32
BF16 = jnp.bfloat16
HIGHEST = lax.Precision.HIGHEST


def dot(a, b, dims, precision=None):
    return lax.dot_general(a, b, (dims, ((), ())), precision=precision, preferred_element_type=F32)


def two_parts(x):
    high = x.astype(BF16)
    return high, (x - high.astype(F32)).astype(BF16)


def iota(shape, dim):
    return lax.broadcasted_iota(jnp.int32, shape, dim)


def turned(v):
    half = v.shape[0] // 2
    return jnp.concatenate([v[half:], -v[:half]], axis=0)


def own_kernel(cluster_ref, h_any, v_any, out_ref, own_ref, v_ref, h_ref, sems):
    blocks, parts, points, antennas, users = h_ref.shape
    chips = out_ref.shape[0]
    piece = users // chips
    copies = []
    for block in range(blocks):
        for source, target in ((h_any, h_ref), (v_any, v_ref)):
            copy = pltpu.make_async_copy(source.at[block], target.at[block], sems.at[len(copies)])
            copy.start()
            copies.append(copy)
    on_diag = iota((users, users), 0) == iota((users, users), 1)
    high, low = [], []
    for block in range(blocks):
        copies[2 * block].wait()
        for point in range(points):
            served = cluster_ref[point, 0].astype(F32)
            for part in range(parts):
                own_ref[block, part, point] = (h_ref[block, part, point].astype(F32) * served).astype(BF16)
        copies[2 * block + 1].wait()
        h = jnp.transpose(own_ref[block].reshape(parts * points * antennas, users))
        v = v_ref[block].reshape(parts * points * antennas, users)
        for part, w in enumerate((v, turned(v))):
            g = dot(h, w, ((1,), (0,)))
            own = jnp.sum(jnp.where(on_diag, g, 0.0), axis=0, keepdims=True)
            first, second = two_parts(own)
            high.append(first.astype(F32))
            low.append(second.astype(F32))
            g = jnp.where(on_diag, 0.0, g)
            at = (block * 2 + part) * piece
            out_ref[:, at : at + piece] = g.reshape(chips, piece, users).astype(BF16)
    extra = jnp.concatenate(high + low, axis=0).astype(BF16)
    out_ref[:, 4 * piece :] = jnp.broadcast_to(extra[None], (chips,) + extra.shape)


def own_gains(cluster, h, v, chips):
    users = h.shape[-1]
    vm = pl.BlockSpec(memory_space=pltpu.VMEM)
    raw = pl.BlockSpec(memory_space=pltpu.HBM)
    return pl.pallas_call(
        own_kernel,
        out_shape=(
            jax.ShapeDtypeStruct((chips, 4 * (users // chips) + 8, users), BF16),
            jax.ShapeDtypeStruct(h.shape, BF16),
            jax.ShapeDtypeStruct(v.shape, BF16),
        ),
        in_specs=[pl.BlockSpec(memory_space=pltpu.SMEM), raw, raw],
        out_specs=(vm,) * 3,
        scratch_shapes=[pltpu.VMEM(h.shape, BF16), pltpu.SemaphoreType.DMA((2 * h.shape[0],))],
        name="own_gains",
        compiler_params=pltpu.CompilerParams(vmem_limit_bytes=8 << 20),
    )(cluster, h, v)


def gain_kernel(block, core_ref, ht_ref, ha_ref, vt_ref, vb_ref, keep_ref, send_ref):
    _, _, users = ht_ref.shape
    half = users // 2
    chips = keep_ref.shape[0]
    piece = users // chips
    first = core_ref[0] == 0
    vt, vb = vt_ref[block], vb_ref[block]
    ht, ha = jnp.transpose(ht_ref[block]), jnp.transpose(ha_ref[block])
    for out_ref, low in ((keep_ref, first), (send_ref, jnp.logical_not(first))):
        own = jnp.where(low, vt[:, :half], vt[:, half:])
        far = jnp.where(low, vb[:, :half], vb[:, half:])
        both = jnp.concatenate([own, far], axis=1)
        g = dot(ht, jnp.concatenate([far, turned(far)], axis=1), ((1,), (0,)))
        for part in range(2):
            out_ref[:, part, :, :half] = g[:, part * half : (part + 1) * half].reshape(chips, piece, half).astype(BF16)
        for part, w in enumerate((both, turned(both))):
            out_ref[:, part, :, half:] = dot(ha, w, ((1,), (0,))).reshape(chips, piece, users).astype(BF16)


def partial_gains(block, core, ht, ha, vt, vb, chips):
    _, rows, users = ht.shape
    shape = (chips, 2, users // chips, users + users // 2)
    vm = pl.BlockSpec(memory_space=pltpu.VMEM)
    return pl.pallas_call(
        functools.partial(gain_kernel, block),
        out_shape=(jax.ShapeDtypeStruct(shape, BF16), jax.ShapeDtypeStruct(shape, BF16)),
        in_specs=[pl.BlockSpec(memory_space=pltpu.SMEM)] + [vm] * 4,
        out_specs=(vm, vm),
        name="gains",
        compiler_params=pltpu.CompilerParams(vmem_limit_bytes=8 << 20),
        cost_estimate=pl.CostEstimate(flops=12 * users * users * rows, bytes_accessed=4 << 20, transcendentals=0),
    )(core, ht, ha, vt, vb)


def combine_kernel(keep0_ref, keep1_ref, came0_ref, came1_ref, out_ref):
    chips, _, piece, width = keep0_ref.shape
    rows = 2 * piece
    for block, (keep_ref, came_ref) in enumerate(((keep0_ref, came0_ref), (keep1_ref, came1_ref))):
        g = keep_ref[...] + came_ref[...]
        out_ref[:, block * rows : (block + 1) * rows] = g.reshape(chips, rows, width)


def combined(keeps, cames):
    chips, _, piece, width = keeps[0].shape
    vm = pl.BlockSpec(memory_space=pltpu.VMEM)
    return pl.pallas_call(
        combine_kernel,
        out_shape=jax.ShapeDtypeStruct((chips, 4 * piece, width), BF16),
        in_specs=[vm] * 4,
        out_specs=vm,
        name="combine",
        compiler_params=pltpu.CompilerParams(vmem_limit_bytes=8 << 20),
    )(*keeps, *cames)


def own_sum_kernel(where_ref, g_ref, noise_ref, penalty_ref, power_ref, sum_ref, line_ref, penalty_out, power_out):
    chip, core = where_ref[0], where_ref[1]
    chips, rows, users = g_ref.shape
    piece = (rows - 8) // 4
    lanes = line_ref.shape[1]

    def summed(at):
        total = g_ref[0, at].astype(F32)
        for source in range(1, chips):
            total = total + g_ref[source, at].astype(F32)
        return total

    sum_ref[...] = summed(slice(0, 4 * piece))
    extra = summed(slice(4 * piece, 4 * piece + 8))
    signal = extra + pltpu.roll(extra, 4, 0)
    noise = jnp.where(core == 0, noise_ref[...], 0.0)
    signal = jnp.concatenate([signal[:4], noise, noise], axis=0)
    pick = iota((users, lanes), 0) == chip * piece + iota((users, lanes), 1) % piece
    mine = dot(signal, pick.astype(F32), ((1,), (0,)), HIGHEST)
    group = iota((1, lanes), 1) // piece
    line = jnp.zeros((1, lanes), F32)
    for block in range(2):
        for part in range(2):
            at = block * 2 + part
            line = line + jnp.where(group == block * 4 + 2 + part, mine[at : at + 1], 0.0)
        line = line + jnp.where(group == block * 4, mine[4 + block : 5 + block], 0.0)
    line_ref[...] = line
    penalty_out[...] = penalty_ref[...]
    power_out[...] = power_ref[...]


def own_sum(where, g, noise, penalty, power):
    _, rows, users = g.shape
    points = penalty.shape[0]
    vm = pl.BlockSpec(memory_space=pltpu.VMEM)
    return pl.pallas_call(
        own_sum_kernel,
        out_shape=(
            jax.ShapeDtypeStruct((rows - 8, users), F32),
            jax.ShapeDtypeStruct((1, 128), F32),
            jax.ShapeDtypeStruct((1, points), F32),
            jax.ShapeDtypeStruct((1, points), F32),
        ),
        in_specs=[pl.BlockSpec(memory_space=pltpu.SMEM)] + [vm] * 4,
        out_specs=(vm,) * 4,
        name="own_sum",
        compiler_params=pltpu.CompilerParams(vmem_limit_bytes=8 << 20),
    )(where, g, noise, penalty.reshape(1, points), power.reshape(1, points))


def placed(line, total, start):
    lane = iota((total.shape[0], line.shape[1]), 1)
    row = iota((total.shape[0], line.shape[1]), 0)
    return line + jnp.sum(jnp.where(lane == row + start, total, 0.0), axis=0, keepdims=True)


def own_total_kernel(where_ref, mine_ref, came_ref, line_ref, out_ref):
    piece = mine_ref.shape[0] // 4
    line = line_ref[...]
    g = jnp.where(where_ref[1] == 0, mine_ref[...] + came_ref[...], 0.0)
    square = jnp.sum(g * g, axis=1, keepdims=True)
    for block in range(2):
        at = 2 * block * piece
        line = placed(line, square[at : at + piece] + square[at + piece : at + 2 * piece], 4 * block * piece)
    out_ref[...] = line


def own_total(where, mine, came, line):
    vm = pl.BlockSpec(memory_space=pltpu.VMEM)
    return pl.pallas_call(
        own_total_kernel,
        out_shape=jax.ShapeDtypeStruct(line.shape, F32),
        in_specs=[pl.BlockSpec(memory_space=pltpu.SMEM)] + [vm] * 3,
        out_specs=vm,
        name="own_total",
        compiler_params=pltpu.CompilerParams(vmem_limit_bytes=4 << 20),
    )(where, mine, came, line)


def total_kernel(g_ref, line_ref, out_ref):
    chips, rows, width = g_ref.shape
    piece = rows // 4
    half = width // 3
    line = line_ref[...]
    for block in range(2):
        square = None
        for part in range(2):
            at = slice((block * 2 + part) * piece, (block * 2 + part + 1) * piece)
            g = g_ref[0, at].astype(F32)
            for source in range(1, chips):
                g = g + g_ref[source, at].astype(F32)
            square = g * g if square is None else square + g * g
        own = jnp.sum(square[:, :half], axis=1, keepdims=True)
        near = jnp.sum(square[:, half : 2 * half] + square[:, 2 * half :], axis=1, keepdims=True)
        line = placed(placed(line, own, block * 4 * piece), near, (block * 4 + 1) * piece)
    out_ref[...] = jnp.broadcast_to(line, out_ref.shape)


def totals(g, line, devices):
    vm = pl.BlockSpec(memory_space=pltpu.VMEM)
    return pl.pallas_call(
        total_kernel,
        out_shape=jax.ShapeDtypeStruct((devices, 128), F32),
        in_specs=[vm] * 2,
        out_specs=vm,
        name="totals",
        compiler_params=pltpu.CompilerParams(vmem_limit_bytes=8 << 20),
    )(g, line)


def user_lines(r_ref, line_ref, weight_ref, tile):
    chips, _, lanes = r_ref.shape
    groups = 8
    piece = lanes // groups
    halves = chips // groups
    group = iota((8, lanes), 1) // piece
    sublane = iota((8, lanes), 0)
    rolled = [r_ref[0]] + [pltpu.roll(r_ref[p], p * piece % lanes, 1) if p % groups else r_ref[p] for p in range(1, chips)]

    def gathered(g, half):
        total = None
        for p in range(half * groups, (half + 1) * groups):
            term = jnp.where(group == (p + g) % groups, rolled[p], 0.0)
            total = term if total is None else total + term
        if g:
            total = pltpu.roll(total, lanes - g * piece, 1)
        return total + pltpu.roll(total, 4, 0)

    def line(g):
        return jnp.concatenate([gathered(g, half) for half in range(halves)], axis=1)

    for block in range(2):
        base = block * 4
        from_mate = line(base + 1)
        even = iota(from_mate.shape, 0) % 2 == 0
        swapped = jnp.where(even, pltpu.roll(from_mate, 7, 0), pltpu.roll(from_mate, 1, 0))
        rest = line(base) + swapped
        signal_re = line(base + 2)
        signal_im = line(base + 3)
        strength = signal_re * signal_re + signal_im * signal_im
        level = rest + strength
        line_ref[block, 0] = strength / (rest * level)
        line_ref[block, 1] = signal_re / rest
        line_ref[block, 2] = signal_im / rest
        line_ref[block, 3] = level / rest
        weight_ref[block : block + 1, :] = line_ref[block, 3, pl.ds(tile, 1)]


def picked(pieces, g):
    lanes = pieces[0].shape[1]
    group = iota(pieces[0].shape, 1) // (lanes // 8)
    total = pieces[0]
    for s in range(1, 8):
        total = jnp.where(group == (s + g) % 8, pieces[s], total)
    return total


def eliminate(work_ref, sys_ref, scale_ref):
    _, rows, lanes = work_ref.shape
    width = lanes // 8
    lane = iota((8, lanes), 1)
    sublane = iota((8, lanes), 0)
    for high in range(rows // 8):
        at = slice(high * 8, high * 8 + 8)
        pieces = [sys_ref[s, at, :] for s in range(8)]
        for g in range(8):
            group = picked(pieces, g)
            work_ref[g, at, :] = pltpu.roll(group, lanes - g * width, 1) if g else group

    def spread(value, k):
        return jnp.take_along_axis(value, lane // width * width + k % width, axis=1, mode="promise_in_bounds")

    def row_of(g, k):
        return jnp.broadcast_to(work_ref[g, k : k + 1, :], (8, lanes))

    def pivot(k):
        column = k // width
        line = [row_of(g, k) for g in range(8)]
        value = spread(line[column], k)
        root = lax.rsqrt(value)
        scale_ref[k : k + 1, :] = root[:1]
        line[column] = line[column] + jnp.where(lane % width == k % width, 1.0, 0.0)
        return line, 1.0 / value

    def update(k, high, line, inverse):
        column = k // width
        at = slice(high * 8, high * 8 + 8)
        f_re = spread(work_ref[column, at, :], k) * inverse
        f_im = spread(work_ref[4 + column, at, :], k) * inverse
        if high == k // 8:
            below = sublane > k % 8
            f_re = jnp.where(below, f_re, 0.0)
            f_im = jnp.where(below, f_im, 0.0)
        for c in range(4):
            real, imag = line[c], line[4 + c]
            work_ref[c, at, :] = work_ref[c, at, :] - (f_re * real - f_im * imag)
            work_ref[4 + c, at, :] = work_ref[4 + c, at, :] - (f_re * imag + f_im * real)

    now = pivot(0)
    for k in range(rows - 1):
        first = (k + 1) // 8
        update(k, first, *now)
        later = pivot(k + 1)
        for high in range(first + 1, rows // 8):
            update(k, high, *now)
        now = later

    for high in range(rows // 8):
        at = slice(high * 8, high * 8 + 8)
        scale = scale_ref[at, :]
        pieces = []
        for g in range(8):
            start = g % 4 * width
            here = start + lane % width
            row = high * 8 + sublane
            kept = jnp.where(here < row, work_ref[g, at, :], 0.0)
            if g < 4:
                kept = jnp.where(here == row, 1.0, kept)
            kept = kept * scale
            pieces.append(pltpu.roll(kept, g * width, 1) if g else kept)
        for s in range(8):
            sys_ref[s, at, :] = picked(pieces, s)


def solve_kernel(tile_ref, penalty_ref, power_ref, r_ref, *refs):
    h_refs = refs[:4]
    out_ref, weight_ref, line_ref, sys_ref, work_ref, scale_ref, y_ref, made_ref, sems = refs[4:]
    blocks, _, points, antennas, users = h_refs[0].shape
    size = 2 * antennas
    systems = blocks * points
    tile = tile_ref[0]

    user_lines(r_ref, line_ref, weight_ref, tile)

    def line(block, which, slot):
        return line_ref[block, which, pl.ds(tile ^ SLOTS[slot], 1), :]

    def channel(block, slot, point):
        h_ref = h_refs[slot]
        return jnp.concatenate([h_ref[block, 0, point], h_ref[block, 1, point]], axis=0)

    width = size // systems
    lane = iota((antennas, size), 1)
    row = iota((antennas, size), 0)

    def turn(x, n):
        cut = size - n * width
        return jnp.concatenate([x[cut:], x[:cut]], axis=0) if n else x

    def column(n):
        return (lane + (size - n * width)) % size

    for block in range(blocks):
        for point in range(points):
            n = block * points + point
            xs, highs, lows = [], [], []
            for slot in range(4):
                x = channel(block, slot, point)
                high, low = two_parts(turn(x, n).astype(F32) * line(block, 0, slot))
                xs.append(x)
                highs.append(high)
                lows.append(low)
            parts = jnp.concatenate([jnp.concatenate(highs, axis=1), jnp.concatenate(lows, axis=1)], axis=0)
            acc = dot(jnp.concatenate(xs, axis=1), parts, ((1,), (1,)))
            p = acc[:, :size] + acc[:, size:]
            a = jnp.where(column(n) < antennas, p[:antennas], -p[:antennas]) + pltpu.roll(p[antennas:], antennas, 1)
            a = a + jnp.where(column(n) == row, penalty_ref[0, point], 0.0)
            sys_ref[n] = a

    eliminate(work_ref, sys_ref, scale_ref)

    copies = []
    for point in range(points):
        total = jnp.zeros((1, users), F32)
        for block in range(blocks):
            n = block * points + point
            high, low = two_parts(sys_ref[n])
            left = jnp.concatenate([high, high, low, low], axis=0)
            right = jnp.concatenate([high, low, high, low], axis=0)
            q = turn(dot(left, right, ((0,), (0,))), (systems - n) % systems)
            top = jnp.where(column(n) < antennas, q[:antennas], -q[:antennas]) + pltpu.roll(q[antennas:], antennas, 1)
            bottom = pltpu.roll(top, antennas, 1)
            bottom = jnp.where(column(n) < antennas, -bottom, bottom)
            parts = jnp.concatenate(two_parts(jnp.concatenate([top, bottom], axis=0)), axis=1)
            for slot in range(4):
                x = turn(channel(block, slot, point), n)
                y = dot(parts, jnp.concatenate([x, x], axis=0), ((1,), (0,)))
                w_re, w_im = line(block, 1, slot), line(block, 2, slot)
                total = total + jnp.sum(y * y, axis=0, keepdims=True) * (w_re * w_re + w_im * w_im)
                if slot == 0:
                    y_ref[block] = y
        mean = jnp.sum(total, axis=1, keepdims=True) / (2.0 * blocks * antennas * 4 * users)
        gain = jnp.sqrt(power_ref[0, point] / (mean + 1e-06))
        for block in range(blocks):
            y_re, y_im = y_ref[block, :antennas], y_ref[block, antennas:]
            w_re = line(block, 1, 0) * gain
            w_im = line(block, 2, 0) * gain
            made_ref[point, block, 0] = (y_re * w_re - y_im * w_im).astype(out_ref.dtype)
            made_ref[point, block, 1] = (y_re * w_im + y_im * w_re).astype(out_ref.dtype)
        copy = pltpu.make_async_copy(made_ref.at[point], out_ref.at[:, :, point], sems.at[point])
        copy.start()
        copies.append(copy)
    for copy in copies:
        copy.wait()


def solve(tile, penalty, power, r, channels, out_shape):
    blocks, _, points, antennas, users = out_shape
    size = 2 * antennas
    vm = pl.BlockSpec(memory_space=pltpu.VMEM)
    sm = pl.BlockSpec(memory_space=pltpu.SMEM)
    return pl.pallas_call(
        solve_kernel,
        out_shape=(
            jax.ShapeDtypeStruct(out_shape, BF16),
            jax.ShapeDtypeStruct((blocks, users), F32),
        ),
        in_specs=[sm] * 3 + [vm] * 5,
        out_specs=(pl.BlockSpec(memory_space=pl.ANY), vm),
        scratch_shapes=[
            pltpu.VMEM((blocks, 4, 8, users), F32),
            pltpu.VMEM((blocks * points, antennas, size), F32),
            pltpu.VMEM((8, antennas, size), F32),
            pltpu.VMEM((antennas, size), F32),
            pltpu.VMEM((blocks, size, users), F32),
            pltpu.VMEM((points, blocks, 2, antennas, users), BF16),
            pltpu.SemaphoreType.DMA((points,)),
        ],
        name="solve",
        compiler_params=pltpu.CompilerParams(vmem_limit_bytes=16 << 20),
    )(tile, penalty, power, r, *channels)


def across(value, axis, mask):
    size = lax.axis_size(axis)
    return lax.ppermute(value, axis, [(i, i ^ mask) for i in range(size)])


def local(channel, start_precoder, cluster, noise, penalty, power):
    blocks, parts, points, antennas, users = channel.shape
    chips = lax.axis_size(CHIPS)
    devices = lax.axis_size(EVERY)
    rows = parts * points * antennas
    core = lax.axis_index("core")
    tile = lax.axis_index("ut")
    chip = lax.axis_index(CHIPS)

    near_cluster = across(cluster, "ut", 1)
    near = across(channel, "ut", 1)
    v_far = across(start_precoder, "ut", 3)

    early, own, v_own = own_gains(cluster, channel, start_precoder, chips)
    early = lax.all_to_all(early, CHIPS, 0, 0, tiled=True)
    near = near * near_cluster[:, 0].astype(BF16)[None, None, :, None, None]

    far = across(own, "ut", 3)
    far_near = across(near, "ut", 3)

    where = jnp.stack([chip, core])
    flat = [x.reshape(blocks, rows, users) for x in (own, near, v_own, v_far)]
    keeps, cames = [], []
    for b in range(blocks):
        keep, send = partial_gains(b, core.reshape(1), *flat, chips)
        keeps.append(keep)
        cames.append(across(send, "core", 1))
    late = combined(keeps, cames)
    late = lax.all_to_all(late, CHIPS, 0, 0, tiled=True)

    mine, line, penalty, power = own_sum(where, early, noise, penalty, power)
    line = own_total(where, mine, across(mine, "core", 1), line)
    line = totals(late, line, devices)
    r = lax.all_to_all(line, EVERY, 0, 0, tiled=True).reshape(chips, devices // chips, 128)

    precoder, weight = solve(tile.reshape(1), penalty, power, r, (own, near, far, far_near), channel.shape)
    return precoder, weight


def solution(mesh):
    split = Mesh(mesh.devices.reshape(4, 4, 2, mesh.shape["ut"]), EVERY)
    placed = (
        P(None, None, AP, None, "ut"),
        P(None, None, AP, None, "ut"),
        P(AP, "ut"),
        P(None, "ut"),
        P(AP),
        P(AP),
    )

    return jax.shard_map(
        local,
        mesh=split,
        in_specs=placed,
        out_specs=(P(None, None, AP, None, "ut"), P(None, "ut")),
        check_vma=False,
    )
```

```python
import functools

import jax
import jax.numpy as jnp
from jax import lax
from jax.experimental import pallas as pl
from jax.experimental.pallas import tpu as pltpu
from jax.sharding import Mesh
from jax.sharding import PartitionSpec as P


AP = ("z", "x", "core")
CHIPS = ("z", "x")
EVERY = ("z", "x", "core", "ut")
SLOTS = (0, 1, 3, 2)
F32 = jnp.float32
BF16 = jnp.bfloat16
HIGHEST = lax.Precision.HIGHEST


def dot(a, b, dims, precision=None):
    return lax.dot_general(a, b, (dims, ((), ())), precision=precision, preferred_element_type=F32)


def two_parts(x):
    high = x.astype(BF16)
    return high, (x - high.astype(F32)).astype(BF16)


def iota(shape, dim):
    return lax.broadcasted_iota(jnp.int32, shape, dim)


def turned(v):
    half = v.shape[0] // 2
    return jnp.concatenate([v[half:], -v[:half]], axis=0)


def own_kernel(h_ref, v_ref, out_ref):
    blocks, _, users = h_ref.shape
    chips = out_ref.shape[0]
    piece = users // chips
    on_diag = iota((users, users), 0) == iota((users, users), 1)
    high, low = [], []
    for block in range(blocks):
        h = jnp.transpose(h_ref[block])
        v = v_ref[block]
        for part, w in enumerate((v, turned(v))):
            g = dot(h, w, ((1,), (0,)))
            own = jnp.sum(jnp.where(on_diag, g, 0.0), axis=0, keepdims=True)
            first, second = two_parts(own)
            high.append(first.astype(F32))
            low.append(second.astype(F32))
            g = jnp.where(on_diag, 0.0, g)
            at = (block * 2 + part) * piece
            out_ref[:, at : at + piece] = g.reshape(chips, piece, users).astype(BF16)
    extra = jnp.concatenate(high + low, axis=0).astype(BF16)
    out_ref[:, 4 * piece :] = jnp.broadcast_to(extra[None], (chips,) + extra.shape)


def own_gains(h, v, chips):
    _, _, users = h.shape
    vm = pl.BlockSpec(memory_space=pltpu.VMEM)
    return pl.pallas_call(
        own_kernel,
        out_shape=jax.ShapeDtypeStruct((chips, 4 * (users // chips) + 8, users), BF16),
        in_specs=[vm] * 2,
        out_specs=vm,
        name="own_gains",
        compiler_params=pltpu.CompilerParams(vmem_limit_bytes=8 << 20),
    )(h, v)


def gain_kernel(block, core_ref, ht_ref, ha_ref, vt_ref, vb_ref, keep_ref, send_ref):
    _, _, users = ht_ref.shape
    half = users // 2
    chips = keep_ref.shape[0]
    piece = users // chips
    first = core_ref[0] == 0
    vt, vb = vt_ref[block], vb_ref[block]
    ht, ha = jnp.transpose(ht_ref[block]), jnp.transpose(ha_ref[block])
    for out_ref, low in ((keep_ref, first), (send_ref, jnp.logical_not(first))):
        own = jnp.where(low, vt[:, :half], vt[:, half:])
        far = jnp.where(low, vb[:, :half], vb[:, half:])
        both = jnp.concatenate([own, far], axis=1)
        g = dot(ht, jnp.concatenate([far, turned(far)], axis=1), ((1,), (0,)))
        for part in range(2):
            out_ref[:, part, :, :half] = g[:, part * half : (part + 1) * half].reshape(chips, piece, half).astype(BF16)
        for part, w in enumerate((both, turned(both))):
            out_ref[:, part, :, half:] = dot(ha, w, ((1,), (0,))).reshape(chips, piece, users).astype(BF16)


def partial_gains(block, core, ht, ha, vt, vb, chips):
    _, rows, users = ht.shape
    shape = (chips, 2, users // chips, users + users // 2)
    vm = pl.BlockSpec(memory_space=pltpu.VMEM)
    return pl.pallas_call(
        functools.partial(gain_kernel, block),
        out_shape=(jax.ShapeDtypeStruct(shape, BF16), jax.ShapeDtypeStruct(shape, BF16)),
        in_specs=[pl.BlockSpec(memory_space=pltpu.SMEM)] + [vm] * 4,
        out_specs=(vm, vm),
        name="gains",
        compiler_params=pltpu.CompilerParams(vmem_limit_bytes=8 << 20),
        cost_estimate=pl.CostEstimate(flops=12 * users * users * rows, bytes_accessed=4 << 20, transcendentals=0),
    )(core, ht, ha, vt, vb)


def combine_kernel(keep0_ref, keep1_ref, came0_ref, came1_ref, out_ref):
    chips, _, piece, width = keep0_ref.shape
    rows = 2 * piece
    for block, (keep_ref, came_ref) in enumerate(((keep0_ref, came0_ref), (keep1_ref, came1_ref))):
        g = keep_ref[...] + came_ref[...]
        out_ref[:, block * rows : (block + 1) * rows] = g.reshape(chips, rows, width)


def combined(keeps, cames):
    chips, _, piece, width = keeps[0].shape
    vm = pl.BlockSpec(memory_space=pltpu.VMEM)
    return pl.pallas_call(
        combine_kernel,
        out_shape=jax.ShapeDtypeStruct((chips, 4 * piece, width), BF16),
        in_specs=[vm] * 4,
        out_specs=vm,
        name="combine",
        compiler_params=pltpu.CompilerParams(vmem_limit_bytes=8 << 20),
    )(*keeps, *cames)


def own_sum_kernel(where_ref, g_ref, noise_ref, penalty_ref, power_ref, sum_ref, line_ref, penalty_out, power_out):
    chip, core = where_ref[0], where_ref[1]
    chips, rows, users = g_ref.shape
    piece = (rows - 8) // 4
    lanes = line_ref.shape[1]

    def summed(at):
        total = g_ref[0, at].astype(F32)
        for source in range(1, chips):
            total = total + g_ref[source, at].astype(F32)
        return total

    sum_ref[...] = summed(slice(0, 4 * piece))
    extra = summed(slice(4 * piece, 4 * piece + 8))
    signal = extra + pltpu.roll(extra, 4, 0)
    noise = jnp.where(core == 0, noise_ref[...], 0.0)
    signal = jnp.concatenate([signal[:4], noise, noise], axis=0)
    pick = iota((users, lanes), 0) == chip * piece + iota((users, lanes), 1) % piece
    mine = dot(signal, pick.astype(F32), ((1,), (0,)), HIGHEST)
    group = iota((1, lanes), 1) // piece
    line = jnp.zeros((1, lanes), F32)
    for block in range(2):
        for part in range(2):
            at = block * 2 + part
            line = line + jnp.where(group == block * 4 + 2 + part, mine[at : at + 1], 0.0)
        line = line + jnp.where(group == block * 4, mine[4 + block : 5 + block], 0.0)
    line_ref[...] = line
    penalty_out[...] = penalty_ref[...]
    power_out[...] = power_ref[...]


def own_sum(where, g, noise, penalty, power):
    _, rows, users = g.shape
    points = penalty.shape[0]
    vm = pl.BlockSpec(memory_space=pltpu.VMEM)
    return pl.pallas_call(
        own_sum_kernel,
        out_shape=(
            jax.ShapeDtypeStruct((rows - 8, users), F32),
            jax.ShapeDtypeStruct((1, 128), F32),
            jax.ShapeDtypeStruct((1, points), F32),
            jax.ShapeDtypeStruct((1, points), F32),
        ),
        in_specs=[pl.BlockSpec(memory_space=pltpu.SMEM)] + [vm] * 4,
        out_specs=(vm,) * 4,
        name="own_sum",
        compiler_params=pltpu.CompilerParams(vmem_limit_bytes=8 << 20),
    )(where, g, noise, penalty.reshape(1, points), power.reshape(1, points))


def placed(line, total, start):
    lane = iota((total.shape[0], line.shape[1]), 1)
    row = iota((total.shape[0], line.shape[1]), 0)
    return line + jnp.sum(jnp.where(lane == row + start, total, 0.0), axis=0, keepdims=True)


def own_total_kernel(where_ref, mine_ref, came_ref, line_ref, out_ref):
    piece = mine_ref.shape[0] // 4
    line = line_ref[...]
    g = jnp.where(where_ref[1] == 0, mine_ref[...] + came_ref[...], 0.0)
    square = jnp.sum(g * g, axis=1, keepdims=True)
    for block in range(2):
        at = 2 * block * piece
        line = placed(line, square[at : at + piece] + square[at + piece : at + 2 * piece], 4 * block * piece)
    out_ref[...] = line


def own_total(where, mine, came, line):
    vm = pl.BlockSpec(memory_space=pltpu.VMEM)
    return pl.pallas_call(
        own_total_kernel,
        out_shape=jax.ShapeDtypeStruct(line.shape, F32),
        in_specs=[pl.BlockSpec(memory_space=pltpu.SMEM)] + [vm] * 3,
        out_specs=vm,
        name="own_total",
        compiler_params=pltpu.CompilerParams(vmem_limit_bytes=4 << 20),
    )(where, mine, came, line)


def total_kernel(g_ref, line_ref, out_ref):
    chips, rows, width = g_ref.shape
    piece = rows // 4
    half = width // 3
    line = line_ref[...]
    for block in range(2):
        square = None
        for part in range(2):
            at = slice((block * 2 + part) * piece, (block * 2 + part + 1) * piece)
            g = g_ref[0, at].astype(F32)
            for source in range(1, chips):
                g = g + g_ref[source, at].astype(F32)
            square = g * g if square is None else square + g * g
        own = jnp.sum(square[:, :half], axis=1, keepdims=True)
        near = jnp.sum(square[:, half : 2 * half] + square[:, 2 * half :], axis=1, keepdims=True)
        line = placed(placed(line, own, block * 4 * piece), near, (block * 4 + 1) * piece)
    out_ref[...] = jnp.broadcast_to(line, out_ref.shape)


def totals(g, line, devices):
    vm = pl.BlockSpec(memory_space=pltpu.VMEM)
    return pl.pallas_call(
        total_kernel,
        out_shape=jax.ShapeDtypeStruct((devices, 128), F32),
        in_specs=[vm] * 2,
        out_specs=vm,
        name="totals",
        compiler_params=pltpu.CompilerParams(vmem_limit_bytes=8 << 20),
    )(g, line)


def user_lines(r_ref, line_ref, weight_ref, tile):
    chips, _, lanes = r_ref.shape
    groups = 8
    piece = lanes // groups
    halves = chips // groups
    group = iota((8, lanes), 1) // piece
    sublane = iota((8, lanes), 0)
    rolled = [r_ref[0]] + [pltpu.roll(r_ref[p], p * piece % lanes, 1) if p % groups else r_ref[p] for p in range(1, chips)]

    def gathered(g, half):
        total = None
        for p in range(half * groups, (half + 1) * groups):
            term = jnp.where(group == (p + g) % groups, rolled[p], 0.0)
            total = term if total is None else total + term
        if g:
            total = pltpu.roll(total, lanes - g * piece, 1)
        return total + pltpu.roll(total, 4, 0)

    def line(g):
        return jnp.concatenate([gathered(g, half) for half in range(halves)], axis=1)

    for block in range(2):
        base = block * 4
        from_mate = line(base + 1)
        even = iota(from_mate.shape, 0) % 2 == 0
        swapped = jnp.where(even, pltpu.roll(from_mate, 7, 0), pltpu.roll(from_mate, 1, 0))
        rest = line(base) + swapped
        signal_re = line(base + 2)
        signal_im = line(base + 3)
        strength = signal_re * signal_re + signal_im * signal_im
        level = rest + strength
        line_ref[block, 0] = strength / (rest * level)
        line_ref[block, 1] = signal_re / rest
        line_ref[block, 2] = signal_im / rest
        line_ref[block, 3] = level / rest
        weight_ref[block : block + 1, :] = line_ref[block, 3, pl.ds(tile, 1)]


def picked(pieces, g):
    lanes = pieces[0].shape[1]
    group = iota(pieces[0].shape, 1) // (lanes // 8)
    total = pieces[0]
    for s in range(1, 8):
        total = jnp.where(group == (s + g) % 8, pieces[s], total)
    return total


def eliminate(work_ref, sys_ref, scale_ref):
    _, rows, lanes = work_ref.shape
    width = lanes // 8
    lane = iota((8, lanes), 1)
    sublane = iota((8, lanes), 0)
    for high in range(rows // 8):
        at = slice(high * 8, high * 8 + 8)
        pieces = [sys_ref[s, at, :] for s in range(8)]
        for g in range(8):
            group = picked(pieces, g)
            work_ref[g, at, :] = pltpu.roll(group, lanes - g * width, 1) if g else group

    def spread(value, k):
        return jnp.take_along_axis(value, lane // width * width + k % width, axis=1, mode="promise_in_bounds")

    def row_of(g, k):
        return jnp.broadcast_to(work_ref[g, k : k + 1, :], (8, lanes))

    def pivot(k):
        column = k // width
        line = [row_of(g, k) for g in range(8)]
        value = spread(line[column], k)
        root = lax.rsqrt(value)
        scale_ref[k : k + 1, :] = root[:1]
        line[column] = line[column] + jnp.where(lane % width == k % width, 1.0, 0.0)
        return line, 1.0 / value

    def update(k, high, line, inverse):
        column = k // width
        at = slice(high * 8, high * 8 + 8)
        f_re = spread(work_ref[column, at, :], k) * inverse
        f_im = spread(work_ref[4 + column, at, :], k) * inverse
        if high == k // 8:
            below = sublane > k % 8
            f_re = jnp.where(below, f_re, 0.0)
            f_im = jnp.where(below, f_im, 0.0)
        for c in range(4):
            real, imag = line[c], line[4 + c]
            work_ref[c, at, :] = work_ref[c, at, :] - (f_re * real - f_im * imag)
            work_ref[4 + c, at, :] = work_ref[4 + c, at, :] - (f_re * imag + f_im * real)

    now = pivot(0)
    for k in range(rows - 1):
        first = (k + 1) // 8
        update(k, first, *now)
        later = pivot(k + 1)
        for high in range(first + 1, rows // 8):
            update(k, high, *now)
        now = later

    for high in range(rows // 8):
        at = slice(high * 8, high * 8 + 8)
        scale = scale_ref[at, :]
        pieces = []
        for g in range(8):
            start = g % 4 * width
            here = start + lane % width
            row = high * 8 + sublane
            kept = jnp.where(here < row, work_ref[g, at, :], 0.0)
            if g < 4:
                kept = jnp.where(here == row, 1.0, kept)
            kept = kept * scale
            pieces.append(pltpu.roll(kept, g * width, 1) if g else kept)
        for s in range(8):
            sys_ref[s, at, :] = picked(pieces, s)


def solve_kernel(tile_ref, penalty_ref, power_ref, r_ref, *refs):
    h_refs = refs[:4]
    out_ref, weight_ref, line_ref, sys_ref, work_ref, scale_ref, y_ref, made_ref, inverse_ref, sems = refs[4:]
    blocks, _, points, antennas, users = h_refs[0].shape
    size = 2 * antennas
    systems = blocks * points
    tile = tile_ref[0]

    user_lines(r_ref, line_ref, weight_ref, tile)

    def line(block, which, slot):
        return line_ref[block, which, pl.ds(tile ^ SLOTS[slot], 1), :]

    def channel(block, slot, point):
        h_ref = h_refs[slot]
        return jnp.concatenate([h_ref[block, 0, point], h_ref[block, 1, point]], axis=0)

    width = size // systems
    lane = iota((antennas, size), 1)
    row = iota((antennas, size), 0)

    def turn(x, n):
        cut = size - n * width
        return jnp.concatenate([x[cut:], x[:cut]], axis=0) if n else x

    def column(n):
        return (lane + (size - n * width)) % size

    for block in range(blocks):
        for point in range(points):
            n = block * points + point
            xs, highs, lows = [], [], []
            for slot in range(4):
                x = channel(block, slot, point)
                high, low = two_parts(turn(x, n).astype(F32) * line(block, 0, slot))
                xs.append(x)
                highs.append(high)
                lows.append(low)
            parts = jnp.concatenate([jnp.concatenate(highs, axis=1), jnp.concatenate(lows, axis=1)], axis=0)
            acc = dot(jnp.concatenate(xs, axis=1), parts, ((1,), (1,)))
            p = acc[:, :size] + acc[:, size:]
            a = jnp.where(column(n) < antennas, p[:antennas], -p[:antennas]) + pltpu.roll(p[antennas:], antennas, 1)
            a = a + jnp.where(column(n) == row, penalty_ref[0, point], 0.0)
            sys_ref[n] = a

    eliminate(work_ref, sys_ref, scale_ref)

    for n in range(systems):
        high, low = two_parts(sys_ref[n])
        left = jnp.concatenate([high, high, low, low], axis=0)
        right = jnp.concatenate([high, low, high, low], axis=0)
        q = turn(dot(left, right, ((0,), (0,))), (systems - n) % systems)
        top = jnp.where(column(n) < antennas, q[:antennas], -q[:antennas]) + pltpu.roll(q[antennas:], antennas, 1)
        bottom = pltpu.roll(top, antennas, 1)
        bottom = jnp.where(column(n) < antennas, -bottom, bottom)
        for at, half in enumerate((top, bottom)):
            high, low = two_parts(half)
            inverse_ref[n, at * antennas : (at + 1) * antennas, :size] = high
            inverse_ref[n, at * antennas : (at + 1) * antennas, size:] = low

    copies = []
    for point in range(points):
        total = jnp.zeros((1, users), F32)
        for block in range(blocks):
            n = block * points + point
            parts = inverse_ref[n]
            for slot in range(4):
                x = turn(channel(block, slot, point), n)
                y = dot(parts, jnp.concatenate([x, x], axis=0), ((1,), (0,)))
                w_re, w_im = line(block, 1, slot), line(block, 2, slot)
                total = total + jnp.sum(y * y, axis=0, keepdims=True) * (w_re * w_re + w_im * w_im)
                if slot == 0:
                    y_ref[block] = y
        mean = jnp.sum(total, axis=1, keepdims=True) / (2.0 * blocks * antennas * 4 * users)
        gain = jnp.sqrt(power_ref[0, point] / (mean + 1e-06))
        for block in range(blocks):
            y_re, y_im = y_ref[block, :antennas], y_ref[block, antennas:]
            w_re = line(block, 1, 0) * gain
            w_im = line(block, 2, 0) * gain
            made_ref[point, block, 0] = (y_re * w_re - y_im * w_im).astype(out_ref.dtype)
            made_ref[point, block, 1] = (y_re * w_im + y_im * w_re).astype(out_ref.dtype)
        copy = pltpu.make_async_copy(made_ref.at[point], out_ref.at[:, :, point], sems.at[point])
        copy.start()
        copies.append(copy)
    for copy in copies:
        copy.wait()


def solve(tile, penalty, power, r, channels, out_shape):
    blocks, _, points, antennas, users = out_shape
    size = 2 * antennas
    vm = pl.BlockSpec(memory_space=pltpu.VMEM)
    sm = pl.BlockSpec(memory_space=pltpu.SMEM)
    return pl.pallas_call(
        solve_kernel,
        out_shape=(
            jax.ShapeDtypeStruct(out_shape, BF16),
            jax.ShapeDtypeStruct((blocks, users), F32),
        ),
        in_specs=[sm] * 3 + [vm] * 5,
        out_specs=(pl.BlockSpec(memory_space=pl.ANY), vm),
        scratch_shapes=[
            pltpu.VMEM((blocks, 4, 8, users), F32),
            pltpu.VMEM((blocks * points, antennas, size), F32),
            pltpu.VMEM((8, antennas, size), F32),
            pltpu.VMEM((antennas, size), F32),
            pltpu.VMEM((blocks, size, users), F32),
            pltpu.VMEM((points, blocks, 2, antennas, users), BF16),
            pltpu.VMEM((blocks * points, size, 2 * size), BF16),
            pltpu.SemaphoreType.DMA((points,)),
        ],
        name="solve",
        compiler_params=pltpu.CompilerParams(vmem_limit_bytes=16 << 20),
    )(tile, penalty, power, r, *channels)


def across(value, axis, mask):
    size = lax.axis_size(axis)
    return lax.ppermute(value, axis, [(i, i ^ mask) for i in range(size)])


def local(channel, start_precoder, cluster, noise, penalty, power):
    blocks, parts, points, antennas, users = channel.shape
    chips = lax.axis_size(CHIPS)
    devices = lax.axis_size(EVERY)
    rows = parts * points * antennas
    core = lax.axis_index("core")
    tile = lax.axis_index("ut")
    chip = lax.axis_index(CHIPS)

    near_cluster = across(cluster, "ut", 1)
    near = across(channel, "ut", 1)
    v_far = across(start_precoder, "ut", 3)

    own = channel * cluster[:, 0].astype(BF16)[None, None, :, None, None]
    early = own_gains(own.reshape(blocks, rows, users), start_precoder.reshape(blocks, rows, users), chips)
    early = lax.all_to_all(early, CHIPS, 0, 0, tiled=True)
    near = near * near_cluster[:, 0].astype(BF16)[None, None, :, None, None]

    far = across(own, "ut", 3)
    far_near = across(near, "ut", 3)

    where = jnp.stack([chip, core])
    flat = [x.reshape(blocks, rows, users) for x in (own, near, start_precoder, v_far)]
    keeps, cames = [], []
    for b in range(blocks):
        keep, send = partial_gains(b, core.reshape(1), *flat, chips)
        keeps.append(keep)
        cames.append(across(send, "core", 1))
    late = combined(keeps, cames)
    late = lax.all_to_all(late, CHIPS, 0, 0, tiled=True)

    mine, line, penalty, power = own_sum(where, early, noise, penalty, power)
    line = own_total(where, mine, across(mine, "core", 1), line)
    line = totals(late, line, devices)
    r = lax.all_to_all(line, EVERY, 0, 0, tiled=True).reshape(chips, devices // chips, 128)

    precoder, weight = solve(tile.reshape(1), penalty, power, r, (own, near, far, far_near), channel.shape)
    return precoder, weight


def solution(mesh):
    split = Mesh(mesh.devices.reshape(4, 4, 2, mesh.shape["ut"]), EVERY)
    placed = (
        P(None, None, AP, None, "ut"),
        P(None, None, AP, None, "ut"),
        P(AP, "ut"),
        P(None, "ut"),
        P(AP),
        P(AP),
    )

    return jax.shard_map(
        local,
        mesh=split,
        in_specs=placed,
        out_specs=(P(None, None, AP, None, "ut"), P(None, "ut")),
        check_vma=False,
    )
```

```python
import functools

import jax
import jax.numpy as jnp
from jax import lax
from jax.experimental import pallas as pl
from jax.experimental.pallas import tpu as pltpu
from jax.sharding import Mesh
from jax.sharding import PartitionSpec as P


AP = ("z", "x", "core")
CHIPS = ("z", "x")
EVERY = ("z", "x", "core", "ut")
SLOTS = (0, 1, 3, 2)
F32 = jnp.float32
BF16 = jnp.bfloat16
HIGHEST = lax.Precision.HIGHEST


def dot(a, b, dims, precision=None):
    return lax.dot_general(a, b, (dims, ((), ())), precision=precision, preferred_element_type=F32)


def two_parts(x):
    high = x.astype(BF16)
    return high, (x - high.astype(F32)).astype(BF16)


def iota(shape, dim):
    return lax.broadcasted_iota(jnp.int32, shape, dim)


def turned(v):
    half = v.shape[0] // 2
    return jnp.concatenate([v[half:], -v[:half]], axis=0)


def own_kernel(h_ref, v_ref, out_ref):
    blocks, _, users = h_ref.shape
    chips = out_ref.shape[0]
    piece = users // chips
    on_diag = iota((users, users), 0) == iota((users, users), 1)
    high, low = [], []
    for block in range(blocks):
        h = jnp.transpose(h_ref[block])
        v = v_ref[block]
        for part, w in enumerate((v, turned(v))):
            g = dot(h, w, ((1,), (0,)))
            own = jnp.sum(jnp.where(on_diag, g, 0.0), axis=0, keepdims=True)
            first, second = two_parts(own)
            high.append(first.astype(F32))
            low.append(second.astype(F32))
            g = jnp.where(on_diag, 0.0, g)
            at = (block * 2 + part) * piece
            out_ref[:, at : at + piece] = g.reshape(chips, piece, users).astype(BF16)
    extra = jnp.concatenate(high + low, axis=0).astype(BF16)
    out_ref[:, 4 * piece :] = jnp.broadcast_to(extra[None], (chips,) + extra.shape)


def own_gains(h, v, chips):
    _, _, users = h.shape
    vm = pl.BlockSpec(memory_space=pltpu.VMEM)
    return pl.pallas_call(
        own_kernel,
        out_shape=jax.ShapeDtypeStruct((chips, 4 * (users // chips) + 8, users), BF16),
        in_specs=[vm] * 2,
        out_specs=vm,
        name="own_gains",
        compiler_params=pltpu.CompilerParams(vmem_limit_bytes=8 << 20),
    )(h, v)


def gain_kernel(block, core_ref, cluster_ref, ht_ref, ha_ref, vt_ref, vb_ref, keep_ref, send_ref):
    _, _, users = ht_ref.shape
    half = users // 2
    chips = keep_ref.shape[0]
    piece = users // chips
    first = core_ref[0] == 0
    vt, vb = vt_ref[block], vb_ref[block]
    _, parts, points, _, _ = ha_ref.shape
    ha = []
    for part in range(parts):
        for point in range(points):
            near = ha_ref[block, part, point]
            ha.append(jnp.where(cluster_ref[point] != 0, near, jnp.zeros_like(near)))
    ht, ha = jnp.transpose(ht_ref[block]), jnp.transpose(jnp.concatenate(ha, axis=0))
    for out_ref, low in ((keep_ref, first), (send_ref, jnp.logical_not(first))):
        own = jnp.where(low, vt[:, :half], vt[:, half:])
        far = jnp.where(low, vb[:, :half], vb[:, half:])
        both = jnp.concatenate([own, far], axis=1)
        g = dot(ht, jnp.concatenate([far, turned(far)], axis=1), ((1,), (0,)))
        for part in range(2):
            out_ref[:, part, :, :half] = g[:, part * half : (part + 1) * half].reshape(chips, piece, half).astype(BF16)
        for part, w in enumerate((both, turned(both))):
            out_ref[:, part, :, half:] = dot(ha, w, ((1,), (0,))).reshape(chips, piece, users).astype(BF16)


def partial_gains(block, core, near_cluster, ht, ha, vt, vb, chips):
    _, rows, users = ht.shape
    shape = (chips, 2, users // chips, users + users // 2)
    vm = pl.BlockSpec(memory_space=pltpu.VMEM)
    return pl.pallas_call(
        functools.partial(gain_kernel, block),
        out_shape=(jax.ShapeDtypeStruct(shape, BF16), jax.ShapeDtypeStruct(shape, BF16)),
        in_specs=[pl.BlockSpec(memory_space=pltpu.SMEM)] * 2 + [vm] * 4,
        out_specs=(vm, vm),
        name="gains",
        compiler_params=pltpu.CompilerParams(vmem_limit_bytes=8 << 20),
        cost_estimate=pl.CostEstimate(flops=12 * users * users * rows, bytes_accessed=4 << 20, transcendentals=0),
    )(core, near_cluster, ht, ha, vt, vb)


def combine_kernel(keep0_ref, keep1_ref, came0_ref, came1_ref, out_ref):
    chips, _, piece, width = keep0_ref.shape
    rows = 2 * piece
    for block, (keep_ref, came_ref) in enumerate(((keep0_ref, came0_ref), (keep1_ref, came1_ref))):
        g = keep_ref[...] + came_ref[...]
        out_ref[:, block * rows : (block + 1) * rows] = g.reshape(chips, rows, width)


def combined(keeps, cames):
    chips, _, piece, width = keeps[0].shape
    vm = pl.BlockSpec(memory_space=pltpu.VMEM)
    return pl.pallas_call(
        combine_kernel,
        out_shape=jax.ShapeDtypeStruct((chips, 4 * piece, width), BF16),
        in_specs=[vm] * 4,
        out_specs=vm,
        name="combine",
        compiler_params=pltpu.CompilerParams(vmem_limit_bytes=8 << 20),
    )(*keeps, *cames)


def own_sum_kernel(where_ref, g_ref, noise_ref, penalty_ref, power_ref, sum_ref, line_ref, penalty_out, power_out):
    chip, core = where_ref[0], where_ref[1]
    chips, rows, users = g_ref.shape
    piece = (rows - 8) // 4
    lanes = line_ref.shape[1]

    def summed(at):
        total = g_ref[0, at].astype(F32)
        for source in range(1, chips):
            total = total + g_ref[source, at].astype(F32)
        return total

    sum_ref[...] = summed(slice(0, 4 * piece))
    extra = summed(slice(4 * piece, 4 * piece + 8))
    signal = extra + pltpu.roll(extra, 4, 0)
    noise = jnp.where(core == 0, noise_ref[...], 0.0)
    signal = jnp.concatenate([signal[:4], noise, noise], axis=0)
    pick = iota((users, lanes), 0) == chip * piece + iota((users, lanes), 1) % piece
    mine = dot(signal, pick.astype(F32), ((1,), (0,)), HIGHEST)
    group = iota((1, lanes), 1) // piece
    line = jnp.zeros((1, lanes), F32)
    for block in range(2):
        for part in range(2):
            at = block * 2 + part
            line = line + jnp.where(group == block * 4 + 2 + part, mine[at : at + 1], 0.0)
        line = line + jnp.where(group == block * 4, mine[4 + block : 5 + block], 0.0)
    line_ref[...] = line
    penalty_out[...] = penalty_ref[...]
    power_out[...] = power_ref[...]


def own_sum(where, g, noise, penalty, power):
    _, rows, users = g.shape
    points = penalty.shape[0]
    vm = pl.BlockSpec(memory_space=pltpu.VMEM)
    return pl.pallas_call(
        own_sum_kernel,
        out_shape=(
            jax.ShapeDtypeStruct((rows - 8, users), F32),
            jax.ShapeDtypeStruct((1, 128), F32),
            jax.ShapeDtypeStruct((1, points), F32),
            jax.ShapeDtypeStruct((1, points), F32),
        ),
        in_specs=[pl.BlockSpec(memory_space=pltpu.SMEM)] + [vm] * 4,
        out_specs=(vm,) * 4,
        name="own_sum",
        compiler_params=pltpu.CompilerParams(vmem_limit_bytes=8 << 20),
    )(where, g, noise, penalty.reshape(1, points), power.reshape(1, points))


def placed(line, total, start):
    lane = iota((total.shape[0], line.shape[1]), 1)
    row = iota((total.shape[0], line.shape[1]), 0)
    return line + jnp.sum(jnp.where(lane == row + start, total, 0.0), axis=0, keepdims=True)


def own_total_kernel(where_ref, mine_ref, came_ref, line_ref, out_ref):
    piece = mine_ref.shape[0] // 4
    line = line_ref[...]
    g = jnp.where(where_ref[1] == 0, mine_ref[...] + came_ref[...], 0.0)
    square = jnp.sum(g * g, axis=1, keepdims=True)
    for block in range(2):
        at = 2 * block * piece
        line = placed(line, square[at : at + piece] + square[at + piece : at + 2 * piece], 4 * block * piece)
    out_ref[...] = line


def own_total(where, mine, came, line):
    vm = pl.BlockSpec(memory_space=pltpu.VMEM)
    return pl.pallas_call(
        own_total_kernel,
        out_shape=jax.ShapeDtypeStruct(line.shape, F32),
        in_specs=[pl.BlockSpec(memory_space=pltpu.SMEM)] + [vm] * 3,
        out_specs=vm,
        name="own_total",
        compiler_params=pltpu.CompilerParams(vmem_limit_bytes=4 << 20),
    )(where, mine, came, line)


def total_kernel(g_ref, line_ref, out_ref):
    chips, rows, width = g_ref.shape
    piece = rows // 4
    half = width // 3
    line = line_ref[...]
    for block in range(2):
        square = None
        for part in range(2):
            at = slice((block * 2 + part) * piece, (block * 2 + part + 1) * piece)
            g = g_ref[0, at].astype(F32)
            for source in range(1, chips):
                g = g + g_ref[source, at].astype(F32)
            square = g * g if square is None else square + g * g
        own = jnp.sum(square[:, :half], axis=1, keepdims=True)
        near = jnp.sum(square[:, half : 2 * half] + square[:, 2 * half :], axis=1, keepdims=True)
        line = placed(placed(line, own, block * 4 * piece), near, (block * 4 + 1) * piece)
    out_ref[...] = jnp.broadcast_to(line, out_ref.shape)


def totals(g, line, devices):
    vm = pl.BlockSpec(memory_space=pltpu.VMEM)
    return pl.pallas_call(
        total_kernel,
        out_shape=jax.ShapeDtypeStruct((devices, 128), F32),
        in_specs=[vm] * 2,
        out_specs=vm,
        name="totals",
        compiler_params=pltpu.CompilerParams(vmem_limit_bytes=8 << 20),
    )(g, line)


def user_lines(r_ref, line_ref, weight_ref, tile):
    chips, _, lanes = r_ref.shape
    groups = 8
    piece = lanes // groups
    halves = chips // groups
    group = iota((8, lanes), 1) // piece
    sublane = iota((8, lanes), 0)
    rolled = [r_ref[0]] + [pltpu.roll(r_ref[p], p * piece % lanes, 1) if p % groups else r_ref[p] for p in range(1, chips)]

    def gathered(g, half):
        total = None
        for p in range(half * groups, (half + 1) * groups):
            term = jnp.where(group == (p + g) % groups, rolled[p], 0.0)
            total = term if total is None else total + term
        if g:
            total = pltpu.roll(total, lanes - g * piece, 1)
        return total + pltpu.roll(total, 4, 0)

    def line(g):
        return jnp.concatenate([gathered(g, half) for half in range(halves)], axis=1)

    for block in range(2):
        base = block * 4
        from_mate = line(base + 1)
        even = iota(from_mate.shape, 0) % 2 == 0
        swapped = jnp.where(even, pltpu.roll(from_mate, 7, 0), pltpu.roll(from_mate, 1, 0))
        rest = line(base) + swapped
        signal_re = line(base + 2)
        signal_im = line(base + 3)
        strength = signal_re * signal_re + signal_im * signal_im
        level = rest + strength
        line_ref[block, 0] = strength / (rest * level)
        line_ref[block, 1] = signal_re / rest
        line_ref[block, 2] = signal_im / rest
        line_ref[block, 3] = level / rest
        weight_ref[block : block + 1, :] = line_ref[block, 3, pl.ds(tile, 1)]


def picked(pieces, g):
    lanes = pieces[0].shape[1]
    group = iota(pieces[0].shape, 1) // (lanes // 8)
    total = pieces[0]
    for s in range(1, 8):
        total = jnp.where(group == (s + g) % 8, pieces[s], total)
    return total


def eliminate(work_ref, sys_ref, scale_ref):
    _, rows, lanes = work_ref.shape
    width = lanes // 8
    lane = iota((8, lanes), 1)
    sublane = iota((8, lanes), 0)
    for high in range(rows // 8):
        at = slice(high * 8, high * 8 + 8)
        pieces = [sys_ref[s, at, :] for s in range(8)]
        for g in range(8):
            group = picked(pieces, g)
            work_ref[g, at, :] = pltpu.roll(group, lanes - g * width, 1) if g else group

    def spread(value, k):
        return jnp.take_along_axis(value, lane // width * width + k % width, axis=1, mode="promise_in_bounds")

    def row_of(g, k):
        return jnp.broadcast_to(work_ref[g, k : k + 1, :], (8, lanes))

    def pivot(k):
        column = k // width
        line = [row_of(g, k) for g in range(8)]
        value = spread(line[column], k)
        root = lax.rsqrt(value)
        scale_ref[k : k + 1, :] = root[:1]
        line[column] = line[column] + jnp.where(lane % width == k % width, 1.0, 0.0)
        return line, 1.0 / value

    def update(k, high, line, inverse):
        column = k // width
        at = slice(high * 8, high * 8 + 8)
        f_re = spread(work_ref[column, at, :], k) * inverse
        f_im = spread(work_ref[4 + column, at, :], k) * inverse
        if high == k // 8:
            below = sublane > k % 8
            f_re = jnp.where(below, f_re, 0.0)
            f_im = jnp.where(below, f_im, 0.0)
        for c in range(4):
            real, imag = line[c], line[4 + c]
            work_ref[c, at, :] = work_ref[c, at, :] - (f_re * real - f_im * imag)
            work_ref[4 + c, at, :] = work_ref[4 + c, at, :] - (f_re * imag + f_im * real)

    now = pivot(0)
    for k in range(rows - 1):
        first = (k + 1) // 8
        update(k, first, *now)
        later = pivot(k + 1)
        for high in range(first + 1, rows // 8):
            update(k, high, *now)
        now = later

    for high in range(rows // 8):
        at = slice(high * 8, high * 8 + 8)
        scale = scale_ref[at, :]
        pieces = []
        for g in range(8):
            start = g % 4 * width
            here = start + lane % width
            row = high * 8 + sublane
            kept = jnp.where(here < row, work_ref[g, at, :], 0.0)
            if g < 4:
                kept = jnp.where(here == row, 1.0, kept)
            kept = kept * scale
            pieces.append(pltpu.roll(kept, g * width, 1) if g else kept)
        for s in range(8):
            sys_ref[s, at, :] = picked(pieces, s)


def solve_kernel(tile_ref, penalty_ref, power_ref, r_ref, *refs):
    h_refs = refs[:4]
    out_ref, weight_ref, line_ref, sys_ref, work_ref, scale_ref, y_ref, made_ref, inverse_ref, sems = refs[4:]
    blocks, _, points, antennas, users = h_refs[0].shape
    size = 2 * antennas
    systems = blocks * points
    tile = tile_ref[0]

    user_lines(r_ref, line_ref, weight_ref, tile)

    def line(block, which, slot):
        return line_ref[block, which, pl.ds(tile ^ SLOTS[slot], 1), :]

    def channel(block, slot, point):
        h_ref = h_refs[slot]
        return jnp.concatenate([h_ref[block, 0, point], h_ref[block, 1, point]], axis=0)

    width = size // systems
    lane = iota((antennas, size), 1)
    row = iota((antennas, size), 0)

    def turn(x, n):
        cut = size - n * width
        return jnp.concatenate([x[cut:], x[:cut]], axis=0) if n else x

    def column(n):
        return (lane + (size - n * width)) % size

    for block in range(blocks):
        for point in range(points):
            n = block * points + point
            xs, highs, lows = [], [], []
            for slot in range(4):
                x = channel(block, slot, point)
                high, low = two_parts(turn(x, n).astype(F32) * line(block, 0, slot))
                xs.append(x)
                highs.append(high)
                lows.append(low)
            parts = jnp.concatenate([jnp.concatenate(highs, axis=1), jnp.concatenate(lows, axis=1)], axis=0)
            acc = dot(jnp.concatenate(xs, axis=1), parts, ((1,), (1,)))
            p = acc[:, :size] + acc[:, size:]
            a = jnp.where(column(n) < antennas, p[:antennas], -p[:antennas]) + pltpu.roll(p[antennas:], antennas, 1)
            a = a + jnp.where(column(n) == row, penalty_ref[0, point], 0.0)
            sys_ref[n] = a

    eliminate(work_ref, sys_ref, scale_ref)

    for n in range(systems):
        high, low = two_parts(sys_ref[n])
        left = jnp.concatenate([high, high, low, low], axis=0)
        right = jnp.concatenate([high, low, high, low], axis=0)
        q = turn(dot(left, right, ((0,), (0,))), (systems - n) % systems)
        top = jnp.where(column(n) < antennas, q[:antennas], -q[:antennas]) + pltpu.roll(q[antennas:], antennas, 1)
        bottom = pltpu.roll(top, antennas, 1)
        bottom = jnp.where(column(n) < antennas, -bottom, bottom)
        for at, half in enumerate((top, bottom)):
            high, low = two_parts(half)
            inverse_ref[n, at * antennas : (at + 1) * antennas, :size] = high
            inverse_ref[n, at * antennas : (at + 1) * antennas, size:] = low

    copies = []
    for point in range(points):
        total = jnp.zeros((1, users), F32)
        for block in range(blocks):
            n = block * points + point
            parts = inverse_ref[n]
            for slot in range(4):
                x = turn(channel(block, slot, point), n)
                y = dot(parts, jnp.concatenate([x, x], axis=0), ((1,), (0,)))
                w_re, w_im = line(block, 1, slot), line(block, 2, slot)
                total = total + jnp.sum(y * y, axis=0, keepdims=True) * (w_re * w_re + w_im * w_im)
                if slot == 0:
                    y_ref[block] = y
        mean = jnp.sum(total, axis=1, keepdims=True) / (2.0 * blocks * antennas * 4 * users)
        gain = jnp.sqrt(power_ref[0, point] / (mean + 1e-06))
        for block in range(blocks):
            y_re, y_im = y_ref[block, :antennas], y_ref[block, antennas:]
            w_re = line(block, 1, 0) * gain
            w_im = line(block, 2, 0) * gain
            made_ref[point, block, 0] = (y_re * w_re - y_im * w_im).astype(out_ref.dtype)
            made_ref[point, block, 1] = (y_re * w_im + y_im * w_re).astype(out_ref.dtype)
        copy = pltpu.make_async_copy(made_ref.at[point], out_ref.at[:, :, point], sems.at[point])
        copy.start()
        copies.append(copy)
    for copy in copies:
        copy.wait()


def solve(tile, penalty, power, r, channels, out_shape):
    blocks, _, points, antennas, users = out_shape
    size = 2 * antennas
    vm = pl.BlockSpec(memory_space=pltpu.VMEM)
    sm = pl.BlockSpec(memory_space=pltpu.SMEM)
    return pl.pallas_call(
        solve_kernel,
        out_shape=(
            jax.ShapeDtypeStruct(out_shape, BF16),
            jax.ShapeDtypeStruct((blocks, users), F32),
        ),
        in_specs=[sm] * 3 + [vm] * 5,
        out_specs=(pl.BlockSpec(memory_space=pl.ANY), vm),
        scratch_shapes=[
            pltpu.VMEM((blocks, 4, 8, users), F32),
            pltpu.VMEM((blocks * points, antennas, size), F32),
            pltpu.VMEM((8, antennas, size), F32),
            pltpu.VMEM((antennas, size), F32),
            pltpu.VMEM((blocks, size, users), F32),
            pltpu.VMEM((points, blocks, 2, antennas, users), BF16),
            pltpu.VMEM((blocks * points, size, 2 * size), BF16),
            pltpu.SemaphoreType.DMA((points,)),
        ],
        name="solve",
        compiler_params=pltpu.CompilerParams(vmem_limit_bytes=16 << 20),
    )(tile, penalty, power, r, *channels)


def across(value, axis, mask):
    size = lax.axis_size(axis)
    return lax.ppermute(value, axis, [(i, i ^ mask) for i in range(size)])


def local(channel, start_precoder, cluster, noise, penalty, power):
    blocks, parts, points, antennas, users = channel.shape
    chips = lax.axis_size(CHIPS)
    devices = lax.axis_size(EVERY)
    rows = parts * points * antennas
    core = lax.axis_index("core")
    tile = lax.axis_index("ut")
    chip = lax.axis_index(CHIPS)

    near_cluster = across(cluster[:, 0], "ut", 1)
    near = across(channel, "ut", 1)
    v_far = across(start_precoder, "ut", 3)

    own = channel * cluster[:, 0].astype(BF16)[None, None, :, None, None]
    early = own_gains(own.reshape(blocks, rows, users), start_precoder.reshape(blocks, rows, users), chips)
    early = lax.all_to_all(early, CHIPS, 0, 0, tiled=True)

    far = across(own, "ut", 3)

    where = jnp.stack([chip, core])
    ht, vt, vb = (x.reshape(blocks, rows, users) for x in (own, start_precoder, v_far))
    keeps, cames = [], []
    for b in range(blocks):
        keep, send = partial_gains(b, core.reshape(1), near_cluster, ht, near, vt, vb, chips)
        keeps.append(keep)
        cames.append(across(send, "core", 1))
    near = near * near_cluster.astype(BF16)[None, None, :, None, None]
    far_near = across(near, "ut", 3)
    late = combined(keeps, cames)
    late = lax.all_to_all(late, CHIPS, 0, 0, tiled=True)

    mine, line, penalty, power = own_sum(where, early, noise, penalty, power)
    line = own_total(where, mine, across(mine, "core", 1), line)
    line = totals(late, line, devices)
    r = lax.all_to_all(line, EVERY, 0, 0, tiled=True).reshape(chips, devices // chips, 128)

    precoder, weight = solve(tile.reshape(1), penalty, power, r, (own, near, far, far_near), channel.shape)
    return precoder, weight


def solution(mesh):
    split = Mesh(mesh.devices.reshape(4, 4, 2, mesh.shape["ut"]), EVERY)
    placed = (
        P(None, None, AP, None, "ut"),
        P(None, None, AP, None, "ut"),
        P(AP, "ut"),
        P(None, "ut"),
        P(AP),
        P(AP),
    )

    return jax.shard_map(
        local,
        mesh=split,
        in_specs=placed,
        out_specs=(P(None, None, AP, None, "ut"), P(None, "ut")),
        check_vma=False,
    )
```

```python
import functools

import jax
import jax.numpy as jnp
from jax import lax
from jax.experimental import pallas as pl
from jax.experimental.pallas import tpu as pltpu
from jax.sharding import Mesh
from jax.sharding import PartitionSpec as P


AP = ("z", "x", "core")
CHIPS = ("z", "x")
EVERY = ("z", "x", "core", "ut")
SLOTS = (0, 1, 3, 2)
F32 = jnp.float32
BF16 = jnp.bfloat16
HIGHEST = lax.Precision.HIGHEST


def dot(a, b, dims, precision=None):
    return lax.dot_general(a, b, (dims, ((), ())), precision=precision, preferred_element_type=F32)


def two_parts(x):
    high = x.astype(BF16)
    return high, (x - high.astype(F32)).astype(BF16)


def iota(shape, dim):
    return lax.broadcasted_iota(jnp.int32, shape, dim)


def turned(v):
    half = v.shape[0] // 2
    return jnp.concatenate([v[half:], -v[:half]], axis=0)


def sent(source, target, sems, at, rows):
    copy = pltpu.make_async_copy(source.at[:, rows], target.at[:, rows], sems.at[at])
    copy.start()
    return copy


def own_kernel(h_ref, v_ref, result_ref, out_ref, sems):
    blocks, _, users = h_ref.shape
    chips = out_ref.shape[0]
    piece = users // chips
    on_diag = iota((users, users), 0) == iota((users, users), 1)
    high, low, copies = [], [], []
    for block in range(blocks):
        h = jnp.transpose(h_ref[block])
        v = v_ref[block]
        for part, w in enumerate((v, turned(v))):
            g = dot(h, w, ((1,), (0,)))
            own = jnp.sum(jnp.where(on_diag, g, 0.0), axis=0, keepdims=True)
            first, second = two_parts(own)
            high.append(first.astype(F32))
            low.append(second.astype(F32))
            g = jnp.where(on_diag, 0.0, g)
            at = (block * 2 + part) * piece
            out_ref[:, at : at + piece] = g.reshape(chips, piece, users).astype(BF16)
            copies.append(sent(out_ref, result_ref, sems, len(copies), slice(at, at + piece)))
    extra = jnp.concatenate(high + low, axis=0).astype(BF16)
    out_ref[:, 4 * piece :] = jnp.broadcast_to(extra[None], (chips,) + extra.shape)
    copies.append(sent(out_ref, result_ref, sems, len(copies), slice(4 * piece, 4 * piece + 8)))
    for copy in copies:
        copy.wait()


def own_gains(h, v, chips):
    _, _, users = h.shape
    shape = (chips, 4 * (users // chips) + 8, users)
    vm = pl.BlockSpec(memory_space=pltpu.VMEM)
    return pl.pallas_call(
        own_kernel,
        out_shape=jax.ShapeDtypeStruct(shape, BF16),
        in_specs=[vm] * 2,
        out_specs=pl.BlockSpec(memory_space=pl.ANY),
        scratch_shapes=[pltpu.VMEM(shape, BF16), pltpu.SemaphoreType.DMA((5,))],
        name="own_gains",
        compiler_params=pltpu.CompilerParams(vmem_limit_bytes=8 << 20),
    )(h, v)


def gain_kernel(block, core_ref, cluster_ref, ht_ref, ha_ref, vt_ref, vb_ref, keep_ref, send_ref):
    _, _, users = ht_ref.shape
    half = users // 2
    chips = keep_ref.shape[0]
    piece = users // chips
    first = core_ref[0] == 0
    vt, vb = vt_ref[block], vb_ref[block]
    points = cluster_ref.shape[0]
    lane = iota((1, ht_ref.shape[1]), 1)
    point = lane // (ht_ref.shape[1] // (2 * points)) % points
    served = jnp.zeros(lane.shape, F32)
    for p in range(points):
        served = jnp.where(point == p, cluster_ref[p].astype(F32), served)
    ht, ha = jnp.transpose(ht_ref[block]), jnp.transpose(ha_ref[block])
    ha = ha * served.astype(BF16)
    for out_ref, low in ((keep_ref, first), (send_ref, jnp.logical_not(first))):
        own = jnp.where(low, vt[:, :half], vt[:, half:])
        far = jnp.where(low, vb[:, :half], vb[:, half:])
        both = jnp.concatenate([own, far], axis=1)
        g = dot(ht, jnp.concatenate([far, turned(far)], axis=1), ((1,), (0,)))
        for part in range(2):
            out_ref[:, part, :, :half] = g[:, part * half : (part + 1) * half].reshape(chips, piece, half).astype(BF16)
        for part, w in enumerate((both, turned(both))):
            out_ref[:, part, :, half:] = dot(ha, w, ((1,), (0,))).reshape(chips, piece, users).astype(BF16)


def partial_gains(block, core, near_cluster, ht, ha, vt, vb, chips):
    _, rows, users = ht.shape
    shape = (chips, 2, users // chips, users + users // 2)
    vm = pl.BlockSpec(memory_space=pltpu.VMEM)
    return pl.pallas_call(
        functools.partial(gain_kernel, block),
        out_shape=(jax.ShapeDtypeStruct(shape, BF16), jax.ShapeDtypeStruct(shape, BF16)),
        in_specs=[pl.BlockSpec(memory_space=pltpu.SMEM)] * 2 + [vm] * 4,
        out_specs=(vm, vm),
        name="gains",
        compiler_params=pltpu.CompilerParams(vmem_limit_bytes=8 << 20),
        cost_estimate=pl.CostEstimate(flops=12 * users * users * rows, bytes_accessed=4 << 20, transcendentals=0),
    )(core, near_cluster, ht, ha, vt, vb)


def combine_kernel(keep0_ref, keep1_ref, came0_ref, came1_ref, result_ref, out_ref, sems):
    chips, _, piece, width = keep0_ref.shape
    rows = 2 * piece
    copies = []
    for block, (keep_ref, came_ref) in enumerate(((keep0_ref, came0_ref), (keep1_ref, came1_ref))):
        g = keep_ref[...] + came_ref[...]
        at = slice(block * rows, (block + 1) * rows)
        out_ref[:, at] = g.reshape(chips, rows, width)
        copies.append(sent(out_ref, result_ref, sems, block, at))
    for copy in copies:
        copy.wait()


def combined(keeps, cames):
    chips, _, piece, width = keeps[0].shape
    shape = (chips, 4 * piece, width)
    vm = pl.BlockSpec(memory_space=pltpu.VMEM)
    return pl.pallas_call(
        combine_kernel,
        out_shape=jax.ShapeDtypeStruct(shape, BF16),
        in_specs=[vm] * 4,
        out_specs=pl.BlockSpec(memory_space=pl.ANY),
        scratch_shapes=[pltpu.VMEM(shape, BF16), pltpu.SemaphoreType.DMA((2,))],
        name="combine",
        compiler_params=pltpu.CompilerParams(vmem_limit_bytes=8 << 20),
    )(*keeps, *cames)


def own_sum_kernel(where_ref, g_ref, noise_ref, penalty_ref, power_ref, sum_ref, line_ref, penalty_out, power_out):
    chip, core = where_ref[0], where_ref[1]
    chips, rows, users = g_ref.shape
    piece = (rows - 8) // 4
    lanes = line_ref.shape[1]

    def summed(at):
        total = g_ref[0, at].astype(F32)
        for source in range(1, chips):
            total = total + g_ref[source, at].astype(F32)
        return total

    sum_ref[...] = summed(slice(0, 4 * piece))
    extra = summed(slice(4 * piece, 4 * piece + 8))
    signal = extra + pltpu.roll(extra, 4, 0)
    noise = jnp.where(core == 0, noise_ref[...], 0.0)
    signal = jnp.concatenate([signal[:4], noise, noise], axis=0)
    pick = iota((users, lanes), 0) == chip * piece + iota((users, lanes), 1) % piece
    mine = dot(signal, pick.astype(F32), ((1,), (0,)), HIGHEST)
    group = iota((1, lanes), 1) // piece
    line = jnp.zeros((1, lanes), F32)
    for block in range(2):
        for part in range(2):
            at = block * 2 + part
            line = line + jnp.where(group == block * 4 + 2 + part, mine[at : at + 1], 0.0)
        line = line + jnp.where(group == block * 4, mine[4 + block : 5 + block], 0.0)
    line_ref[...] = line
    penalty_out[...] = penalty_ref[...]
    power_out[...] = power_ref[...]


def own_sum(where, g, noise, penalty, power):
    _, rows, users = g.shape
    points = penalty.shape[0]
    vm = pl.BlockSpec(memory_space=pltpu.VMEM)
    return pl.pallas_call(
        own_sum_kernel,
        out_shape=(
            jax.ShapeDtypeStruct((rows - 8, users), F32),
            jax.ShapeDtypeStruct((1, 128), F32),
            jax.ShapeDtypeStruct((1, points), F32),
            jax.ShapeDtypeStruct((1, points), F32),
        ),
        in_specs=[pl.BlockSpec(memory_space=pltpu.SMEM)] + [vm] * 4,
        out_specs=(vm,) * 4,
        name="own_sum",
        compiler_params=pltpu.CompilerParams(vmem_limit_bytes=8 << 20),
    )(where, g, noise, penalty.reshape(1, points), power.reshape(1, points))


def placed(line, total, start):
    lane = iota((total.shape[0], line.shape[1]), 1)
    row = iota((total.shape[0], line.shape[1]), 0)
    return line + jnp.sum(jnp.where(lane == row + start, total, 0.0), axis=0, keepdims=True)


def own_total_kernel(where_ref, mine_ref, came_ref, line_ref, out_ref):
    piece = mine_ref.shape[0] // 4
    line = line_ref[...]
    g = jnp.where(where_ref[1] == 0, mine_ref[...] + came_ref[...], 0.0)
    square = jnp.sum(g * g, axis=1, keepdims=True)
    for block in range(2):
        at = 2 * block * piece
        line = placed(line, square[at : at + piece] + square[at + piece : at + 2 * piece], 4 * block * piece)
    out_ref[...] = line


def own_total(where, mine, came, line):
    vm = pl.BlockSpec(memory_space=pltpu.VMEM)
    return pl.pallas_call(
        own_total_kernel,
        out_shape=jax.ShapeDtypeStruct(line.shape, F32),
        in_specs=[pl.BlockSpec(memory_space=pltpu.SMEM)] + [vm] * 3,
        out_specs=vm,
        name="own_total",
        compiler_params=pltpu.CompilerParams(vmem_limit_bytes=4 << 20),
    )(where, mine, came, line)


def total_kernel(g_ref, line_ref, out_ref):
    chips, rows, width = g_ref.shape
    piece = rows // 4
    half = width // 3
    line = line_ref[...]
    for block in range(2):
        square = None
        for part in range(2):
            at = slice((block * 2 + part) * piece, (block * 2 + part + 1) * piece)
            g = g_ref[0, at].astype(F32)
            for source in range(1, chips):
                g = g + g_ref[source, at].astype(F32)
            square = g * g if square is None else square + g * g
        own = jnp.sum(square[:, :half], axis=1, keepdims=True)
        near = jnp.sum(square[:, half : 2 * half] + square[:, 2 * half :], axis=1, keepdims=True)
        line = placed(placed(line, own, block * 4 * piece), near, (block * 4 + 1) * piece)
    out_ref[...] = jnp.broadcast_to(line, out_ref.shape)


def totals(g, line, devices):
    vm = pl.BlockSpec(memory_space=pltpu.VMEM)
    return pl.pallas_call(
        total_kernel,
        out_shape=jax.ShapeDtypeStruct((devices, 128), F32),
        in_specs=[vm] * 2,
        out_specs=vm,
        name="totals",
        compiler_params=pltpu.CompilerParams(vmem_limit_bytes=8 << 20),
    )(g, line)


def user_lines(r_ref, line_ref, weight_ref, tile):
    chips, _, lanes = r_ref.shape
    groups = 8
    piece = lanes // groups
    halves = chips // groups
    group = iota((8, lanes), 1) // piece
    sublane = iota((8, lanes), 0)
    rolled = [r_ref[0]] + [pltpu.roll(r_ref[p], p * piece % lanes, 1) if p % groups else r_ref[p] for p in range(1, chips)]

    def gathered(g, half):
        total = None
        for p in range(half * groups, (half + 1) * groups):
            term = jnp.where(group == (p + g) % groups, rolled[p], 0.0)
            total = term if total is None else total + term
        if g:
            total = pltpu.roll(total, lanes - g * piece, 1)
        return total + pltpu.roll(total, 4, 0)

    def line(g):
        return jnp.concatenate([gathered(g, half) for half in range(halves)], axis=1)

    for block in range(2):
        base = block * 4
        from_mate = line(base + 1)
        even = iota(from_mate.shape, 0) % 2 == 0
        swapped = jnp.where(even, pltpu.roll(from_mate, 7, 0), pltpu.roll(from_mate, 1, 0))
        rest = line(base) + swapped
        signal_re = line(base + 2)
        signal_im = line(base + 3)
        strength = signal_re * signal_re + signal_im * signal_im
        level = rest + strength
        line_ref[block, 0] = strength / (rest * level)
        line_ref[block, 1] = signal_re / rest
        line_ref[block, 2] = signal_im / rest
        line_ref[block, 3] = level / rest
        weight_ref[block : block + 1, :] = line_ref[block, 3, pl.ds(tile, 1)]


def picked(pieces, g):
    lanes = pieces[0].shape[1]
    group = iota(pieces[0].shape, 1) // (lanes // 8)
    total = pieces[0]
    for s in range(1, 8):
        total = jnp.where(group == (s + g) % 8, pieces[s], total)
    return total


def eliminate(work_ref, sys_ref, scale_ref):
    _, rows, lanes = work_ref.shape
    width = lanes // 8
    lane = iota((8, lanes), 1)
    sublane = iota((8, lanes), 0)
    for high in range(rows // 8):
        at = slice(high * 8, high * 8 + 8)
        pieces = [sys_ref[s, at, :] for s in range(8)]
        for g in range(8):
            group = picked(pieces, g)
            work_ref[g, at, :] = pltpu.roll(group, lanes - g * width, 1) if g else group

    def spread(value, k):
        return jnp.take_along_axis(value, lane // width * width + k % width, axis=1, mode="promise_in_bounds")

    def row_of(g, k):
        return jnp.broadcast_to(work_ref[g, k : k + 1, :], (8, lanes))

    def pivot(k):
        column = k // width
        line = [row_of(g, k) for g in range(8)]
        value = spread(line[column], k)
        root = lax.rsqrt(value)
        scale_ref[k : k + 1, :] = root[:1]
        line[column] = line[column] + jnp.where(lane % width == k % width, 1.0, 0.0)
        return line, 1.0 / value

    def update(k, high, line, inverse):
        column = k // width
        at = slice(high * 8, high * 8 + 8)
        f_re = spread(work_ref[column, at, :], k) * inverse
        f_im = spread(work_ref[4 + column, at, :], k) * inverse
        if high == k // 8:
            below = sublane > k % 8
            f_re = jnp.where(below, f_re, 0.0)
            f_im = jnp.where(below, f_im, 0.0)
        for c in range(4):
            real, imag = line[c], line[4 + c]
            work_ref[c, at, :] = work_ref[c, at, :] - (f_re * real - f_im * imag)
            work_ref[4 + c, at, :] = work_ref[4 + c, at, :] - (f_re * imag + f_im * real)

    now = pivot(0)
    for k in range(rows - 1):
        first = (k + 1) // 8
        update(k, first, *now)
        later = pivot(k + 1)
        for high in range(first + 1, rows // 8):
            update(k, high, *now)
        now = later

    for high in range(rows // 8):
        at = slice(high * 8, high * 8 + 8)
        scale = scale_ref[at, :]
        pieces = []
        for g in range(8):
            start = g % 4 * width
            here = start + lane % width
            row = high * 8 + sublane
            kept = jnp.where(here < row, work_ref[g, at, :], 0.0)
            if g < 4:
                kept = jnp.where(here == row, 1.0, kept)
            kept = kept * scale
            pieces.append(pltpu.roll(kept, g * width, 1) if g else kept)
        for s in range(8):
            sys_ref[s, at, :] = picked(pieces, s)


def solve_kernel(tile_ref, penalty_ref, power_ref, r_ref, *refs):
    h_refs = refs[:4]
    out_ref, weight_ref, line_ref, sys_ref, work_ref, scale_ref, y_ref, made_ref, inverse_ref, sems = refs[4:]
    blocks, _, points, antennas, users = h_refs[0].shape
    size = 2 * antennas
    systems = blocks * points
    tile = tile_ref[0]

    user_lines(r_ref, line_ref, weight_ref, tile)

    def line(block, which, slot):
        return line_ref[block, which, pl.ds(tile ^ SLOTS[slot], 1), :]

    def channel(block, slot, point):
        h_ref = h_refs[slot]
        return jnp.concatenate([h_ref[block, 0, point], h_ref[block, 1, point]], axis=0)

    width = size // systems
    lane = iota((antennas, size), 1)
    row = iota((antennas, size), 0)

    def turn(x, n):
        cut = size - n * width
        return jnp.concatenate([x[cut:], x[:cut]], axis=0) if n else x

    def column(n):
        return (lane + (size - n * width)) % size

    for block in range(blocks):
        for point in range(points):
            n = block * points + point
            xs, highs, lows = [], [], []
            for slot in range(4):
                x = channel(block, slot, point)
                high, low = two_parts(turn(x, n).astype(F32) * line(block, 0, slot))
                xs.append(x)
                highs.append(high)
                lows.append(low)
            parts = jnp.concatenate([jnp.concatenate(highs, axis=1), jnp.concatenate(lows, axis=1)], axis=0)
            acc = dot(jnp.concatenate(xs, axis=1), parts, ((1,), (1,)))
            p = acc[:, :size] + acc[:, size:]
            a = jnp.where(column(n) < antennas, p[:antennas], -p[:antennas]) + pltpu.roll(p[antennas:], antennas, 1)
            a = a + jnp.where(column(n) == row, penalty_ref[0, point], 0.0)
            sys_ref[n] = a

    eliminate(work_ref, sys_ref, scale_ref)

    for n in range(systems):
        high, low = two_parts(sys_ref[n])
        left = jnp.concatenate([high, high, low, low], axis=0)
        right = jnp.concatenate([high, low, high, low], axis=0)
        q = turn(dot(left, right, ((0,), (0,))), (systems - n) % systems)
        top = jnp.where(column(n) < antennas, q[:antennas], -q[:antennas]) + pltpu.roll(q[antennas:], antennas, 1)
        bottom = pltpu.roll(top, antennas, 1)
        bottom = jnp.where(column(n) < antennas, -bottom, bottom)
        for at, half in enumerate((top, bottom)):
            high, low = two_parts(half)
            inverse_ref[n, at * antennas : (at + 1) * antennas, :size] = high
            inverse_ref[n, at * antennas : (at + 1) * antennas, size:] = low

    copies = []
    for point in range(points):
        total = jnp.zeros((1, users), F32)
        for block in range(blocks):
            n = block * points + point
            parts = inverse_ref[n]
            for slot in range(4):
                x = turn(channel(block, slot, point), n)
                y = dot(parts, jnp.concatenate([x, x], axis=0), ((1,), (0,)))
                w_re, w_im = line(block, 1, slot), line(block, 2, slot)
                total = total + jnp.sum(y * y, axis=0, keepdims=True) * (w_re * w_re + w_im * w_im)
                if slot == 0:
                    y_ref[block] = y
        mean = jnp.sum(total, axis=1, keepdims=True) / (2.0 * blocks * antennas * 4 * users)
        gain = jnp.sqrt(power_ref[0, point] / (mean + 1e-06))
        for block in range(blocks):
            y_re, y_im = y_ref[block, :antennas], y_ref[block, antennas:]
            w_re = line(block, 1, 0) * gain
            w_im = line(block, 2, 0) * gain
            made_ref[point, block, 0] = (y_re * w_re - y_im * w_im).astype(out_ref.dtype)
            made_ref[point, block, 1] = (y_re * w_im + y_im * w_re).astype(out_ref.dtype)
        copy = pltpu.make_async_copy(made_ref.at[point], out_ref.at[:, :, point], sems.at[point])
        copy.start()
        copies.append(copy)
    for copy in copies:
        copy.wait()


def solve(tile, penalty, power, r, channels, out_shape):
    blocks, _, points, antennas, users = out_shape
    size = 2 * antennas
    vm = pl.BlockSpec(memory_space=pltpu.VMEM)
    sm = pl.BlockSpec(memory_space=pltpu.SMEM)
    return pl.pallas_call(
        solve_kernel,
        out_shape=(
            jax.ShapeDtypeStruct(out_shape, BF16),
            jax.ShapeDtypeStruct((blocks, users), F32),
        ),
        in_specs=[sm] * 3 + [vm] * 5,
        out_specs=(pl.BlockSpec(memory_space=pl.ANY), vm),
        scratch_shapes=[
            pltpu.VMEM((blocks, 4, 8, users), F32),
            pltpu.VMEM((blocks * points, antennas, size), F32),
            pltpu.VMEM((8, antennas, size), F32),
            pltpu.VMEM((antennas, size), F32),
            pltpu.VMEM((blocks, size, users), F32),
            pltpu.VMEM((points, blocks, 2, antennas, users), BF16),
            pltpu.VMEM((blocks * points, size, 2 * size), BF16),
            pltpu.SemaphoreType.DMA((points,)),
        ],
        name="solve",
        compiler_params=pltpu.CompilerParams(vmem_limit_bytes=16 << 20),
    )(tile, penalty, power, r, *channels)


def across(value, axis, mask):
    size = lax.axis_size(axis)
    return lax.ppermute(value, axis, [(i, i ^ mask) for i in range(size)])


def local(channel, start_precoder, cluster, noise, penalty, power):
    blocks, parts, points, antennas, users = channel.shape
    chips = lax.axis_size(CHIPS)
    devices = lax.axis_size(EVERY)
    rows = parts * points * antennas
    core = lax.axis_index("core")
    tile = lax.axis_index("ut")
    chip = lax.axis_index(CHIPS)

    near_cluster = across(cluster[:, 0], "ut", 1)
    near = across(channel, "ut", 1)
    v_far = across(start_precoder, "ut", 3)

    own = channel * cluster[:, 0].astype(BF16)[None, None, :, None, None]
    early = own_gains(own.reshape(blocks, rows, users), start_precoder.reshape(blocks, rows, users), chips)
    early = lax.all_to_all(early, CHIPS, 0, 0, tiled=True)

    far = across(own, "ut", 3)

    where = jnp.stack([chip, core])
    ht, ha, vt, vb = (x.reshape(blocks, rows, users) for x in (own, near, start_precoder, v_far))
    keeps, cames = [], []
    for b in range(blocks):
        keep, send = partial_gains(b, core.reshape(1), near_cluster, ht, ha, vt, vb, chips)
        keeps.append(keep)
        cames.append(across(send, "core", 1))
    near = near * near_cluster.astype(BF16)[None, None, :, None, None]
    far_near = across(near, "ut", 3)
    late = combined(keeps, cames)
    late = lax.all_to_all(late, CHIPS, 0, 0, tiled=True)

    mine, line, penalty, power = own_sum(where, early, noise, penalty, power)
    line = own_total(where, mine, across(mine, "core", 1), line)
    line = totals(late, line, devices)
    r = lax.all_to_all(line, EVERY, 0, 0, tiled=True).reshape(chips, devices // chips, 128)

    precoder, weight = solve(tile.reshape(1), penalty, power, r, (own, near, far, far_near), channel.shape)
    return precoder, weight


def solution(mesh):
    split = Mesh(mesh.devices.reshape(4, 4, 2, mesh.shape["ut"]), EVERY)
    placed = (
        P(None, None, AP, None, "ut"),
        P(None, None, AP, None, "ut"),
        P(AP, "ut"),
        P(None, "ut"),
        P(AP),
        P(AP),
    )

    return jax.shard_map(
        local,
        mesh=split,
        in_specs=placed,
        out_specs=(P(None, None, AP, None, "ut"), P(None, "ut")),
        check_vma=False,
    )
```

```python
import functools

import jax
import jax.numpy as jnp
from jax import lax
from jax.experimental import pallas as pl
from jax.experimental.pallas import tpu as pltpu
from jax.sharding import Mesh
from jax.sharding import PartitionSpec as P


AP = ("z", "x", "core")
CHIPS = ("z", "x")
EVERY = ("z", "x", "core", "ut")
SLOTS = (0, 1, 3, 2)
F32 = jnp.float32
BF16 = jnp.bfloat16
HIGHEST = lax.Precision.HIGHEST


def dot(a, b, dims, precision=None):
    return lax.dot_general(a, b, (dims, ((), ())), precision=precision, preferred_element_type=F32)


def two_parts(x):
    high = x.astype(BF16)
    return high, (x - high.astype(F32)).astype(BF16)


def iota(shape, dim):
    return lax.broadcasted_iota(jnp.int32, shape, dim)


def turned(v):
    half = v.shape[0] // 2
    return jnp.concatenate([v[half:], -v[:half]], axis=0)


def sent(source, target, sems, at, rows):
    copy = pltpu.make_async_copy(source.at[:, rows], target.at[:, rows], sems.at[at])
    copy.start()
    return copy


def own_kernel(h_ref, v_ref, result_ref, out_ref, sems):
    blocks, _, users = h_ref.shape
    chips = out_ref.shape[0]
    piece = users // chips
    on_diag = iota((users, users), 0) == iota((users, users), 1)
    high, low, copies = [], [], []
    for block in range(blocks):
        h = jnp.transpose(h_ref[block])
        v = v_ref[block]
        for part, w in enumerate((v, turned(v))):
            g = dot(h, w, ((1,), (0,)))
            own = jnp.sum(jnp.where(on_diag, g, 0.0), axis=0, keepdims=True)
            first, second = two_parts(own)
            high.append(first.astype(F32))
            low.append(second.astype(F32))
            g = jnp.where(on_diag, 0.0, g)
            at = (block * 2 + part) * piece
            out_ref[:, at : at + piece] = g.reshape(chips, piece, users).astype(BF16)
            copies.append(sent(out_ref, result_ref, sems, len(copies), slice(at, at + piece)))
    extra = jnp.concatenate(high + low, axis=0).astype(BF16)
    out_ref[:, 4 * piece :] = jnp.broadcast_to(extra[None], (chips,) + extra.shape)
    copies.append(sent(out_ref, result_ref, sems, len(copies), slice(4 * piece, 4 * piece + 8)))
    for copy in copies:
        copy.wait()


def own_gains(h, v, chips):
    _, _, users = h.shape
    shape = (chips, 4 * (users // chips) + 8, users)
    vm = pl.BlockSpec(memory_space=pltpu.VMEM)
    return pl.pallas_call(
        own_kernel,
        out_shape=jax.ShapeDtypeStruct(shape, BF16),
        in_specs=[vm] * 2,
        out_specs=pl.BlockSpec(memory_space=pl.ANY),
        scratch_shapes=[pltpu.VMEM(shape, BF16), pltpu.SemaphoreType.DMA((5,))],
        name="own_gains",
        compiler_params=pltpu.CompilerParams(vmem_limit_bytes=8 << 20),
    )(h, v)


def gain_kernel(block, core_ref, cluster_ref, ht_ref, ha_ref, vt_ref, vb_ref, keep_ref, send_ref):
    _, _, users = ht_ref.shape
    half = users // 2
    chips = keep_ref.shape[0]
    piece = users // chips
    first = core_ref[0] == 0
    vt, vb = vt_ref[block], vb_ref[block]
    points = cluster_ref.shape[1]
    lane = iota((1, ht_ref.shape[1]), 1)
    point = lane // (ht_ref.shape[1] // (2 * points)) % points
    served = jnp.zeros(lane.shape, F32)
    for p in range(points):
        served = jnp.where(point == p, cluster_ref[:, p : p + 1].astype(F32), served)
    ht, ha = jnp.transpose(ht_ref[block]), jnp.transpose(ha_ref[block])
    ha = ha * served.astype(BF16)
    for out_ref, low in ((keep_ref, first), (send_ref, jnp.logical_not(first))):
        own = jnp.where(low, vt[:, :half], vt[:, half:])
        far = jnp.where(low, vb[:, :half], vb[:, half:])
        both = jnp.concatenate([own, far], axis=1)
        g = dot(ht, jnp.concatenate([far, turned(far)], axis=1), ((1,), (0,)))
        for part in range(2):
            out_ref[:, part, :, :half] = g[:, part * half : (part + 1) * half].reshape(chips, piece, half).astype(BF16)
        for part, w in enumerate((both, turned(both))):
            out_ref[:, part, :, half:] = dot(ha, w, ((1,), (0,))).reshape(chips, piece, users).astype(BF16)


def partial_gains(block, core, near_cluster, ht, ha, vt, vb, chips):
    _, rows, users = ht.shape
    shape = (chips, 2, users // chips, users + users // 2)
    vm = pl.BlockSpec(memory_space=pltpu.VMEM)
    return pl.pallas_call(
        functools.partial(gain_kernel, block),
        out_shape=(jax.ShapeDtypeStruct(shape, BF16), jax.ShapeDtypeStruct(shape, BF16)),
        in_specs=[pl.BlockSpec(memory_space=pltpu.SMEM)] + [vm] * 5,
        out_specs=(vm, vm),
        name="gains",
        compiler_params=pltpu.CompilerParams(vmem_limit_bytes=8 << 20),
        cost_estimate=pl.CostEstimate(flops=12 * users * users * rows, bytes_accessed=4 << 20, transcendentals=0),
    )(core, near_cluster.reshape(1, -1), ht, ha, vt, vb)


def combine_kernel(keep0_ref, keep1_ref, came0_ref, came1_ref, result_ref, out_ref, sems):
    chips, _, piece, width = keep0_ref.shape
    rows = 2 * piece
    copies = []
    for block, (keep_ref, came_ref) in enumerate(((keep0_ref, came0_ref), (keep1_ref, came1_ref))):
        g = keep_ref[...] + came_ref[...]
        at = slice(block * rows, (block + 1) * rows)
        out_ref[:, at] = g.reshape(chips, rows, width)
        copies.append(sent(out_ref, result_ref, sems, block, at))
    for copy in copies:
        copy.wait()


def combined(keeps, cames):
    chips, _, piece, width = keeps[0].shape
    shape = (chips, 4 * piece, width)
    vm = pl.BlockSpec(memory_space=pltpu.VMEM)
    return pl.pallas_call(
        combine_kernel,
        out_shape=jax.ShapeDtypeStruct(shape, BF16),
        in_specs=[vm] * 4,
        out_specs=pl.BlockSpec(memory_space=pl.ANY),
        scratch_shapes=[pltpu.VMEM(shape, BF16), pltpu.SemaphoreType.DMA((2,))],
        name="combine",
        compiler_params=pltpu.CompilerParams(vmem_limit_bytes=8 << 20),
    )(*keeps, *cames)


def own_sum_kernel(where_ref, g_ref, noise_ref, penalty_ref, power_ref, sum_ref, line_ref, penalty_out, power_out):
    chip, core = where_ref[0], where_ref[1]
    chips, rows, users = g_ref.shape
    piece = (rows - 8) // 4
    lanes = line_ref.shape[1]

    def summed(at):
        total = g_ref[0, at].astype(F32)
        for source in range(1, chips):
            total = total + g_ref[source, at].astype(F32)
        return total

    sum_ref[...] = summed(slice(0, 4 * piece))
    extra = summed(slice(4 * piece, 4 * piece + 8))
    signal = extra + pltpu.roll(extra, 4, 0)
    noise = jnp.where(core == 0, noise_ref[...], 0.0)
    signal = jnp.concatenate([signal[:4], noise, noise], axis=0)
    pick = iota((users, lanes), 0) == chip * piece + iota((users, lanes), 1) % piece
    mine = dot(signal, pick.astype(F32), ((1,), (0,)), HIGHEST)
    group = iota((1, lanes), 1) // piece
    line = jnp.zeros((1, lanes), F32)
    for block in range(2):
        for part in range(2):
            at = block * 2 + part
            line = line + jnp.where(group == block * 4 + 2 + part, mine[at : at + 1], 0.0)
        line = line + jnp.where(group == block * 4, mine[4 + block : 5 + block], 0.0)
    line_ref[...] = line
    penalty_out[...] = penalty_ref[...]
    power_out[...] = power_ref[...]


def own_sum(where, g, noise, penalty, power):
    _, rows, users = g.shape
    points = penalty.shape[0]
    vm = pl.BlockSpec(memory_space=pltpu.VMEM)
    return pl.pallas_call(
        own_sum_kernel,
        out_shape=(
            jax.ShapeDtypeStruct((rows - 8, users), F32),
            jax.ShapeDtypeStruct((1, 128), F32),
            jax.ShapeDtypeStruct((1, points), F32),
            jax.ShapeDtypeStruct((1, points), F32),
        ),
        in_specs=[pl.BlockSpec(memory_space=pltpu.SMEM)] + [vm] * 4,
        out_specs=(vm,) * 4,
        name="own_sum",
        compiler_params=pltpu.CompilerParams(vmem_limit_bytes=8 << 20),
    )(where, g, noise, penalty.reshape(1, points), power.reshape(1, points))


def placed(line, total, start):
    lane = iota((total.shape[0], line.shape[1]), 1)
    row = iota((total.shape[0], line.shape[1]), 0)
    return line + jnp.sum(jnp.where(lane == row + start, total, 0.0), axis=0, keepdims=True)


def own_total_kernel(where_ref, mine_ref, came_ref, line_ref, out_ref):
    piece = mine_ref.shape[0] // 4
    line = line_ref[...]
    g = jnp.where(where_ref[1] == 0, mine_ref[...] + came_ref[...], 0.0)
    square = jnp.sum(g * g, axis=1, keepdims=True)
    for block in range(2):
        at = 2 * block * piece
        line = placed(line, square[at : at + piece] + square[at + piece : at + 2 * piece], 4 * block * piece)
    out_ref[...] = line


def own_total(where, mine, came, line):
    vm = pl.BlockSpec(memory_space=pltpu.VMEM)
    return pl.pallas_call(
        own_total_kernel,
        out_shape=jax.ShapeDtypeStruct(line.shape, F32),
        in_specs=[pl.BlockSpec(memory_space=pltpu.SMEM)] + [vm] * 3,
        out_specs=vm,
        name="own_total",
        compiler_params=pltpu.CompilerParams(vmem_limit_bytes=4 << 20),
    )(where, mine, came, line)


def total_kernel(g_ref, line_ref, out_ref):
    chips, rows, width = g_ref.shape
    piece = rows // 4
    half = width // 3
    line = line_ref[...]
    for block in range(2):
        square = None
        for part in range(2):
            at = slice((block * 2 + part) * piece, (block * 2 + part + 1) * piece)
            g = g_ref[0, at].astype(F32)
            for source in range(1, chips):
                g = g + g_ref[source, at].astype(F32)
            square = g * g if square is None else square + g * g
        own = jnp.sum(square[:, :half], axis=1, keepdims=True)
        near = jnp.sum(square[:, half : 2 * half] + square[:, 2 * half :], axis=1, keepdims=True)
        line = placed(placed(line, own, block * 4 * piece), near, (block * 4 + 1) * piece)
    out_ref[...] = jnp.broadcast_to(line, out_ref.shape)


def totals(g, line, devices):
    vm = pl.BlockSpec(memory_space=pltpu.VMEM)
    return pl.pallas_call(
        total_kernel,
        out_shape=jax.ShapeDtypeStruct((devices, 128), F32),
        in_specs=[vm] * 2,
        out_specs=vm,
        name="totals",
        compiler_params=pltpu.CompilerParams(vmem_limit_bytes=8 << 20),
    )(g, line)


def user_lines(r_ref, line_ref, weight_ref, tile):
    chips, _, lanes = r_ref.shape
    groups = 8
    piece = lanes // groups
    halves = chips // groups
    group = iota((8, lanes), 1) // piece
    sublane = iota((8, lanes), 0)
    rolled = [r_ref[0]] + [pltpu.roll(r_ref[p], p * piece % lanes, 1) if p % groups else r_ref[p] for p in range(1, chips)]

    def gathered(g, half):
        total = None
        for p in range(half * groups, (half + 1) * groups):
            term = jnp.where(group == (p + g) % groups, rolled[p], 0.0)
            total = term if total is None else total + term
        if g:
            total = pltpu.roll(total, lanes - g * piece, 1)
        return total + pltpu.roll(total, 4, 0)

    def line(g):
        return jnp.concatenate([gathered(g, half) for half in range(halves)], axis=1)

    for block in range(2):
        base = block * 4
        from_mate = line(base + 1)
        even = iota(from_mate.shape, 0) % 2 == 0
        swapped = jnp.where(even, pltpu.roll(from_mate, 7, 0), pltpu.roll(from_mate, 1, 0))
        rest = line(base) + swapped
        signal_re = line(base + 2)
        signal_im = line(base + 3)
        strength = signal_re * signal_re + signal_im * signal_im
        level = rest + strength
        line_ref[block, 0] = strength / (rest * level)
        line_ref[block, 1] = signal_re / rest
        line_ref[block, 2] = signal_im / rest
        line_ref[block, 3] = level / rest
        weight_ref[block : block + 1, :] = line_ref[block, 3, pl.ds(tile, 1)]


def picked(pieces, g):
    lanes = pieces[0].shape[1]
    group = iota(pieces[0].shape, 1) // (lanes // 8)
    total = pieces[0]
    for s in range(1, 8):
        total = jnp.where(group == (s + g) % 8, pieces[s], total)
    return total


def eliminate(work_ref, sys_ref, scale_ref):
    _, rows, lanes = work_ref.shape
    width = lanes // 8
    lane = iota((8, lanes), 1)
    sublane = iota((8, lanes), 0)
    for high in range(rows // 8):
        at = slice(high * 8, high * 8 + 8)
        pieces = [sys_ref[s, at, :] for s in range(8)]
        for g in range(8):
            group = picked(pieces, g)
            work_ref[g, at, :] = pltpu.roll(group, lanes - g * width, 1) if g else group

    def spread(value, k):
        return jnp.take_along_axis(value, lane // width * width + k % width, axis=1, mode="promise_in_bounds")

    def row_of(g, k):
        return jnp.broadcast_to(work_ref[g, k : k + 1, :], (8, lanes))

    def pivot(k):
        column = k // width
        line = [row_of(g, k) for g in range(8)]
        value = spread(line[column], k)
        root = lax.rsqrt(value)
        scale_ref[k : k + 1, :] = root[:1]
        line[column] = line[column] + jnp.where(lane % width == k % width, 1.0, 0.0)
        return line, 1.0 / value

    def update(k, high, line, inverse):
        column = k // width
        at = slice(high * 8, high * 8 + 8)
        f_re = spread(work_ref[column, at, :], k) * inverse
        f_im = spread(work_ref[4 + column, at, :], k) * inverse
        if high == k // 8:
            below = sublane > k % 8
            f_re = jnp.where(below, f_re, 0.0)
            f_im = jnp.where(below, f_im, 0.0)
        for c in range(4):
            real, imag = line[c], line[4 + c]
            work_ref[c, at, :] = work_ref[c, at, :] - (f_re * real - f_im * imag)
            work_ref[4 + c, at, :] = work_ref[4 + c, at, :] - (f_re * imag + f_im * real)

    now = pivot(0)
    for k in range(rows - 1):
        first = (k + 1) // 8
        update(k, first, *now)
        later = pivot(k + 1)
        for high in range(first + 1, rows // 8):
            update(k, high, *now)
        now = later

    for high in range(rows // 8):
        at = slice(high * 8, high * 8 + 8)
        scale = scale_ref[at, :]
        pieces = []
        for g in range(8):
            start = g % 4 * width
            here = start + lane % width
            row = high * 8 + sublane
            kept = jnp.where(here < row, work_ref[g, at, :], 0.0)
            if g < 4:
                kept = jnp.where(here == row, 1.0, kept)
            kept = kept * scale
            pieces.append(pltpu.roll(kept, g * width, 1) if g else kept)
        for s in range(8):
            sys_ref[s, at, :] = picked(pieces, s)


def solve_kernel(tile_ref, penalty_ref, power_ref, r_ref, *refs):
    h_refs = refs[:4]
    out_ref, weight_ref, line_ref, sys_ref, work_ref, scale_ref, y_ref, made_ref, inverse_ref, sems = refs[4:]
    blocks, _, points, antennas, users = h_refs[0].shape
    size = 2 * antennas
    systems = blocks * points
    tile = tile_ref[0]

    user_lines(r_ref, line_ref, weight_ref, tile)

    def line(block, which, slot):
        return line_ref[block, which, pl.ds(tile ^ SLOTS[slot], 1), :]

    def channel(block, slot, point):
        h_ref = h_refs[slot]
        return jnp.concatenate([h_ref[block, 0, point], h_ref[block, 1, point]], axis=0)

    width = size // systems
    lane = iota((antennas, size), 1)
    row = iota((antennas, size), 0)

    def turn(x, n):
        cut = size - n * width
        return jnp.concatenate([x[cut:], x[:cut]], axis=0) if n else x

    def column(n):
        return (lane + (size - n * width)) % size

    for block in range(blocks):
        for point in range(points):
            n = block * points + point
            xs, highs, lows = [], [], []
            for slot in range(4):
                x = channel(block, slot, point)
                high, low = two_parts(turn(x, n).astype(F32) * line(block, 0, slot))
                xs.append(x)
                highs.append(high)
                lows.append(low)
            parts = jnp.concatenate([jnp.concatenate(highs, axis=1), jnp.concatenate(lows, axis=1)], axis=0)
            acc = dot(jnp.concatenate(xs, axis=1), parts, ((1,), (1,)))
            p = acc[:, :size] + acc[:, size:]
            a = jnp.where(column(n) < antennas, p[:antennas], -p[:antennas]) + pltpu.roll(p[antennas:], antennas, 1)
            a = a + jnp.where(column(n) == row, penalty_ref[0, point], 0.0)
            sys_ref[n] = a

    eliminate(work_ref, sys_ref, scale_ref)

    for n in range(systems):
        high, low = two_parts(sys_ref[n])
        left = jnp.concatenate([high, high, low, low], axis=0)
        right = jnp.concatenate([high, low, high, low], axis=0)
        q = turn(dot(left, right, ((0,), (0,))), (systems - n) % systems)
        top = jnp.where(column(n) < antennas, q[:antennas], -q[:antennas]) + pltpu.roll(q[antennas:], antennas, 1)
        bottom = pltpu.roll(top, antennas, 1)
        bottom = jnp.where(column(n) < antennas, -bottom, bottom)
        for at, half in enumerate((top, bottom)):
            high, low = two_parts(half)
            inverse_ref[n, at * antennas : (at + 1) * antennas, :size] = high
            inverse_ref[n, at * antennas : (at + 1) * antennas, size:] = low

    copies = []
    for point in range(points):
        total = jnp.zeros((1, users), F32)
        for block in range(blocks):
            n = block * points + point
            parts = inverse_ref[n]
            for slot in range(4):
                x = turn(channel(block, slot, point), n)
                y = dot(parts, jnp.concatenate([x, x], axis=0), ((1,), (0,)))
                w_re, w_im = line(block, 1, slot), line(block, 2, slot)
                total = total + jnp.sum(y * y, axis=0, keepdims=True) * (w_re * w_re + w_im * w_im)
                if slot == 0:
                    y_ref[block] = y
        mean = jnp.sum(total, axis=1, keepdims=True) / (2.0 * blocks * antennas * 4 * users)
        gain = jnp.sqrt(power_ref[0, point] / (mean + 1e-06))
        for block in range(blocks):
            y_re, y_im = y_ref[block, :antennas], y_ref[block, antennas:]
            w_re = line(block, 1, 0) * gain
            w_im = line(block, 2, 0) * gain
            made_ref[point, block, 0] = (y_re * w_re - y_im * w_im).astype(out_ref.dtype)
            made_ref[point, block, 1] = (y_re * w_im + y_im * w_re).astype(out_ref.dtype)
        copy = pltpu.make_async_copy(made_ref.at[point], out_ref.at[:, :, point], sems.at[point])
        copy.start()
        copies.append(copy)
    for copy in copies:
        copy.wait()


def solve(tile, penalty, power, r, channels, out_shape):
    blocks, _, points, antennas, users = out_shape
    size = 2 * antennas
    vm = pl.BlockSpec(memory_space=pltpu.VMEM)
    sm = pl.BlockSpec(memory_space=pltpu.SMEM)
    return pl.pallas_call(
        solve_kernel,
        out_shape=(
            jax.ShapeDtypeStruct(out_shape, BF16),
            jax.ShapeDtypeStruct((blocks, users), F32),
        ),
        in_specs=[sm] * 3 + [vm] * 5,
        out_specs=(pl.BlockSpec(memory_space=pl.ANY), vm),
        scratch_shapes=[
            pltpu.VMEM((blocks, 4, 8, users), F32),
            pltpu.VMEM((blocks * points, antennas, size), F32),
            pltpu.VMEM((8, antennas, size), F32),
            pltpu.VMEM((antennas, size), F32),
            pltpu.VMEM((blocks, size, users), F32),
            pltpu.VMEM((points, blocks, 2, antennas, users), BF16),
            pltpu.VMEM((blocks * points, size, 2 * size), BF16),
            pltpu.SemaphoreType.DMA((points,)),
        ],
        name="solve",
        compiler_params=pltpu.CompilerParams(vmem_limit_bytes=16 << 20),
    )(tile, penalty, power, r, *channels)


def across(value, axis, mask):
    size = lax.axis_size(axis)
    return lax.ppermute(value, axis, [(i, i ^ mask) for i in range(size)])


def local(channel, start_precoder, cluster, noise, penalty, power):
    blocks, parts, points, antennas, users = channel.shape
    chips = lax.axis_size(CHIPS)
    devices = lax.axis_size(EVERY)
    rows = parts * points * antennas
    core = lax.axis_index("core")
    tile = lax.axis_index("ut")
    chip = lax.axis_index(CHIPS)

    near_cluster = across(cluster[:, 0], "ut", 1)
    near = across(channel, "ut", 1)
    v_far = across(start_precoder, "ut", 3)

    own = channel * cluster[:, 0].astype(BF16)[None, None, :, None, None]
    early = own_gains(own.reshape(blocks, rows, users), start_precoder.reshape(blocks, rows, users), chips)
    early = lax.all_to_all(early, CHIPS, 0, 0, tiled=True)

    far = across(own, "ut", 3)

    where = jnp.stack([chip, core])
    ht, ha, vt, vb = (x.reshape(blocks, rows, users) for x in (own, near, start_precoder, v_far))
    keeps, cames = [], []
    for b in range(blocks):
        keep, send = partial_gains(b, core.reshape(1), near_cluster, ht, ha, vt, vb, chips)
        keeps.append(keep)
        cames.append(across(send, "core", 1))
    near = near * near_cluster.astype(BF16)[None, None, :, None, None]
    far_near = across(near, "ut", 3)
    late = combined(keeps, cames)
    late = lax.all_to_all(late, CHIPS, 0, 0, tiled=True)

    mine, line, penalty, power = own_sum(where, early, noise, penalty, power)
    line = own_total(where, mine, across(mine, "core", 1), line)
    line = totals(late, line, devices)
    r = lax.all_to_all(line, EVERY, 0, 0, tiled=True).reshape(chips, devices // chips, 128)

    precoder, weight = solve(tile.reshape(1), penalty, power, r, (own, near, far, far_near), channel.shape)
    return precoder, weight


def solution(mesh):
    split = Mesh(mesh.devices.reshape(4, 4, 2, mesh.shape["ut"]), EVERY)
    placed = (
        P(None, None, AP, None, "ut"),
        P(None, None, AP, None, "ut"),
        P(AP, "ut"),
        P(None, "ut"),
        P(AP),
        P(AP),
    )

    return jax.shard_map(
        local,
        mesh=split,
        in_specs=placed,
        out_specs=(P(None, None, AP, None, "ut"), P(None, "ut")),
        check_vma=False,
    )
```
